128 devices in a mesh: outer: 8 (over x, core), inner: 16 (over z, y).
Axes of the slice: x: 4, y: 4, z: 4, core: 2. Of those that a mesh axis runs over, the one named last changes fastest.
Arguments:
- tokens: bfloat16 [2048, 3584], P(('outer', 'inner')), may hold values from -6 to 6
- experts: int32 [2048, 8], P(('outer', 'inner')), may hold values from 0 to 127, as said below
- gate_score: int32 [2048, 8], P(('outer', 'inner')), may hold values from 1 to 16
- expert_gate: bfloat16 [128, 3584, 1024], P(('outer', 'inner')), may hold values from -0.09375 to 0.09375
- expert_up: bfloat16 [128, 3584, 1024], P(('outer', 'inner')), may hold values from -0.09375 to 0.09375
- expert_down: bfloat16 [128, 1024, 3584], P(('outer', 'inner')), may hold values from -0.1875 to 0.1875
- shared_gate: bfloat16 [3584, 2048], P(None, 'inner'), may hold values from -0.09375 to 0.09375
- shared_up: bfloat16 [3584, 2048], P(None, 'inner'), may hold values from -0.09375 to 0.09375
- shared_down: bfloat16 [2048, 3584], P('inner'), may hold values from -0.125 to 0.125
Outputs:
- moe_out: bfloat16 [2048, 3584], P(('outer', 'inner'))
The draws below stay inside these ranges and needn't reach their ends.
Inputs may be any that keep to these rules, and one draw needn't show every extreme that they name: Each token names 8 different experts, exactly two in each of 4 different groups, where expert e lies in group e // 16. One group, drawn from the seed, is named by every token. The 16 tokens of one device name one expert at most 2 times, and name each expert of that group exactly 2 times.
All inputs are finite; a program needn't handle non-finite values.
Results may differ from the reference program's by a relative error of at most 0.012.
Values may be sent and summed in bfloat16 or wider, within the bound.
A program may use at most 128 MiB of HBM per device.

```python
import jax
import jax.numpy as jnp
from jax import lax

D = 3584
FFE = 1024
SHARED_FF = 2048
TOPK = 8
TOP_GROUPS = 4
TOK_DEV = 16
EXPERTS = 128
CAP = 2
TOKENS = 2048
N_OUTER = 8
N_INNER = 16


def draw_experts(key, part):
    device_total = N_OUTER * N_INNER
    per_group = TOPK // TOP_GROUPS
    favored = jax.random.randint(jax.random.fold_in(key, 11), (), 0, N_OUTER).astype(jnp.int32)

    def one_device(device_index):
        device_key = jax.random.fold_in(jax.random.fold_in(key, 23), device_index)
        token_keys = jax.random.split(jax.random.fold_in(device_key, 1), TOK_DEV)
        others = jax.vmap(lambda subkey: jax.random.permutation(subkey, N_OUTER - 1))(token_keys)
        others = others[:, :TOP_GROUPS - 1].astype(jnp.int32)
        chosen = jnp.concatenate([jnp.full((TOK_DEV, 1), favored, jnp.int32), (favored + 1 + others) % N_OUTER], axis=1)
        group_keys = jax.random.split(jax.random.fold_in(device_key, 2), N_OUTER)
        shuffled = jax.vmap(lambda subkey: jax.random.permutation(subkey, N_INNER))(group_keys).astype(jnp.int32)
        member = jnp.any(chosen[:, :, None] == jnp.arange(N_OUTER, dtype=jnp.int32)[None, None, :], axis=1).astype(jnp.int32)
        ordinal = jnp.cumsum(member, axis=0) - member
        seen = jnp.take_along_axis(ordinal, chosen, axis=1)
        position = (per_group * seen[:, :, None] + jnp.arange(per_group, dtype=jnp.int32)[None, None, :]) % N_INNER
        local_ids = shuffled[chosen[:, :, None], position]
        ids = (chosen[:, :, None] * N_INNER + local_ids).reshape(TOK_DEV, TOPK)
        slot_keys = jax.random.split(jax.random.fold_in(device_key, 3), TOK_DEV)
        mixing = jax.vmap(lambda subkey: jax.random.permutation(subkey, TOPK))(slot_keys).astype(jnp.int32)
        return jnp.take_along_axis(ids, mixing, axis=1).astype(jnp.int32)
    every = jax.vmap(one_device)(jnp.arange(device_total, dtype=jnp.int32))
    return every.reshape(device_total * TOK_DEV, TOPK)


def place_ends(values, stream_key, smallest, top_value):
    longest = values.shape.index(max(values.shape))
    spots = []
    for shift in (0, 1):
        where = [jax.random.randint(jax.random.fold_in(stream_key, axis), (), 0, length) for axis, length in enumerate(values.shape)]
        where[longest] = (where[longest] + shift) % values.shape[longest]
        spots.append(tuple(where))
    return values.at[spots[0]].set(smallest).at[spots[1]].set(top_value)


def block_scale(stream_key, extent, pieces, low, top_value):
    gain, own = 1.0, jax.random.fold_in(stream_key, 6)
    for axis_at, blocks in pieces:
        heights = jnp.exp(jax.random.uniform(jax.random.fold_in(own, axis_at), (blocks,), jnp.float32, low / len(pieces), top_value / len(pieces)))
        gain = gain * jnp.repeat(heights, extent[axis_at] // blocks).reshape([-1 if axis == axis_at else 1 for axis in range(len(extent))])
    return gain


def scatter_about(key, shape, deviation, bound, cuts=(), kind=jnp.bfloat16):
    entries = deviation * jax.random.normal(key, shape, jnp.float32)
    if cuts:
        entries = entries * block_scale(key, shape, cuts, -0.22, 0.18)
    return jnp.clip(entries, -bound, bound).astype(kind)


def setup_inputs(seed: int = 0) -> dict:
    arg_keys = jax.random.split(jax.random.key(seed), 10)
    tokens = scatter_about(arg_keys[0], (TOKENS, D), 1.0, 6.0, ((0, 128),))
    experts = draw_experts(jax.random.fold_in(arg_keys[9], 71), 0)
    gate_score = place_ends(jax.random.randint(arg_keys[2], (TOKENS, TOPK), 1, 17), jax.random.fold_in(arg_keys[2], 1), 1, 16).astype(jnp.int32)
    expert_gate = scatter_about(arg_keys[3], (EXPERTS, D, FFE), D ** -0.5, 0.09375, ((0, 128),))
    expert_up = scatter_about(arg_keys[4], (EXPERTS, D, FFE), D ** -0.5, 0.09375, ((0, 128),))
    expert_down = scatter_about(arg_keys[5], (EXPERTS, FFE, D), FFE ** -0.5, 0.1875, ((0, 128),))
    shared_gate = scatter_about(arg_keys[6], (D, SHARED_FF), D ** -0.5, 0.09375, ((1, 16),))
    shared_up = scatter_about(arg_keys[7], (D, SHARED_FF), D ** -0.5, 0.09375, ((1, 16),))
    shared_down = scatter_about(arg_keys[8], (SHARED_FF, D), SHARED_FF ** -0.5, 0.125, ((0, 16),))
    return {"tokens": tokens, "experts": experts, "gate_score": gate_score, "expert_gate": expert_gate, "expert_up": expert_up, "expert_down": expert_down, "shared_gate": shared_gate, "shared_up": shared_up, "shared_down": shared_down}


def gated_mlp(inputs, gate_matrix, up_matrix, down_matrix):
    gate_part = jnp.dot(inputs, gate_matrix, preferred_element_type=jnp.float32)
    up_part = jnp.dot(inputs, up_matrix, preferred_element_type=jnp.float32)
    hidden = (jax.nn.silu(gate_part) * up_part).astype(jnp.bfloat16)
    return jnp.dot(hidden, down_matrix, preferred_element_type=jnp.float32).astype(jnp.bfloat16)


def gate_weights(gate_score):
    values = gate_score.astype(jnp.float32)
    return 2.5 * values / jnp.sum(values, axis=-1, keepdims=True)


def group_rank(group_ids):
    slot_width = group_ids.shape[-1]
    same_group = group_ids[..., :, None] == group_ids[..., None, :]
    earlier = jnp.arange(slot_width)[None, :] < jnp.arange(slot_width)[:, None]
    return jnp.sum(jnp.logical_and(same_group, earlier), axis=-1).astype(jnp.int32)


def combine_pairs(pair_rows, pair_weights):
    values = pair_rows.astype(jnp.float32)
    mixed = pair_weights[..., 0, None] * values[..., 0, :] + pair_weights[..., 1, None] * values[..., 1, :]
    return mixed.astype(jnp.bfloat16)


def reference(tokens, experts, gate_score, expert_gate, expert_up, expert_down, shared_gate, shared_up, shared_down):
    token_total = tokens.shape[0]
    device_total = N_OUTER * N_INNER
    per_expert = device_total * CAP
    weights = gate_weights(gate_score)
    blocks = experts.reshape(device_total, TOK_DEV, TOPK)
    expert_ids = jnp.arange(EXPERTS, dtype=jnp.int32)

    def block_ranks(device_block):
        matches = device_block[:, :, None] == expert_ids[None, None, :]
        named_mask = jnp.any(matches, axis=1).astype(jnp.int32)
        earlier = jnp.cumsum(named_mask, axis=0) - named_mask
        return jnp.sum(jnp.where(matches, earlier[:, None, :], 0), axis=2).astype(jnp.int32)

    slot_ranks = jax.vmap(block_ranks)(blocks).reshape(token_total, TOPK)
    device_of = (jnp.arange(token_total, dtype=jnp.int32) // TOK_DEV)[:, None]
    slot_index = (experts * per_expert + device_of * CAP + slot_ranks).astype(jnp.int32)
    owners = jnp.repeat(jnp.arange(token_total, dtype=jnp.int32), TOPK)
    row_table = jnp.full((EXPERTS * per_expert,), token_total, dtype=jnp.int32).at[slot_index.reshape(-1)].set(owners)
    padded = jnp.concatenate([tokens, jnp.zeros((1, D), tokens.dtype)], axis=0)

    def run_expert(operands):
        gate_matrix, up_matrix, down_matrix, expert_rows = operands
        return gated_mlp(padded[expert_rows], gate_matrix, up_matrix, down_matrix)

    outputs = lax.map(run_expert, (expert_gate, expert_up, expert_down, row_table.reshape(EXPERTS, per_expert)))
    flat_rows = outputs.reshape(EXPERTS * per_expert, D)
    group_ids = experts // N_INNER
    slot_rank = group_rank(group_ids)
    routed = jnp.zeros((token_total, D), jnp.float32)
    for group_index in range(N_OUTER):
        pair_rows = []
        pair_weights = []
        for second in range(2):
            picked = jnp.logical_and(group_ids == group_index, slot_rank == second)
            present = jnp.any(picked, axis=1)
            chosen = jnp.sum(jnp.where(picked, slot_index, 0), axis=1).astype(jnp.int32)
            pair_rows.append(jnp.where(present[:, None], flat_rows[chosen], jnp.zeros((), jnp.bfloat16)))
            pair_weights.append(jnp.sum(jnp.where(picked, weights, 0.0), axis=1))
        partial_value = combine_pairs(jnp.stack(pair_rows, axis=1), jnp.stack(pair_weights, axis=1))
        routed = routed + partial_value.astype(jnp.float32)
    gate_part = jnp.dot(tokens, shared_gate, preferred_element_type=jnp.float32)
    up_part = jnp.dot(tokens, shared_up, preferred_element_type=jnp.float32)
    shared_hidden = (jax.nn.silu(gate_part) * up_part).astype(jnp.bfloat16)
    shared = jnp.dot(shared_hidden, shared_down, preferred_element_type=jnp.float32)
    return (shared + routed).astype(jnp.bfloat16)
```

```python
import jax
import jax.numpy as jnp
from jax import lax
from jax.sharding import PartitionSpec as P

TOPK = 8
TOP_GROUPS = 4


def gated_mlp(inputs, gate_matrix, up_matrix, down_matrix):
    gate_part = jnp.dot(inputs, gate_matrix, preferred_element_type=jnp.float32)
    up_part = jnp.dot(inputs, up_matrix, preferred_element_type=jnp.float32)
    hidden = (jax.nn.silu(gate_part) * up_part).astype(jnp.bfloat16)
    return jnp.dot(hidden, down_matrix, preferred_element_type=jnp.float32).astype(jnp.bfloat16)


def gate_weights(gate_score):
    values = gate_score.astype(jnp.float32)
    return 2.5 * values / jnp.sum(values, axis=-1, keepdims=True)


def group_rank(group_ids):
    slot_width = group_ids.shape[-1]
    same_group = group_ids[..., :, None] == group_ids[..., None, :]
    earlier = jnp.arange(slot_width)[None, :] < jnp.arange(slot_width)[:, None]
    return jnp.sum(jnp.logical_and(same_group, earlier), axis=-1)


def combine_pairs(pair_rows, pair_weights):
    values = pair_rows.astype(jnp.float32)
    mixed = (
        pair_weights[..., 0, None] * values[..., 0, :]
        + pair_weights[..., 1, None] * values[..., 1, :]
    )
    return mixed.astype(jnp.bfloat16)


def rank_slots(matches):
    named_mask = jnp.any(matches, axis=-2).astype(jnp.int32)
    earlier = jnp.cumsum(named_mask, axis=-2) - named_mask
    slot_ranks = jnp.sum(jnp.where(matches, earlier[..., None, :], 0), axis=-1)
    return (named_mask, earlier, slot_ranks)


def pair_tables(group_ids, slot_rank, slot_index, weights, group_count):
    wanted = jnp.arange(group_count, dtype=jnp.int32)
    in_group = group_ids[..., None, None, :] == wanted[:, None, None]
    in_place = slot_rank[..., None, None, :] == jnp.arange(2, dtype=jnp.int32)[None, :, None]
    picked = jnp.logical_and(in_group, in_place)
    chosen = jnp.sum(jnp.where(picked, slot_index[..., None, None, :], 0), axis=-1)
    present = jnp.any(picked, axis=-1)
    pair_weights = jnp.sum(jnp.where(picked, weights[..., None, None, :], 0.0), axis=-1)
    return (chosen, present, pair_weights)


def per_device(
    tokens,
    experts,
    gate_score,
    expert_gate,
    expert_up,
    expert_down,
    shared_gate,
    shared_up,
    shared_down,
):
    row_count = tokens.shape[0]
    model_width = tokens.shape[1]
    inner_count = lax.axis_size("inner")
    outer_count = lax.axis_size("outer")
    capacity = TOPK // TOP_GROUPS * row_count // inner_count
    gate_matrix = expert_gate[0]
    up_matrix = expert_up[0]
    down_matrix = expert_down[0]
    tiled_tokens = jnp.broadcast_to(tokens[None], (inner_count,) + tokens.shape)
    segment = lax.all_to_all(
        tiled_tokens, "inner", split_axis=0, concat_axis=0, tiled=True
    ).reshape(inner_count * row_count, model_width)
    gate_part = jnp.dot(segment, shared_gate, preferred_element_type=jnp.float32)
    up_part = jnp.dot(segment, shared_up, preferred_element_type=jnp.float32)
    shared_hidden = (jax.nn.silu(gate_part) * up_part).astype(jnp.bfloat16)
    shared_partial = jnp.dot(
        shared_hidden, shared_down, preferred_element_type=jnp.float32
    ).astype(jnp.bfloat16)
    shared_parts = lax.all_to_all(
        shared_partial.reshape(inner_count, row_count, model_width),
        "inner",
        split_axis=0,
        concat_axis=0,
        tiled=True,
    )
    shared = jnp.sum(shared_parts.astype(jnp.float32), axis=0)
    weights = gate_weights(gate_score)
    group_ids = experts // inner_count
    slot_rank = group_rank(group_ids)
    total_count = inner_count * outer_count
    matches = experts[:, :, None] == jnp.arange(total_count, dtype=jnp.int32)[None, None, :]
    named_mask, earlier, slot_ranks = rank_slots(matches)
    slot_ids = jnp.arange(capacity, dtype=jnp.int32)[None, :, None]
    selector = jnp.logical_and(
        named_mask.T[:, None, :] == 1, earlier.T[:, None, :] == slot_ids
    ).astype(jnp.bfloat16)
    outbound = jnp.einsum(
        "ecr,rd->ecd", selector, tokens, preferred_element_type=jnp.float32
    ).astype(jnp.bfloat16)
    received = lax.all_to_all(outbound, ("outer", "inner"), split_axis=0, concat_axis=0, tiled=True)
    answer = gated_mlp(received.reshape(-1, model_width), gate_matrix, up_matrix, down_matrix)
    returned = lax.all_to_all(
        answer.reshape(received.shape), ("outer", "inner"), split_axis=0, concat_axis=0, tiled=True
    )
    flat_rows = returned.reshape(-1, model_width)
    slot_index = experts * capacity + slot_ranks
    chosen, present, pair_weights = pair_tables(
        group_ids, slot_rank, slot_index, weights, outer_count
    )
    pair_rows = jnp.where(present[..., None], flat_rows[chosen], jnp.zeros((), jnp.bfloat16))
    partial_value = combine_pairs(pair_rows, pair_weights)
    routed = jnp.sum(partial_value.astype(jnp.float32), axis=1)
    return (shared + routed).astype(jnp.bfloat16)


def solution(mesh):
    return jax.shard_map(
        per_device,
        mesh=mesh,
        in_specs=(
            P(("outer", "inner"), None),
            P(("outer", "inner"), None),
            P(("outer", "inner"), None),
            P(("outer", "inner"), None, None),
            P(("outer", "inner"), None, None),
            P(("outer", "inner"), None, None),
            P(None, "inner"),
            P(None, "inner"),
            P("inner", None),
        ),
        out_specs=P(("outer", "inner"), None),
        check_vma=False,
    )
```

```python
import functools

import jax
import jax.numpy as jnp
from jax import lax
from jax.experimental import pallas as pl
from jax.experimental.pallas import tpu as pltpu
from jax.sharding import PartitionSpec as P

TOPK = 8
TOP_GROUPS = 4
MESH_ID = pl.DeviceIdType.MESH
ALL_AXES = ("outer", "inner")


def flat_index(axes, sizes):
    index = 0
    for axis, size in zip(axes, sizes):
        index = index * size + lax.axis_index(axis)
    return index


def mesh_coords(flat, axes, sizes):
    coords = []
    for size in reversed(sizes):
        coords.append(flat % size)
        flat = flat // size
    return dict(zip(axes, reversed(coords)))


def exchange_kernel(plans, sizes, *refs):
    count = len(plans)
    sends = refs[:count]
    recvs = refs[count:2 * count]
    send_sems = refs[2 * count:3 * count]
    recv_sems = refs[3 * count:4 * count]
    local_sems = refs[4 * count]
    axis_size = dict(zip(ALL_AXES, sizes))
    world = sizes[0] * sizes[1]
    world_me = flat_index(ALL_AXES, sizes)

    barrier = pltpu.get_barrier_semaphore()

    @pl.loop(1, world)
    def _(step):
        peer = lax.rem(world_me + step, world)
        pl.semaphore_signal(
            barrier, inc=1, device_id=mesh_coords(peer, ALL_AXES, sizes),
            device_id_type=MESH_ID,
        )

    pl.semaphore_wait(barrier, world - 1)

    def block(ref, index, rows, same):
        if same:
            return ref
        return ref.at[pl.ds(index * rows, rows)]

    locals_ = []
    for k, (axes, rows, same) in enumerate(plans):
        axis_sizes = tuple(axis_size[a] for a in axes)
        me = flat_index(axes, axis_sizes)
        local = pltpu.make_async_copy(
            block(sends[k], me, rows, same), recvs[k].at[pl.ds(me * rows, rows)],
            local_sems.at[k],
        )
        local.start()
        locals_.append(local)

    for k, (axes, rows, same) in enumerate(plans):
        axis_sizes = tuple(axis_size[a] for a in axes)
        n = 1
        for size in axis_sizes:
            n *= size
        me = flat_index(axes, axis_sizes)

        @pl.loop(1, n)
        def _(step):
            peer = lax.rem(me + step, n)
            pltpu.make_async_remote_copy(
                src_ref=block(sends[k], peer, rows, same),
                dst_ref=recvs[k].at[pl.ds(me * rows, rows)],
                send_sem=send_sems[k].at[peer],
                recv_sem=recv_sems[k].at[me],
                device_id=mesh_coords(peer, axes, axis_sizes),
                device_id_type=MESH_ID,
            ).start()

    for k, (axes, rows, same) in enumerate(plans):
        axis_sizes = tuple(axis_size[a] for a in axes)
        n = 1
        for size in axis_sizes:
            n *= size
        me = flat_index(axes, axis_sizes)

        @pl.loop(1, n)
        def _(step):
            peer = lax.rem(me + step, n)
            pltpu.make_async_remote_copy(
                src_ref=block(sends[k], peer, rows, same),
                dst_ref=recvs[k].at[pl.ds(peer * rows, rows)],
                send_sem=send_sems[k].at[peer],
                recv_sem=recv_sems[k].at[peer],
                device_id=mesh_coords(peer, axes, axis_sizes),
                device_id_type=MESH_ID,
            ).wait()

    for local in locals_:
        local.wait()


def exchange(sends, plans, collective_id):
    sizes = (lax.axis_size("outer"), lax.axis_size("inner"))
    axis_size = dict(zip(ALL_AXES, sizes))
    out_shapes = []
    sem_shapes = []
    for send, (axes, rows, same) in zip(sends, plans):
        n = 1
        for a in axes:
            n *= axis_size[a]
        out_shapes.append(jax.ShapeDtypeStruct((n * rows,) + send.shape[1:], send.dtype))
        sem_shapes.append(n)
    return pl.pallas_call(
        functools.partial(exchange_kernel, plans, sizes),
        out_shape=tuple(out_shapes),
        in_specs=[pl.BlockSpec(memory_space=pl.ANY)] * len(sends),
        out_specs=tuple(pl.BlockSpec(memory_space=pl.ANY) for _ in sends),
        scratch_shapes=[pltpu.SemaphoreType.DMA((n,)) for n in sem_shapes]
        + [pltpu.SemaphoreType.DMA((n,)) for n in sem_shapes]
        + [pltpu.SemaphoreType.DMA((len(sends),))],
        compiler_params=pltpu.CompilerParams(
            collective_id=collective_id, has_side_effects=True
        ),
    )(*sends)


def gated_mlp(inputs, gate_matrix, up_matrix, down_matrix):
    gate_part = jnp.dot(inputs, gate_matrix, preferred_element_type=jnp.float32)
    up_part = jnp.dot(inputs, up_matrix, preferred_element_type=jnp.float32)
    hidden = (jax.nn.silu(gate_part) * up_part).astype(jnp.bfloat16)
    return jnp.dot(hidden, down_matrix, preferred_element_type=jnp.float32).astype(jnp.bfloat16)


def gate_weights(gate_score):
    values = gate_score.astype(jnp.float32)
    return 2.5 * values / jnp.sum(values, axis=-1, keepdims=True)


def group_rank(group_ids):
    slot_width = group_ids.shape[-1]
    same_group = group_ids[..., :, None] == group_ids[..., None, :]
    earlier = jnp.arange(slot_width)[None, :] < jnp.arange(slot_width)[:, None]
    return jnp.sum(jnp.logical_and(same_group, earlier), axis=-1)


def combine_pairs(pair_rows, pair_weights):
    values = pair_rows.astype(jnp.float32)
    mixed = (
        pair_weights[..., 0, None] * values[..., 0, :]
        + pair_weights[..., 1, None] * values[..., 1, :]
    )
    return mixed.astype(jnp.bfloat16)


def rank_slots(matches):
    named_mask = jnp.any(matches, axis=-2).astype(jnp.int32)
    earlier = jnp.cumsum(named_mask, axis=-2) - named_mask
    slot_ranks = jnp.sum(jnp.where(matches, earlier[..., None, :], 0), axis=-1)
    return (named_mask, earlier, slot_ranks)


def pair_tables(group_ids, slot_rank, slot_index, weights, group_count):
    wanted = jnp.arange(group_count, dtype=jnp.int32)
    in_group = group_ids[..., None, None, :] == wanted[:, None, None]
    in_place = slot_rank[..., None, None, :] == jnp.arange(2, dtype=jnp.int32)[None, :, None]
    picked = jnp.logical_and(in_group, in_place)
    chosen = jnp.sum(jnp.where(picked, slot_index[..., None, None, :], 0), axis=-1)
    present = jnp.any(picked, axis=-1)
    pair_weights = jnp.sum(jnp.where(picked, weights[..., None, None, :], 0.0), axis=-1)
    return (chosen, present, pair_weights)


def per_device(
    tokens,
    experts,
    gate_score,
    expert_gate,
    expert_up,
    expert_down,
    shared_gate,
    shared_up,
    shared_down,
):
    row_count = tokens.shape[0]
    model_width = tokens.shape[1]
    inner_count = lax.axis_size("inner")
    outer_count = lax.axis_size("outer")
    capacity = TOPK // TOP_GROUPS * row_count // inner_count
    total_count = inner_count * outer_count
    weights = gate_weights(gate_score)
    group_ids = experts // inner_count
    slot_rank = group_rank(group_ids)
    matches = experts[:, :, None] == jnp.arange(total_count, dtype=jnp.int32)[None, None, :]
    named_mask, earlier, slot_ranks = rank_slots(matches)
    slot_ids = jnp.arange(capacity, dtype=jnp.int32)[None, :, None]
    selector = jnp.logical_and(
        named_mask.T[:, None, :] == 1, earlier.T[:, None, :] == slot_ids
    ).astype(jnp.bfloat16).reshape(total_count * capacity, row_count)
    outbound = jnp.dot(selector, tokens, preferred_element_type=jnp.float32).astype(
        jnp.bfloat16
    )
    segment, received = exchange(
        [tokens, outbound],
        [(("inner",), row_count, True), (ALL_AXES, capacity, False)],
        0,
    )
    gate_part = jnp.dot(segment, shared_gate, preferred_element_type=jnp.float32)
    up_part = jnp.dot(segment, shared_up, preferred_element_type=jnp.float32)
    shared_hidden = (jax.nn.silu(gate_part) * up_part).astype(jnp.bfloat16)
    shared_partial = jnp.dot(
        shared_hidden, shared_down, preferred_element_type=jnp.float32
    ).astype(jnp.bfloat16)
    answer = gated_mlp(received, expert_gate[0], expert_up[0], expert_down[0])
    shared_parts, flat_rows = exchange(
        [shared_partial, answer],
        [(("inner",), row_count, False), (ALL_AXES, capacity, False)],
        1,
    )
    shared = jnp.sum(
        shared_parts.reshape(inner_count, row_count, model_width).astype(jnp.float32),
        axis=0,
    )
    slot_index = experts * capacity + slot_ranks
    chosen, present, pair_weights = pair_tables(
        group_ids, slot_rank, slot_index, weights, outer_count
    )
    pair_rows = jnp.where(present[..., None], flat_rows[chosen], jnp.zeros((), jnp.bfloat16))
    partial_value = combine_pairs(pair_rows, pair_weights)
    routed = jnp.sum(partial_value.astype(jnp.float32), axis=1)
    return (shared + routed).astype(jnp.bfloat16)


def solution(mesh):
    return jax.shard_map(
        per_device,
        mesh=mesh,
        in_specs=(
            P(("outer", "inner"), None),
            P(("outer", "inner"), None),
            P(("outer", "inner"), None),
            P(("outer", "inner"), None, None),
            P(("outer", "inner"), None, None),
            P(("outer", "inner"), None, None),
            P(None, "inner"),
            P(None, "inner"),
            P("inner", None),
        ),
        out_specs=P(("outer", "inner"), None),
        check_vma=False,
    )
```

```python
import functools

import jax
import jax.numpy as jnp
from jax import lax
from jax.experimental import pallas as pl
from jax.experimental.pallas import tpu as pltpu
from jax.sharding import PartitionSpec as P

TOPK = 8
TOP_GROUPS = 4
MESH_ID = pl.DeviceIdType.MESH
ALL_AXES = ("outer", "inner")


def flat_index(axes, sizes):
    index = 0
    for axis, size in zip(axes, sizes):
        index = index * size + lax.axis_index(axis)
    return index


def mesh_coords(flat, axes, sizes):
    coords = []
    for size in reversed(sizes):
        coords.append(flat % size)
        flat = flat // size
    return dict(zip(axes, reversed(coords)))


def exchange_kernel(plans, sizes, *refs):
    count = len(plans)
    sends = refs[:count]
    recvs = refs[count:2 * count]
    send_sems = refs[2 * count:3 * count]
    recv_sems = refs[3 * count:4 * count]
    local_sems = refs[4 * count]
    axis_size = dict(zip(ALL_AXES, sizes))
    greet_axes = max((axes for axes, _, _ in plans), key=len)
    greet_sizes = tuple(axis_size[a] for a in greet_axes)
    world = 1
    for size in greet_sizes:
        world *= size
    world_me = flat_index(greet_axes, greet_sizes)

    barrier = pltpu.get_barrier_semaphore()

    @pl.loop(1, world)
    def _(step):
        peer = lax.rem(world_me + step, world)
        pl.semaphore_signal(
            barrier, inc=1, device_id=mesh_coords(peer, greet_axes, greet_sizes),
            device_id_type=MESH_ID,
        )

    pl.semaphore_wait(barrier, world - 1)

    def block(ref, index, rows, same):
        if same:
            return ref
        return ref.at[pl.ds(index * rows, rows)]

    locals_ = []
    for k, (axes, rows, same) in enumerate(plans):
        axis_sizes = tuple(axis_size[a] for a in axes)
        me = flat_index(axes, axis_sizes)
        local = pltpu.make_async_copy(
            block(sends[k], me, rows, same), recvs[k].at[pl.ds(me * rows, rows)],
            local_sems.at[k],
        )
        local.start()
        locals_.append(local)

    for k, (axes, rows, same) in enumerate(plans):
        axis_sizes = tuple(axis_size[a] for a in axes)
        n = 1
        for size in axis_sizes:
            n *= size
        me = flat_index(axes, axis_sizes)

        @pl.loop(1, n)
        def _(step):
            peer = lax.rem(me + step, n)
            pltpu.make_async_remote_copy(
                src_ref=block(sends[k], peer, rows, same),
                dst_ref=recvs[k].at[pl.ds(me * rows, rows)],
                send_sem=send_sems[k].at[peer],
                recv_sem=recv_sems[k].at[me],
                device_id=mesh_coords(peer, axes, axis_sizes),
                device_id_type=MESH_ID,
            ).start()

    for k, (axes, rows, same) in enumerate(plans):
        axis_sizes = tuple(axis_size[a] for a in axes)
        n = 1
        for size in axis_sizes:
            n *= size
        me = flat_index(axes, axis_sizes)

        @pl.loop(1, n)
        def _(step):
            peer = lax.rem(me + step, n)
            pltpu.make_async_remote_copy(
                src_ref=block(sends[k], peer, rows, same),
                dst_ref=recvs[k].at[pl.ds(peer * rows, rows)],
                send_sem=send_sems[k].at[peer],
                recv_sem=recv_sems[k].at[peer],
                device_id=mesh_coords(peer, axes, axis_sizes),
                device_id_type=MESH_ID,
            ).wait()

    for local in locals_:
        local.wait()


def exchange(sends, plans, collective_id):
    sizes = (lax.axis_size("outer"), lax.axis_size("inner"))
    axis_size = dict(zip(ALL_AXES, sizes))
    out_shapes = []
    sem_shapes = []
    for send, (axes, rows, same) in zip(sends, plans):
        n = 1
        for a in axes:
            n *= axis_size[a]
        out_shapes.append(jax.ShapeDtypeStruct((n * rows,) + send.shape[1:], send.dtype))
        sem_shapes.append(n)
    return pl.pallas_call(
        functools.partial(exchange_kernel, plans, sizes),
        out_shape=tuple(out_shapes),
        in_specs=[pl.BlockSpec(memory_space=pl.ANY)] * len(sends),
        out_specs=tuple(pl.BlockSpec(memory_space=pl.ANY) for _ in sends),
        scratch_shapes=[pltpu.SemaphoreType.DMA((n,)) for n in sem_shapes]
        + [pltpu.SemaphoreType.DMA((n,)) for n in sem_shapes]
        + [pltpu.SemaphoreType.DMA((len(sends),))],
        compiler_params=pltpu.CompilerParams(
            collective_id=collective_id, has_side_effects=True
        ),
    )(*sends)


def gated_mlp(inputs, gate_matrix, up_matrix, down_matrix):
    gate_part = jnp.dot(inputs, gate_matrix, preferred_element_type=jnp.float32)
    up_part = jnp.dot(inputs, up_matrix, preferred_element_type=jnp.float32)
    hidden = (jax.nn.silu(gate_part) * up_part).astype(jnp.bfloat16)
    return jnp.dot(hidden, down_matrix, preferred_element_type=jnp.float32).astype(jnp.bfloat16)


def gate_weights(gate_score):
    values = gate_score.astype(jnp.float32)
    return 2.5 * values / jnp.sum(values, axis=-1, keepdims=True)


def group_rank(group_ids):
    slot_width = group_ids.shape[-1]
    same_group = group_ids[..., :, None] == group_ids[..., None, :]
    earlier = jnp.arange(slot_width)[None, :] < jnp.arange(slot_width)[:, None]
    return jnp.sum(jnp.logical_and(same_group, earlier), axis=-1)


def combine_pairs(pair_rows, pair_weights):
    values = pair_rows.astype(jnp.float32)
    mixed = (
        pair_weights[..., 0, None] * values[..., 0, :]
        + pair_weights[..., 1, None] * values[..., 1, :]
    )
    return mixed.astype(jnp.bfloat16)


def rank_slots(matches):
    named_mask = jnp.any(matches, axis=-2).astype(jnp.int32)
    earlier = jnp.cumsum(named_mask, axis=-2) - named_mask
    slot_ranks = jnp.sum(jnp.where(matches, earlier[..., None, :], 0), axis=-1)
    return (named_mask, earlier, slot_ranks)


def pair_tables(group_ids, slot_rank, slot_index, weights, group_count):
    wanted = jnp.arange(group_count, dtype=jnp.int32)
    in_group = group_ids[..., None, None, :] == wanted[:, None, None]
    in_place = slot_rank[..., None, None, :] == jnp.arange(2, dtype=jnp.int32)[None, :, None]
    picked = jnp.logical_and(in_group, in_place)
    chosen = jnp.sum(jnp.where(picked, slot_index[..., None, None, :], 0), axis=-1)
    present = jnp.any(picked, axis=-1)
    pair_weights = jnp.sum(jnp.where(picked, weights[..., None, None, :], 0.0), axis=-1)
    return (chosen, present, pair_weights)


def per_device(
    tokens,
    experts,
    gate_score,
    expert_gate,
    expert_up,
    expert_down,
    shared_gate,
    shared_up,
    shared_down,
):
    row_count = tokens.shape[0]
    model_width = tokens.shape[1]
    inner_count = lax.axis_size("inner")
    outer_count = lax.axis_size("outer")
    capacity = TOPK // TOP_GROUPS * row_count // inner_count
    total_count = inner_count * outer_count
    weights = gate_weights(gate_score)
    group_ids = experts // inner_count
    slot_rank = group_rank(group_ids)
    matches = experts[:, :, None] == jnp.arange(total_count, dtype=jnp.int32)[None, None, :]
    named_mask, earlier, slot_ranks = rank_slots(matches)
    slot_ids = jnp.arange(capacity, dtype=jnp.int32)[None, :, None]
    selector = jnp.logical_and(
        named_mask.T[:, None, :] == 1, earlier.T[:, None, :] == slot_ids
    ).astype(jnp.bfloat16).reshape(total_count * capacity, row_count)
    outbound = jnp.dot(selector, tokens, preferred_element_type=jnp.float32).astype(
        jnp.bfloat16
    )
    received = lax.all_to_all(
        outbound.reshape(total_count, capacity, model_width),
        ALL_AXES, split_axis=0, concat_axis=0, tiled=True,
    ).reshape(total_count * capacity, model_width)
    (segment,) = exchange([tokens], [(("inner",), row_count, True)], 0)
    gate_part = jnp.dot(segment, shared_gate, preferred_element_type=jnp.float32)
    up_part = jnp.dot(segment, shared_up, preferred_element_type=jnp.float32)
    shared_hidden = (jax.nn.silu(gate_part) * up_part).astype(jnp.bfloat16)
    shared_partial = jnp.dot(
        shared_hidden, shared_down, preferred_element_type=jnp.float32
    ).astype(jnp.bfloat16)
    answer = gated_mlp(received, expert_gate[0], expert_up[0], expert_down[0])
    flat_rows = lax.all_to_all(
        answer.reshape(total_count, capacity, model_width),
        ALL_AXES, split_axis=0, concat_axis=0, tiled=True,
    ).reshape(total_count * capacity, model_width)
    (shared_parts,) = exchange([shared_partial], [(("inner",), row_count, False)], 1)
    shared = jnp.sum(
        shared_parts.reshape(inner_count, row_count, model_width).astype(jnp.float32),
        axis=0,
    )
    slot_index = experts * capacity + slot_ranks
    chosen, present, pair_weights = pair_tables(
        group_ids, slot_rank, slot_index, weights, outer_count
    )
    pair_rows = jnp.where(present[..., None], flat_rows[chosen], jnp.zeros((), jnp.bfloat16))
    partial_value = combine_pairs(pair_rows, pair_weights)
    routed = jnp.sum(partial_value.astype(jnp.float32), axis=1)
    return (shared + routed).astype(jnp.bfloat16)


def solution(mesh):
    return jax.shard_map(
        per_device,
        mesh=mesh,
        in_specs=(
            P(("outer", "inner"), None),
            P(("outer", "inner"), None),
            P(("outer", "inner"), None),
            P(("outer", "inner"), None, None),
            P(("outer", "inner"), None, None),
            P(("outer", "inner"), None, None),
            P(None, "inner"),
            P(None, "inner"),
            P("inner", None),
        ),
        out_specs=P(("outer", "inner"), None),
        check_vma=False,
    )
```

```python
import functools
import math

import jax
import jax.numpy as jnp
from jax import lax
from jax.experimental import pallas as pl
from jax.experimental.pallas import tpu as pltpu
from jax.sharding import PartitionSpec as P

TOPK = 8
TOP_GROUPS = 4
MESH_ID = pl.DeviceIdType.MESH


def torus_gather_kernel(side, tokens_ref, out_ref, send_sems, recv_sems, local_sems):
    me = lax.axis_index("inner")
    z, y = me // side, me % side
    half = tokens_ref.shape[0] // 2

    def node(zz, yy):
        return lax.rem(zz + side, side) * side + lax.rem(yy + side, side)

    steps = [
        (lambda zz, yy, k: node(zz, yy + k), lambda zz, yy, k: node(zz + k, yy)),
        (lambda zz, yy, k: node(zz + k, yy), lambda zz, yy, k: node(zz, yy + k)),
    ]
    neighbours = [node(z, y + 1), node(z, y - 1), node(z + 1, y), node(z - 1, y)]
    barrier = pltpu.get_barrier_semaphore()
    for peer in neighbours:
        pl.semaphore_signal(barrier, inc=1, device_id={"inner": peer}, device_id_type=MESH_ID)
    pl.semaphore_wait(barrier, len(neighbours))

    rows = [pl.ds(0, half), pl.ds(half, half)]
    for h in range(2):
        pltpu.make_async_copy(
            tokens_ref.at[rows[h]], out_ref.at[me, rows[h]], local_sems.at[h]
        ).start()

    counter = [0]

    def run_round(moves):
        started = []
        for block, h, dest, from_tokens in moves:
            index = counter[0]
            counter[0] += 1
            src = tokens_ref.at[rows[h]] if from_tokens else out_ref.at[block, rows[h]]
            copy = pltpu.make_async_remote_copy(
                src_ref=src,
                dst_ref=out_ref.at[block, rows[h]],
                send_sem=send_sems.at[index],
                recv_sem=recv_sems.at[index],
                device_id={"inner": dest},
                device_id_type=MESH_ID,
            )
            copy.start()
            started.append(copy)
        return started

    def finish(started, incoming):
        for copy in started:
            copy.wait_send()
        for index, block, h, sender in incoming:
            pltpu.make_async_remote_copy(
                src_ref=out_ref.at[block, rows[h]],
                dst_ref=out_ref.at[block, rows[h]],
                send_sem=send_sems.at[index],
                recv_sem=recv_sems.at[index],
                device_id={"inner": sender},
                device_id_type=MESH_ID,
            ).wait_recv()

    base = counter[0]
    moves, incoming = [], []
    for h in range(2):
        first = steps[h][0]
        for k in (1, -1):
            moves.append((me, h, first(z, y, k), True))
            incoming.append((base + len(incoming), first(z, y, -k), h, first(z, y, -k)))
    finish(run_round(moves), incoming)
    base = counter[0]
    moves, incoming = [], []
    for h in range(2):
        first = steps[h][0]
        moves.append((first(z, y, -1), h, first(z, y, 1), False))
        incoming.append((base + len(incoming), first(z, y, -2), h, first(z, y, -1)))
    finish(run_round(moves), incoming)
    for h in range(2):
        pltpu.make_async_copy(
            tokens_ref.at[rows[h]], out_ref.at[me, rows[h]], local_sems.at[h]
        ).wait()
    base = counter[0]
    moves, incoming = [], []
    for h in range(2):
        first, second = steps[h]
        for k in (1, -1):
            for j in range(side):
                moves.append((first(z, y, j), h, second(z, y, k), False))
                origin = second(z, y, -k)
                oz, oy = origin // side, origin % side
                incoming.append((base + len(incoming), first(oz, oy, j), h, origin))
    finish(run_round(moves), incoming)
    base = counter[0]
    moves, incoming = [], []
    for h in range(2):
        first, second = steps[h]
        src_node = second(z, y, -1)
        sz, sy = src_node // side, src_node % side
        far = second(z, y, -2)
        fz, fy = far // side, far % side
        for j in range(side):
            moves.append((first(sz, sy, j), h, second(z, y, 1), False))
            incoming.append((base + len(incoming), first(fz, fy, j), h, src_node))
    finish(run_round(moves), incoming)


def torus_gather(tokens, side, collective_id):
    count = lax.axis_size("inner")
    copies = 4 + 2 + 4 * side + 2 * side
    return pl.pallas_call(
        functools.partial(torus_gather_kernel, side),
        out_shape=jax.ShapeDtypeStruct((count,) + tokens.shape, tokens.dtype),
        in_specs=[pl.BlockSpec(memory_space=pl.ANY)],
        out_specs=pl.BlockSpec(memory_space=pl.ANY),
        scratch_shapes=[
            pltpu.SemaphoreType.DMA((copies,)),
            pltpu.SemaphoreType.DMA((copies,)),
            pltpu.SemaphoreType.DMA((2,)),
        ],
        compiler_params=pltpu.CompilerParams(
            collective_id=collective_id, has_side_effects=True
        ),
    )(tokens)


def gated_mlp(inputs, gate_matrix, up_matrix, down_matrix):
    gate_part = jnp.dot(inputs, gate_matrix, preferred_element_type=jnp.float32)
    up_part = jnp.dot(inputs, up_matrix, preferred_element_type=jnp.float32)
    hidden = (jax.nn.silu(gate_part) * up_part).astype(jnp.bfloat16)
    return jnp.dot(hidden, down_matrix, preferred_element_type=jnp.float32).astype(jnp.bfloat16)


def gate_weights(gate_score):
    values = gate_score.astype(jnp.float32)
    return 2.5 * values / jnp.sum(values, axis=-1, keepdims=True)


def group_rank(group_ids):
    slot_width = group_ids.shape[-1]
    same_group = group_ids[..., :, None] == group_ids[..., None, :]
    earlier = jnp.arange(slot_width)[None, :] < jnp.arange(slot_width)[:, None]
    return jnp.sum(jnp.logical_and(same_group, earlier), axis=-1)


def combine_pairs(pair_rows, pair_weights):
    values = pair_rows.astype(jnp.float32)
    mixed = (
        pair_weights[..., 0, None] * values[..., 0, :]
        + pair_weights[..., 1, None] * values[..., 1, :]
    )
    return mixed.astype(jnp.bfloat16)


def rank_slots(matches):
    named_mask = jnp.any(matches, axis=-2).astype(jnp.int32)
    earlier = jnp.cumsum(named_mask, axis=-2) - named_mask
    slot_ranks = jnp.sum(jnp.where(matches, earlier[..., None, :], 0), axis=-1)
    return (named_mask, earlier, slot_ranks)


def pair_tables(group_ids, slot_rank, slot_index, weights, group_count):
    wanted = jnp.arange(group_count, dtype=jnp.int32)
    in_group = group_ids[..., None, None, :] == wanted[:, None, None]
    in_place = slot_rank[..., None, None, :] == jnp.arange(2, dtype=jnp.int32)[None, :, None]
    picked = jnp.logical_and(in_group, in_place)
    chosen = jnp.sum(jnp.where(picked, slot_index[..., None, None, :], 0), axis=-1)
    present = jnp.any(picked, axis=-1)
    pair_weights = jnp.sum(jnp.where(picked, weights[..., None, None, :], 0.0), axis=-1)
    return (chosen, present, pair_weights)


def per_device(
    tokens,
    experts,
    gate_score,
    expert_gate,
    expert_up,
    expert_down,
    shared_gate,
    shared_up,
    shared_down,
):
    row_count = tokens.shape[0]
    model_width = tokens.shape[1]
    inner_count = lax.axis_size("inner")
    outer_count = lax.axis_size("outer")
    capacity = TOPK // TOP_GROUPS * row_count // inner_count
    gate_matrix = expert_gate[0]
    up_matrix = expert_up[0]
    down_matrix = expert_down[0]
    side = math.isqrt(inner_count)
    segment = torus_gather(tokens, side, 0).reshape(inner_count * row_count, model_width)
    gate_part = jnp.dot(segment, shared_gate, preferred_element_type=jnp.float32)
    up_part = jnp.dot(segment, shared_up, preferred_element_type=jnp.float32)
    shared_hidden = (jax.nn.silu(gate_part) * up_part).astype(jnp.bfloat16)
    shared_partial = jnp.dot(
        shared_hidden, shared_down, preferred_element_type=jnp.float32
    ).astype(jnp.bfloat16)
    shared_parts = lax.all_to_all(
        shared_partial.reshape(inner_count, row_count, model_width),
        "inner",
        split_axis=0,
        concat_axis=0,
        tiled=True,
    )
    shared = jnp.sum(shared_parts.astype(jnp.float32), axis=0)
    weights = gate_weights(gate_score)
    group_ids = experts // inner_count
    slot_rank = group_rank(group_ids)
    total_count = inner_count * outer_count
    matches = experts[:, :, None] == jnp.arange(total_count, dtype=jnp.int32)[None, None, :]
    named_mask, earlier, slot_ranks = rank_slots(matches)
    slot_ids = jnp.arange(capacity, dtype=jnp.int32)[None, :, None]
    selector = jnp.logical_and(
        named_mask.T[:, None, :] == 1, earlier.T[:, None, :] == slot_ids
    ).astype(jnp.bfloat16)
    outbound = jnp.einsum(
        "ecr,rd->ecd", selector, tokens, preferred_element_type=jnp.float32
    ).astype(jnp.bfloat16)
    received = lax.all_to_all(outbound, ("outer", "inner"), split_axis=0, concat_axis=0, tiled=True)
    answer = gated_mlp(received.reshape(-1, model_width), gate_matrix, up_matrix, down_matrix)
    returned = lax.all_to_all(
        answer.reshape(received.shape), ("outer", "inner"), split_axis=0, concat_axis=0, tiled=True
    )
    flat_rows = returned.reshape(-1, model_width)
    slot_index = experts * capacity + slot_ranks
    chosen, present, pair_weights = pair_tables(
        group_ids, slot_rank, slot_index, weights, outer_count
    )
    pair_rows = jnp.where(present[..., None], flat_rows[chosen], jnp.zeros((), jnp.bfloat16))
    partial_value = combine_pairs(pair_rows, pair_weights)
    routed = jnp.sum(partial_value.astype(jnp.float32), axis=1)
    return (shared + routed).astype(jnp.bfloat16)


def solution(mesh):
    return jax.shard_map(
        per_device,
        mesh=mesh,
        in_specs=(
            P(("outer", "inner"), None),
            P(("outer", "inner"), None),
            P(("outer", "inner"), None),
            P(("outer", "inner"), None, None),
            P(("outer", "inner"), None, None),
            P(("outer", "inner"), None, None),
            P(None, "inner"),
            P(None, "inner"),
            P("inner", None),
        ),
        out_specs=P(("outer", "inner"), None),
        check_vma=False,
    )
```

```python
import functools
import math

import jax
import jax.numpy as jnp
from jax import lax
from jax.experimental import pallas as pl
from jax.experimental.pallas import tpu as pltpu
from jax.sharding import PartitionSpec as P

TOPK = 8
TOP_GROUPS = 4
MESH_ID = pl.DeviceIdType.MESH

ALL_AXES = ("outer", "inner")


def flat_index(axes, sizes):
    index = 0
    for axis, size in zip(axes, sizes):
        index = index * size + lax.axis_index(axis)
    return index


def mesh_coords(flat, axes, sizes):
    coords = []
    for size in reversed(sizes):
        coords.append(flat % size)
        flat = flat // size
    return dict(zip(axes, reversed(coords)))


def exchange_kernel(plans, sizes, *refs):
    count = len(plans)
    sends = refs[:count]
    recvs = refs[count:2 * count]
    send_sems = refs[2 * count:3 * count]
    recv_sems = refs[3 * count:4 * count]
    local_sems = refs[4 * count]
    axis_size = dict(zip(ALL_AXES, sizes))
    world = sizes[0] * sizes[1]
    world_me = flat_index(ALL_AXES, sizes)

    barrier = pltpu.get_barrier_semaphore()

    @pl.loop(1, world)
    def _(step):
        peer = lax.rem(world_me + step, world)
        pl.semaphore_signal(
            barrier, inc=1, device_id=mesh_coords(peer, ALL_AXES, sizes),
            device_id_type=MESH_ID,
        )

    pl.semaphore_wait(barrier, world - 1)

    def block(ref, index, rows, same):
        if same:
            return ref
        return ref.at[pl.ds(index * rows, rows)]

    locals_ = []
    for k, (axes, rows, same) in enumerate(plans):
        axis_sizes = tuple(axis_size[a] for a in axes)
        me = flat_index(axes, axis_sizes)
        local = pltpu.make_async_copy(
            block(sends[k], me, rows, same), recvs[k].at[pl.ds(me * rows, rows)],
            local_sems.at[k],
        )
        local.start()
        locals_.append(local)

    for k, (axes, rows, same) in enumerate(plans):
        axis_sizes = tuple(axis_size[a] for a in axes)
        n = 1
        for size in axis_sizes:
            n *= size
        me = flat_index(axes, axis_sizes)

        @pl.loop(1, n)
        def _(step):
            peer = lax.rem(me + step, n)
            pltpu.make_async_remote_copy(
                src_ref=block(sends[k], peer, rows, same),
                dst_ref=recvs[k].at[pl.ds(me * rows, rows)],
                send_sem=send_sems[k].at[peer],
                recv_sem=recv_sems[k].at[me],
                device_id=mesh_coords(peer, axes, axis_sizes),
                device_id_type=MESH_ID,
            ).start()

    for k, (axes, rows, same) in enumerate(plans):
        axis_sizes = tuple(axis_size[a] for a in axes)
        n = 1
        for size in axis_sizes:
            n *= size
        me = flat_index(axes, axis_sizes)

        @pl.loop(1, n)
        def _(step):
            peer = lax.rem(me + step, n)
            pltpu.make_async_remote_copy(
                src_ref=block(sends[k], peer, rows, same),
                dst_ref=recvs[k].at[pl.ds(peer * rows, rows)],
                send_sem=send_sems[k].at[peer],
                recv_sem=recv_sems[k].at[peer],
                device_id=mesh_coords(peer, axes, axis_sizes),
                device_id_type=MESH_ID,
            ).wait()

    for local in locals_:
        local.wait()


def exchange(sends, plans, collective_id):
    sizes = (lax.axis_size("outer"), lax.axis_size("inner"))
    axis_size = dict(zip(ALL_AXES, sizes))
    out_shapes = []
    sem_shapes = []
    for send, (axes, rows, same) in zip(sends, plans):
        n = 1
        for a in axes:
            n *= axis_size[a]
        out_shapes.append(jax.ShapeDtypeStruct((n * rows,) + send.shape[1:], send.dtype))
        sem_shapes.append(n)
    return pl.pallas_call(
        functools.partial(exchange_kernel, plans, sizes),
        out_shape=tuple(out_shapes),
        in_specs=[pl.BlockSpec(memory_space=pl.ANY)] * len(sends),
        out_specs=tuple(pl.BlockSpec(memory_space=pl.ANY) for _ in sends),
        scratch_shapes=[pltpu.SemaphoreType.DMA((n,)) for n in sem_shapes]
        + [pltpu.SemaphoreType.DMA((n,)) for n in sem_shapes]
        + [pltpu.SemaphoreType.DMA((len(sends),))],
        compiler_params=pltpu.CompilerParams(
            collective_id=collective_id, has_side_effects=True
        ),
    )(*sends)


def torus_gather_kernel(side, tokens_ref, out_ref, send_sems, recv_sems, local_sems):
    me = lax.axis_index("inner")
    z, y = me // side, me % side
    half = tokens_ref.shape[0] // 2

    def node(zz, yy):
        return lax.rem(zz + side, side) * side + lax.rem(yy + side, side)

    steps = [
        (lambda zz, yy, k: node(zz, yy + k), lambda zz, yy, k: node(zz + k, yy)),
        (lambda zz, yy, k: node(zz + k, yy), lambda zz, yy, k: node(zz, yy + k)),
    ]
    neighbours = [node(z, y + 1), node(z, y - 1), node(z + 1, y), node(z - 1, y)]
    barrier = pltpu.get_barrier_semaphore()
    for peer in neighbours:
        pl.semaphore_signal(barrier, inc=1, device_id={"inner": peer}, device_id_type=MESH_ID)
    pl.semaphore_wait(barrier, len(neighbours))

    rows = [pl.ds(0, half), pl.ds(half, half)]
    for h in range(2):
        pltpu.make_async_copy(
            tokens_ref.at[rows[h]], out_ref.at[me, rows[h]], local_sems.at[h]
        ).start()

    counter = [0]

    def run_round(moves):
        started = []
        for block, h, dest, from_tokens in moves:
            index = counter[0]
            counter[0] += 1
            src = tokens_ref.at[rows[h]] if from_tokens else out_ref.at[block, rows[h]]
            copy = pltpu.make_async_remote_copy(
                src_ref=src,
                dst_ref=out_ref.at[block, rows[h]],
                send_sem=send_sems.at[index],
                recv_sem=recv_sems.at[index],
                device_id={"inner": dest},
                device_id_type=MESH_ID,
            )
            copy.start()
            started.append(copy)
        return started

    def finish(started, incoming):
        for copy in started:
            copy.wait_send()
        for index, block, h, sender in incoming:
            pltpu.make_async_remote_copy(
                src_ref=out_ref.at[block, rows[h]],
                dst_ref=out_ref.at[block, rows[h]],
                send_sem=send_sems.at[index],
                recv_sem=recv_sems.at[index],
                device_id={"inner": sender},
                device_id_type=MESH_ID,
            ).wait_recv()

    base = counter[0]
    moves, incoming = [], []
    for h in range(2):
        first = steps[h][0]
        for k in (1, -1):
            moves.append((me, h, first(z, y, k), True))
            incoming.append((base + len(incoming), first(z, y, -k), h, first(z, y, -k)))
    finish(run_round(moves), incoming)
    base = counter[0]
    moves, incoming = [], []
    for h in range(2):
        first = steps[h][0]
        moves.append((first(z, y, -1), h, first(z, y, 1), False))
        incoming.append((base + len(incoming), first(z, y, -2), h, first(z, y, -1)))
    finish(run_round(moves), incoming)
    for h in range(2):
        pltpu.make_async_copy(
            tokens_ref.at[rows[h]], out_ref.at[me, rows[h]], local_sems.at[h]
        ).wait()
    base = counter[0]
    moves, incoming = [], []
    for h in range(2):
        first, second = steps[h]
        for k in (1, -1):
            for j in range(side):
                moves.append((first(z, y, j), h, second(z, y, k), False))
                origin = second(z, y, -k)
                oz, oy = origin // side, origin % side
                incoming.append((base + len(incoming), first(oz, oy, j), h, origin))
    finish(run_round(moves), incoming)
    base = counter[0]
    moves, incoming = [], []
    for h in range(2):
        first, second = steps[h]
        src_node = second(z, y, -1)
        sz, sy = src_node // side, src_node % side
        far = second(z, y, -2)
        fz, fy = far // side, far % side
        for j in range(side):
            moves.append((first(sz, sy, j), h, second(z, y, 1), False))
            incoming.append((base + len(incoming), first(fz, fy, j), h, src_node))
    finish(run_round(moves), incoming)


def torus_gather(tokens, side, collective_id):
    count = lax.axis_size("inner")
    copies = 4 + 2 + 4 * side + 2 * side
    return pl.pallas_call(
        functools.partial(torus_gather_kernel, side),
        out_shape=jax.ShapeDtypeStruct((count,) + tokens.shape, tokens.dtype),
        in_specs=[pl.BlockSpec(memory_space=pl.ANY)],
        out_specs=pl.BlockSpec(memory_space=pl.ANY),
        scratch_shapes=[
            pltpu.SemaphoreType.DMA((copies,)),
            pltpu.SemaphoreType.DMA((copies,)),
            pltpu.SemaphoreType.DMA((2,)),
        ],
        compiler_params=pltpu.CompilerParams(
            collective_id=collective_id, has_side_effects=True
        ),
    )(tokens)


def gated_mlp(inputs, gate_matrix, up_matrix, down_matrix):
    gate_part = jnp.dot(inputs, gate_matrix, preferred_element_type=jnp.float32)
    up_part = jnp.dot(inputs, up_matrix, preferred_element_type=jnp.float32)
    hidden = (jax.nn.silu(gate_part) * up_part).astype(jnp.bfloat16)
    return jnp.dot(hidden, down_matrix, preferred_element_type=jnp.float32).astype(jnp.bfloat16)


def gate_weights(gate_score):
    values = gate_score.astype(jnp.float32)
    return 2.5 * values / jnp.sum(values, axis=-1, keepdims=True)


def group_rank(group_ids):
    slot_width = group_ids.shape[-1]
    same_group = group_ids[..., :, None] == group_ids[..., None, :]
    earlier = jnp.arange(slot_width)[None, :] < jnp.arange(slot_width)[:, None]
    return jnp.sum(jnp.logical_and(same_group, earlier), axis=-1)


def combine_pairs(pair_rows, pair_weights):
    values = pair_rows.astype(jnp.float32)
    mixed = (
        pair_weights[..., 0, None] * values[..., 0, :]
        + pair_weights[..., 1, None] * values[..., 1, :]
    )
    return mixed.astype(jnp.bfloat16)


def rank_slots(matches):
    named_mask = jnp.any(matches, axis=-2).astype(jnp.int32)
    earlier = jnp.cumsum(named_mask, axis=-2) - named_mask
    slot_ranks = jnp.sum(jnp.where(matches, earlier[..., None, :], 0), axis=-1)
    return (named_mask, earlier, slot_ranks)


def pair_tables(group_ids, slot_rank, slot_index, weights, group_count):
    wanted = jnp.arange(group_count, dtype=jnp.int32)
    in_group = group_ids[..., None, None, :] == wanted[:, None, None]
    in_place = slot_rank[..., None, None, :] == jnp.arange(2, dtype=jnp.int32)[None, :, None]
    picked = jnp.logical_and(in_group, in_place)
    chosen = jnp.sum(jnp.where(picked, slot_index[..., None, None, :], 0), axis=-1)
    present = jnp.any(picked, axis=-1)
    pair_weights = jnp.sum(jnp.where(picked, weights[..., None, None, :], 0.0), axis=-1)
    return (chosen, present, pair_weights)


def per_device(
    tokens,
    experts,
    gate_score,
    expert_gate,
    expert_up,
    expert_down,
    shared_gate,
    shared_up,
    shared_down,
):
    row_count = tokens.shape[0]
    model_width = tokens.shape[1]
    inner_count = lax.axis_size("inner")
    outer_count = lax.axis_size("outer")
    capacity = TOPK // TOP_GROUPS * row_count // inner_count
    gate_matrix = expert_gate[0]
    up_matrix = expert_up[0]
    down_matrix = expert_down[0]
    side = math.isqrt(inner_count)
    segment = torus_gather(tokens, side, 0).reshape(inner_count * row_count, model_width)
    gate_part = jnp.dot(segment, shared_gate, preferred_element_type=jnp.float32)
    up_part = jnp.dot(segment, shared_up, preferred_element_type=jnp.float32)
    shared_hidden = (jax.nn.silu(gate_part) * up_part).astype(jnp.bfloat16)
    shared_partial = jnp.dot(
        shared_hidden, shared_down, preferred_element_type=jnp.float32
    ).astype(jnp.bfloat16)
    shared_parts = lax.all_to_all(
        shared_partial.reshape(inner_count, row_count, model_width),
        "inner",
        split_axis=0,
        concat_axis=0,
        tiled=True,
    )
    shared = jnp.sum(shared_parts.astype(jnp.float32), axis=0)
    weights = gate_weights(gate_score)
    group_ids = experts // inner_count
    slot_rank = group_rank(group_ids)
    total_count = inner_count * outer_count
    matches = experts[:, :, None] == jnp.arange(total_count, dtype=jnp.int32)[None, None, :]
    named_mask, earlier, slot_ranks = rank_slots(matches)
    slot_ids = jnp.arange(capacity, dtype=jnp.int32)[None, :, None]
    selector = jnp.logical_and(
        named_mask.T[:, None, :] == 1, earlier.T[:, None, :] == slot_ids
    ).astype(jnp.bfloat16)
    outbound = jnp.dot(
        selector.reshape(total_count * capacity, row_count),
        tokens,
        preferred_element_type=jnp.float32,
    ).astype(jnp.bfloat16)
    (received,) = exchange([outbound], [(ALL_AXES, capacity, False)], 1)
    answer = gated_mlp(received, gate_matrix, up_matrix, down_matrix)
    (flat_rows,) = exchange([answer], [(ALL_AXES, capacity, False)], 2)
    slot_index = experts * capacity + slot_ranks
    chosen, present, pair_weights = pair_tables(
        group_ids, slot_rank, slot_index, weights, outer_count
    )
    pair_rows = jnp.where(present[..., None], flat_rows[chosen], jnp.zeros((), jnp.bfloat16))
    partial_value = combine_pairs(pair_rows, pair_weights)
    routed = jnp.sum(partial_value.astype(jnp.float32), axis=1)
    return (shared + routed).astype(jnp.bfloat16)


def solution(mesh):
    return jax.shard_map(
        per_device,
        mesh=mesh,
        in_specs=(
            P(("outer", "inner"), None),
            P(("outer", "inner"), None),
            P(("outer", "inner"), None),
            P(("outer", "inner"), None, None),
            P(("outer", "inner"), None, None),
            P(("outer", "inner"), None, None),
            P(None, "inner"),
            P(None, "inner"),
            P("inner", None),
        ),
        out_specs=P(("outer", "inner"), None),
        check_vma=False,
    )
```

```python
import functools
import math

import jax
import jax.numpy as jnp
from jax import lax
from jax.experimental import pallas as pl
from jax.experimental.pallas import tpu as pltpu
from jax.sharding import PartitionSpec as P

TOPK = 8
TOP_GROUPS = 4
MESH_ID = pl.DeviceIdType.MESH


def torus_gather_kernel(side, tokens_ref, out_ref, send_sems, recv_sems, local_sems):
    me = lax.axis_index("inner")
    z, y = me // side, me % side
    half = tokens_ref.shape[0] // 2

    def node(zz, yy):
        return lax.rem(zz + side, side) * side + lax.rem(yy + side, side)

    steps = [
        (lambda zz, yy, k: node(zz, yy + k), lambda zz, yy, k: node(zz + k, yy)),
        (lambda zz, yy, k: node(zz + k, yy), lambda zz, yy, k: node(zz, yy + k)),
    ]
    neighbours = [node(z, y + 1), node(z, y - 1), node(z + 1, y), node(z - 1, y)]
    barrier = pltpu.get_barrier_semaphore()
    for peer in neighbours:
        pl.semaphore_signal(barrier, inc=1, device_id={"inner": peer}, device_id_type=MESH_ID)
    pl.semaphore_wait(barrier, len(neighbours))

    rows = [pl.ds(0, half), pl.ds(half, half)]
    for h in range(2):
        pltpu.make_async_copy(
            tokens_ref.at[rows[h]], out_ref.at[me, rows[h]], local_sems.at[h]
        ).start()

    counter = [0]

    def run_round(moves):
        started = []
        for block, h, dest, from_tokens in moves:
            index = counter[0]
            counter[0] += 1
            src = tokens_ref.at[rows[h]] if from_tokens else out_ref.at[block, rows[h]]
            copy = pltpu.make_async_remote_copy(
                src_ref=src,
                dst_ref=out_ref.at[block, rows[h]],
                send_sem=send_sems.at[index],
                recv_sem=recv_sems.at[index],
                device_id={"inner": dest},
                device_id_type=MESH_ID,
            )
            copy.start()
            started.append(copy)
        return started

    def finish(started, incoming):
        for copy in started:
            copy.wait_send()
        for index, block, h, sender in incoming:
            pltpu.make_async_remote_copy(
                src_ref=out_ref.at[block, rows[h]],
                dst_ref=out_ref.at[block, rows[h]],
                send_sem=send_sems.at[index],
                recv_sem=recv_sems.at[index],
                device_id={"inner": sender},
                device_id_type=MESH_ID,
            ).wait_recv()

    base = counter[0]
    moves, incoming = [], []
    for h in range(2):
        first = steps[h][0]
        for k in (1, -1):
            moves.append((me, h, first(z, y, k), True))
            incoming.append((base + len(incoming), first(z, y, -k), h, first(z, y, -k)))
    finish(run_round(moves), incoming)
    base = counter[0]
    moves, incoming = [], []
    for h in range(2):
        first = steps[h][0]
        moves.append((first(z, y, -1), h, first(z, y, 1), False))
        incoming.append((base + len(incoming), first(z, y, -2), h, first(z, y, -1)))
    finish(run_round(moves), incoming)
    for h in range(2):
        pltpu.make_async_copy(
            tokens_ref.at[rows[h]], out_ref.at[me, rows[h]], local_sems.at[h]
        ).wait()
    base = counter[0]
    moves, incoming = [], []
    for h in range(2):
        first, second = steps[h]
        for k in (1, -1):
            for j in range(side):
                moves.append((first(z, y, j), h, second(z, y, k), False))
                origin = second(z, y, -k)
                oz, oy = origin // side, origin % side
                incoming.append((base + len(incoming), first(oz, oy, j), h, origin))
    finish(run_round(moves), incoming)
    base = counter[0]
    moves, incoming = [], []
    for h in range(2):
        first, second = steps[h]
        src_node = second(z, y, -1)
        sz, sy = src_node // side, src_node % side
        far = second(z, y, -2)
        fz, fy = far // side, far % side
        for j in range(side):
            moves.append((first(sz, sy, j), h, second(z, y, 1), False))
            incoming.append((base + len(incoming), first(fz, fy, j), h, src_node))
    finish(run_round(moves), incoming)


def torus_gather(tokens, side, collective_id):
    count = lax.axis_size("inner")
    copies = 4 + 2 + 4 * side + 2 * side
    return pl.pallas_call(
        functools.partial(torus_gather_kernel, side),
        out_shape=jax.ShapeDtypeStruct((count,) + tokens.shape, tokens.dtype),
        in_specs=[pl.BlockSpec(memory_space=pl.ANY)],
        out_specs=pl.BlockSpec(memory_space=pl.ANY),
        scratch_shapes=[
            pltpu.SemaphoreType.DMA((copies,)),
            pltpu.SemaphoreType.DMA((copies,)),
            pltpu.SemaphoreType.DMA((2,)),
        ],
        compiler_params=pltpu.CompilerParams(
            collective_id=collective_id, has_side_effects=True
        ),
    )(tokens)


def exchange_kernel(axis, rows, send_ref, recv_ref, send_sems, recv_sems, local_sem):
    count = lax.axis_size(axis)
    me = lax.axis_index(axis)
    barrier = pltpu.get_barrier_semaphore()

    @pl.loop(1, count)
    def _(step):
        peer = lax.rem(me + step, count)
        pl.semaphore_signal(barrier, inc=1, device_id={axis: peer}, device_id_type=MESH_ID)

    pl.semaphore_wait(barrier, count - 1)
    local = pltpu.make_async_copy(
        send_ref.at[pl.ds(me * rows, rows)], recv_ref.at[pl.ds(me * rows, rows)], local_sem
    )
    local.start()

    @pl.loop(1, count)
    def _(step):
        peer = lax.rem(me + step, count)
        pltpu.make_async_remote_copy(
            src_ref=send_ref.at[pl.ds(peer * rows, rows)],
            dst_ref=recv_ref.at[pl.ds(me * rows, rows)],
            send_sem=send_sems.at[peer],
            recv_sem=recv_sems.at[me],
            device_id={axis: peer},
            device_id_type=MESH_ID,
        ).start()

    @pl.loop(1, count)
    def _(step):
        peer = lax.rem(me + step, count)
        pltpu.make_async_remote_copy(
            src_ref=send_ref.at[pl.ds(peer * rows, rows)],
            dst_ref=recv_ref.at[pl.ds(peer * rows, rows)],
            send_sem=send_sems.at[peer],
            recv_sem=recv_sems.at[peer],
            device_id={axis: peer},
            device_id_type=MESH_ID,
        ).wait()

    local.wait()


def exchange(send, axis, collective_id):
    count = lax.axis_size(axis)
    rows = send.shape[0] // count
    return pl.pallas_call(
        functools.partial(exchange_kernel, axis, rows),
        out_shape=jax.ShapeDtypeStruct(send.shape, send.dtype),
        in_specs=[pl.BlockSpec(memory_space=pl.ANY)],
        out_specs=pl.BlockSpec(memory_space=pl.ANY),
        scratch_shapes=[
            pltpu.SemaphoreType.DMA((count,)),
            pltpu.SemaphoreType.DMA((count,)),
            pltpu.SemaphoreType.DMA(()),
        ],
        compiler_params=pltpu.CompilerParams(
            collective_id=collective_id, has_side_effects=True
        ),
    )(send)


def gated_mlp(inputs, gate_matrix, up_matrix, down_matrix):
    gate_part = jnp.dot(inputs, gate_matrix, preferred_element_type=jnp.float32)
    up_part = jnp.dot(inputs, up_matrix, preferred_element_type=jnp.float32)
    hidden = (jax.nn.silu(gate_part) * up_part).astype(jnp.bfloat16)
    return jnp.dot(hidden, down_matrix, preferred_element_type=jnp.float32).astype(jnp.bfloat16)


def gate_weights(gate_score):
    values = gate_score.astype(jnp.float32)
    return 2.5 * values / jnp.sum(values, axis=-1, keepdims=True)


def weighted_rows(weights, rows):
    high = weights.astype(jnp.bfloat16)
    low = (weights - high.astype(jnp.float32)).astype(jnp.bfloat16)
    return jnp.dot(high, rows, preferred_element_type=jnp.float32) + jnp.dot(
        low, rows, preferred_element_type=jnp.float32
    )


def per_device(
    tokens,
    experts,
    gate_score,
    expert_gate,
    expert_up,
    expert_down,
    shared_gate,
    shared_up,
    shared_down,
):
    row_count = tokens.shape[0]
    model_width = tokens.shape[1]
    inner_count = lax.axis_size("inner")
    outer_count = lax.axis_size("outer")
    capacity = TOPK // TOP_GROUPS
    me = lax.axis_index("inner")
    side = math.isqrt(inner_count)
    segment = torus_gather(tokens, side, 0).reshape(inner_count * row_count, model_width)
    all_experts = lax.all_gather(experts, "inner", axis=0, tiled=False)
    all_scores = lax.all_gather(gate_score, "inner", axis=0, tiled=False)
    weights = gate_weights(all_scores)
    local_experts = jnp.arange(outer_count, dtype=jnp.int32) * inner_count + me
    matches = all_experts[..., None] == local_experts
    named = jnp.any(matches, axis=2)
    named_int = named.astype(jnp.int32)
    earlier = jnp.cumsum(named_int, axis=1) - named_int
    slot_ids = jnp.arange(capacity, dtype=jnp.int32)
    placed = jnp.logical_and(named[..., None], earlier[..., None] == slot_ids)
    same_block = jnp.eye(inner_count, dtype=jnp.bool_)
    selector = jnp.logical_and(
        jnp.transpose(placed, (2, 0, 3, 1))[:, :, :, None, :],
        same_block[None, :, None, :, None],
    ).reshape(outer_count * inner_count * capacity, inner_count * row_count)
    outbound = jnp.dot(
        selector.astype(jnp.bfloat16), segment, preferred_element_type=jnp.float32
    ).astype(jnp.bfloat16)
    received = exchange(outbound, "outer", 1)
    answer = gated_mlp(received, expert_gate[0], expert_up[0], expert_down[0])
    returned = exchange(answer, "outer", 2)
    slot_weight = jnp.sum(jnp.where(matches, weights[..., None], 0.0), axis=2)
    placed_weight = jnp.where(placed, slot_weight[..., None], 0.0)
    combine = jnp.where(
        same_block[:, None, None, :, None],
        jnp.transpose(placed_weight, (0, 1, 2, 3))[:, :, :, None, :],
        0.0,
    ).reshape(inner_count * row_count, outer_count * inner_count * capacity)
    routed = weighted_rows(combine, returned)
    gate_part = jnp.dot(segment, shared_gate, preferred_element_type=jnp.float32)
    up_part = jnp.dot(segment, shared_up, preferred_element_type=jnp.float32)
    shared_hidden = (jax.nn.silu(gate_part) * up_part).astype(jnp.bfloat16)
    shared = jnp.dot(shared_hidden, shared_down, preferred_element_type=jnp.float32)
    total = (shared + routed).astype(jnp.bfloat16)
    parts = lax.all_to_all(
        total.reshape(inner_count, row_count, model_width),
        "inner",
        split_axis=0,
        concat_axis=0,
        tiled=True,
    )
    return jnp.sum(parts.astype(jnp.float32), axis=0).astype(jnp.bfloat16)


def solution(mesh):
    return jax.shard_map(
        per_device,
        mesh=mesh,
        in_specs=(
            P(("outer", "inner"), None),
            P(("outer", "inner"), None),
            P(("outer", "inner"), None),
            P(("outer", "inner"), None, None),
            P(("outer", "inner"), None, None),
            P(("outer", "inner"), None, None),
            P(None, "inner"),
            P(None, "inner"),
            P("inner", None),
        ),
        out_specs=P(("outer", "inner"), None),
        check_vma=False,
    )
```

```python
import functools
import math

import jax
import jax.numpy as jnp
from jax import lax
from jax.experimental import pallas as pl
from jax.experimental.pallas import tpu as pltpu
from jax.sharding import PartitionSpec as P

TOPK = 8
TOP_GROUPS = 4
MESH_ID = pl.DeviceIdType.MESH


def torus_gather_kernel(side, count, *refs):
    sources = refs[:count]
    outs = refs[count:2 * count]
    send_sems, recv_sems, local_sems = refs[2 * count:]
    me = lax.axis_index("inner")
    z, y = me // side, me % side
    half = sources[0].shape[0] // 2

    def node(zz, yy):
        return lax.rem(zz + side, side) * side + lax.rem(yy + side, side)

    steps = [
        (lambda zz, yy, k: node(zz, yy + k), lambda zz, yy, k: node(zz + k, yy)),
        (lambda zz, yy, k: node(zz + k, yy), lambda zz, yy, k: node(zz, yy + k)),
    ]
    neighbours = [node(z, y + 1), node(z, y - 1), node(z + 1, y), node(z - 1, y)]
    barrier = pltpu.get_barrier_semaphore()
    for peer in neighbours:
        pl.semaphore_signal(barrier, inc=1, device_id={"inner": peer}, device_id_type=MESH_ID)
    pl.semaphore_wait(barrier, len(neighbours))

    rows = [pl.ds(0, half), pl.ds(half, half)]
    local_copies = []
    for a in range(count):
        for h in range(2):
            copy = pltpu.make_async_copy(
                sources[a].at[rows[h]], outs[a].at[me, rows[h]], local_sems.at[a, h]
            )
            copy.start()
            local_copies.append(copy)

    counter = [0]

    def run_round(moves):
        started = []
        for block, h, dest, from_input in moves:
            index = counter[0]
            counter[0] += 1
            for a in range(count):
                src = sources[a].at[rows[h]] if from_input else outs[a].at[block, rows[h]]
                copy = pltpu.make_async_remote_copy(
                    src_ref=src,
                    dst_ref=outs[a].at[block, rows[h]],
                    send_sem=send_sems.at[a, index],
                    recv_sem=recv_sems.at[a, index],
                    device_id={"inner": dest},
                    device_id_type=MESH_ID,
                )
                copy.start()
                started.append(copy)
        return started

    def finish(started, incoming):
        for copy in started:
            copy.wait_send()
        for index, block, h, sender in incoming:
            for a in range(count):
                pltpu.make_async_remote_copy(
                    src_ref=outs[a].at[block, rows[h]],
                    dst_ref=outs[a].at[block, rows[h]],
                    send_sem=send_sems.at[a, index],
                    recv_sem=recv_sems.at[a, index],
                    device_id={"inner": sender},
                    device_id_type=MESH_ID,
                ).wait_recv()

    base = counter[0]
    moves, incoming = [], []
    for h in range(2):
        first = steps[h][0]
        for k in (1, -1):
            moves.append((me, h, first(z, y, k), True))
            incoming.append((base + len(incoming), first(z, y, -k), h, first(z, y, -k)))
    finish(run_round(moves), incoming)
    base = counter[0]
    moves, incoming = [], []
    for h in range(2):
        first = steps[h][0]
        moves.append((first(z, y, -1), h, first(z, y, 1), False))
        incoming.append((base + len(incoming), first(z, y, -2), h, first(z, y, -1)))
    finish(run_round(moves), incoming)
    for copy in local_copies:
        copy.wait()
    base = counter[0]
    moves, incoming = [], []
    for h in range(2):
        first, second = steps[h]
        for k in (1, -1):
            for j in range(side):
                moves.append((first(z, y, j), h, second(z, y, k), False))
                origin = second(z, y, -k)
                oz, oy = origin // side, origin % side
                incoming.append((base + len(incoming), first(oz, oy, j), h, origin))
    finish(run_round(moves), incoming)
    base = counter[0]
    moves, incoming = [], []
    for h in range(2):
        first, second = steps[h]
        src_node = second(z, y, -1)
        sz, sy = src_node // side, src_node % side
        far = second(z, y, -2)
        fz, fy = far // side, far % side
        for j in range(side):
            moves.append((first(sz, sy, j), h, second(z, y, 1), False))
            incoming.append((base + len(incoming), first(fz, fy, j), h, src_node))
    finish(run_round(moves), incoming)


def torus_gather(arrays, side, collective_id):
    members = lax.axis_size("inner")
    count = len(arrays)
    copies = 4 + 2 + 4 * side + 2 * side
    return pl.pallas_call(
        functools.partial(torus_gather_kernel, side, count),
        out_shape=tuple(
            jax.ShapeDtypeStruct((members,) + x.shape, x.dtype) for x in arrays
        ),
        in_specs=[pl.BlockSpec(memory_space=pl.ANY)] * count,
        out_specs=tuple(pl.BlockSpec(memory_space=pl.ANY) for _ in arrays),
        scratch_shapes=[
            pltpu.SemaphoreType.DMA((count, copies)),
            pltpu.SemaphoreType.DMA((count, copies)),
            pltpu.SemaphoreType.DMA((count, 2)),
        ],
        compiler_params=pltpu.CompilerParams(
            collective_id=collective_id, has_side_effects=True
        ),
    )(*arrays)


def exchange_kernel(axis, rows, send_ref, recv_ref, send_sems, recv_sems, local_sem):
    count = lax.axis_size(axis)
    me = lax.axis_index(axis)
    barrier = pltpu.get_barrier_semaphore()

    @pl.loop(1, count)
    def _(step):
        peer = lax.rem(me + step, count)
        pl.semaphore_signal(barrier, inc=1, device_id={axis: peer}, device_id_type=MESH_ID)

    pl.semaphore_wait(barrier, count - 1)
    local = pltpu.make_async_copy(
        send_ref.at[pl.ds(me * rows, rows)], recv_ref.at[pl.ds(me * rows, rows)], local_sem
    )
    local.start()

    @pl.loop(1, count)
    def _(step):
        peer = lax.rem(me + step, count)
        pltpu.make_async_remote_copy(
            src_ref=send_ref.at[pl.ds(peer * rows, rows)],
            dst_ref=recv_ref.at[pl.ds(me * rows, rows)],
            send_sem=send_sems.at[peer],
            recv_sem=recv_sems.at[me],
            device_id={axis: peer},
            device_id_type=MESH_ID,
        ).start()

    @pl.loop(1, count)
    def _(step):
        peer = lax.rem(me + step, count)
        pltpu.make_async_remote_copy(
            src_ref=send_ref.at[pl.ds(peer * rows, rows)],
            dst_ref=recv_ref.at[pl.ds(peer * rows, rows)],
            send_sem=send_sems.at[peer],
            recv_sem=recv_sems.at[peer],
            device_id={axis: peer},
            device_id_type=MESH_ID,
        ).wait()

    local.wait()


def exchange(send, axis, collective_id):
    count = lax.axis_size(axis)
    rows = send.shape[0] // count
    return pl.pallas_call(
        functools.partial(exchange_kernel, axis, rows),
        out_shape=jax.ShapeDtypeStruct(send.shape, send.dtype),
        in_specs=[pl.BlockSpec(memory_space=pl.ANY)],
        out_specs=pl.BlockSpec(memory_space=pl.ANY),
        scratch_shapes=[
            pltpu.SemaphoreType.DMA((count,)),
            pltpu.SemaphoreType.DMA((count,)),
            pltpu.SemaphoreType.DMA(()),
        ],
        compiler_params=pltpu.CompilerParams(
            collective_id=collective_id, has_side_effects=True
        ),
    )(send)


def gated_mlp(inputs, gate_matrix, up_matrix, down_matrix):
    gate_part = jnp.dot(inputs, gate_matrix, preferred_element_type=jnp.float32)
    up_part = jnp.dot(inputs, up_matrix, preferred_element_type=jnp.float32)
    hidden = (jax.nn.silu(gate_part) * up_part).astype(jnp.bfloat16)
    return jnp.dot(hidden, down_matrix, preferred_element_type=jnp.float32).astype(jnp.bfloat16)


def gate_weights(gate_score):
    values = gate_score.astype(jnp.float32)
    return 2.5 * values / jnp.sum(values, axis=-1, keepdims=True)


def weighted_rows(weights, rows):
    high = weights.astype(jnp.bfloat16)
    low = (weights - high.astype(jnp.float32)).astype(jnp.bfloat16)
    return jnp.dot(high, rows, preferred_element_type=jnp.float32) + jnp.dot(
        low, rows, preferred_element_type=jnp.float32
    )


def per_device(
    tokens,
    experts,
    gate_score,
    expert_gate,
    expert_up,
    expert_down,
    shared_gate,
    shared_up,
    shared_down,
):
    row_count = tokens.shape[0]
    model_width = tokens.shape[1]
    inner_count = lax.axis_size("inner")
    outer_count = lax.axis_size("outer")
    capacity = TOPK // TOP_GROUPS
    me = lax.axis_index("inner")
    side = math.isqrt(inner_count)
    routing = jnp.concatenate([experts, gate_score], axis=1).astype(jnp.bfloat16)
    routing = jnp.pad(routing, ((0, 0), (0, 128 - routing.shape[1])))
    gathered, gathered_routing = torus_gather([tokens, routing], side, 0)
    segment = gathered.reshape(inner_count * row_count, model_width)
    all_experts = gathered_routing[:, :, :TOPK].astype(jnp.int32)
    all_scores = gathered_routing[:, :, TOPK:2 * TOPK].astype(jnp.int32)
    weights = gate_weights(all_scores)
    local_experts = jnp.arange(outer_count, dtype=jnp.int32) * inner_count + me
    matches = all_experts[..., None] == local_experts
    named = jnp.any(matches, axis=2)
    named_int = named.astype(jnp.int32)
    earlier = jnp.cumsum(named_int, axis=1) - named_int
    slot_ids = jnp.arange(capacity, dtype=jnp.int32)
    placed = jnp.logical_and(named[..., None], earlier[..., None] == slot_ids)
    same_block = jnp.eye(inner_count, dtype=jnp.bool_)
    selector = jnp.logical_and(
        jnp.transpose(placed, (2, 0, 3, 1))[:, :, :, None, :],
        same_block[None, :, None, :, None],
    ).reshape(outer_count * inner_count * capacity, inner_count * row_count)
    outbound = jnp.dot(
        selector.astype(jnp.bfloat16), segment, preferred_element_type=jnp.float32
    ).astype(jnp.bfloat16)
    received = exchange(outbound, "outer", 1)
    answer = gated_mlp(received, expert_gate[0], expert_up[0], expert_down[0])
    returned = exchange(answer, "outer", 2)
    slot_weight = jnp.sum(jnp.where(matches, weights[..., None], 0.0), axis=2)
    placed_weight = jnp.where(placed, slot_weight[..., None], 0.0)
    combine = jnp.where(
        same_block[:, None, None, :, None],
        jnp.transpose(placed_weight, (0, 1, 2, 3))[:, :, :, None, :],
        0.0,
    ).reshape(inner_count * row_count, outer_count * inner_count * capacity)
    routed = weighted_rows(combine, returned)
    gate_part = jnp.dot(segment, shared_gate, preferred_element_type=jnp.float32)
    up_part = jnp.dot(segment, shared_up, preferred_element_type=jnp.float32)
    shared_hidden = (jax.nn.silu(gate_part) * up_part).astype(jnp.bfloat16)
    shared = jnp.dot(shared_hidden, shared_down, preferred_element_type=jnp.float32)
    total = (shared + routed).astype(jnp.bfloat16)
    parts = lax.all_to_all(
        total.reshape(inner_count, row_count, model_width),
        "inner",
        split_axis=0,
        concat_axis=0,
        tiled=True,
    )
    return jnp.sum(parts.astype(jnp.float32), axis=0).astype(jnp.bfloat16)


def solution(mesh):
    return jax.shard_map(
        per_device,
        mesh=mesh,
        in_specs=(
            P(("outer", "inner"), None),
            P(("outer", "inner"), None),
            P(("outer", "inner"), None),
            P(("outer", "inner"), None, None),
            P(("outer", "inner"), None, None),
            P(("outer", "inner"), None, None),
            P(None, "inner"),
            P(None, "inner"),
            P("inner", None),
        ),
        out_specs=P(("outer", "inner"), None),
        check_vma=False,
    )
```

```python
import functools
import math

import jax
import jax.numpy as jnp
from jax import lax
from jax.experimental import pallas as pl
from jax.experimental.pallas import tpu as pltpu
from jax.sharding import PartitionSpec as P

TOPK = 8
TOP_GROUPS = 4
MESH_ID = pl.DeviceIdType.MESH


def torus_gather_kernel(side, count, *refs):
    sources = refs[:count]
    outs = refs[count:2 * count]
    send_sems, recv_sems, local_sems = refs[2 * count:]
    me = lax.axis_index("inner")
    z, y = me // side, me % side
    half = sources[0].shape[0] // 2

    def node(zz, yy):
        return lax.rem(zz + side, side) * side + lax.rem(yy + side, side)

    steps = [
        (lambda zz, yy, k: node(zz, yy + k), lambda zz, yy, k: node(zz + k, yy)),
        (lambda zz, yy, k: node(zz + k, yy), lambda zz, yy, k: node(zz, yy + k)),
    ]
    neighbours = [node(z, y + 1), node(z, y - 1), node(z + 1, y), node(z - 1, y)]
    barrier = pltpu.get_barrier_semaphore()
    for peer in neighbours:
        pl.semaphore_signal(barrier, inc=1, device_id={"inner": peer}, device_id_type=MESH_ID)
    pl.semaphore_wait(barrier, len(neighbours))

    rows = [pl.ds(0, half), pl.ds(half, half)]
    local_copies = []
    for a in range(count):
        for h in range(2):
            copy = pltpu.make_async_copy(
                sources[a].at[rows[h]], outs[a].at[me, rows[h]], local_sems.at[a, h]
            )
            copy.start()
            local_copies.append(copy)

    counter = [0]

    def run_round(moves):
        started = []
        for block, h, dest, from_input in moves:
            index = counter[0]
            counter[0] += 1
            for a in range(count):
                src = sources[a].at[rows[h]] if from_input else outs[a].at[block, rows[h]]
                copy = pltpu.make_async_remote_copy(
                    src_ref=src,
                    dst_ref=outs[a].at[block, rows[h]],
                    send_sem=send_sems.at[a, index],
                    recv_sem=recv_sems.at[a, index],
                    device_id={"inner": dest},
                    device_id_type=MESH_ID,
                )
                copy.start()
                started.append(copy)
        return started

    def finish(started, incoming):
        for copy in started:
            copy.wait_send()
        for index, block, h, sender in incoming:
            for a in range(count):
                pltpu.make_async_remote_copy(
                    src_ref=outs[a].at[block, rows[h]],
                    dst_ref=outs[a].at[block, rows[h]],
                    send_sem=send_sems.at[a, index],
                    recv_sem=recv_sems.at[a, index],
                    device_id={"inner": sender},
                    device_id_type=MESH_ID,
                ).wait_recv()

    base = counter[0]
    moves, incoming = [], []
    for h in range(2):
        first = steps[h][0]
        for k in (1, -1):
            moves.append((me, h, first(z, y, k), True))
            incoming.append((base + len(incoming), first(z, y, -k), h, first(z, y, -k)))
    finish(run_round(moves), incoming)
    base = counter[0]
    moves, incoming = [], []
    for h in range(2):
        first = steps[h][0]
        moves.append((first(z, y, -1), h, first(z, y, 1), False))
        incoming.append((base + len(incoming), first(z, y, -2), h, first(z, y, -1)))
    finish(run_round(moves), incoming)
    for copy in local_copies:
        copy.wait()
    base = counter[0]
    moves, incoming = [], []
    for h in range(2):
        first, second = steps[h]
        for k in (1, -1):
            for j in range(side):
                moves.append((first(z, y, j), h, second(z, y, k), False))
                origin = second(z, y, -k)
                oz, oy = origin // side, origin % side
                incoming.append((base + len(incoming), first(oz, oy, j), h, origin))
    finish(run_round(moves), incoming)
    base = counter[0]
    moves, incoming = [], []
    for h in range(2):
        first, second = steps[h]
        src_node = second(z, y, -1)
        sz, sy = src_node // side, src_node % side
        far = second(z, y, -2)
        fz, fy = far // side, far % side
        for j in range(side):
            moves.append((first(sz, sy, j), h, second(z, y, 1), False))
            incoming.append((base + len(incoming), first(fz, fy, j), h, src_node))
    finish(run_round(moves), incoming)


def torus_gather(arrays, side, collective_id):
    members = lax.axis_size("inner")
    count = len(arrays)
    copies = 4 + 2 + 4 * side + 2 * side
    return pl.pallas_call(
        functools.partial(torus_gather_kernel, side, count),
        out_shape=tuple(
            jax.ShapeDtypeStruct((members,) + x.shape, x.dtype) for x in arrays
        ),
        in_specs=[pl.BlockSpec(memory_space=pl.ANY)] * count,
        out_specs=tuple(pl.BlockSpec(memory_space=pl.ANY) for _ in arrays),
        scratch_shapes=[
            pltpu.SemaphoreType.DMA((count, copies)),
            pltpu.SemaphoreType.DMA((count, copies)),
            pltpu.SemaphoreType.DMA((count, 2)),
        ],
        compiler_params=pltpu.CompilerParams(
            collective_id=collective_id, has_side_effects=True
        ),
    )(*arrays)


def torus_reduce_kernel(side, x_ref, out_ref, recv_a, recv_bp, recv_bm, send_b, partial,
                        send_a2, recv_a2, send_b2, send_c2, recv_b2p, recv_b2m,
                        send_sems, recv_sems):
    me = lax.axis_index("inner")
    z, y = me // side, me % side
    half = x_ref.shape[1] // 2
    rows = [pl.ds(0, half), pl.ds(half, half)]

    def node(zz, yy):
        return lax.rem(zz + side, side) * side + lax.rem(yy + side, side)

    def wrap(p):
        return lax.rem(p + side, side)

    plans = [
        (lambda k: node(z + k, y), lambda k: node(z, y + k), z, y,
         lambda pos, j: pos * side + j),
        (lambda k: node(z, y + k), lambda k: node(z + k, y), y, z,
         lambda pos, j: j * side + pos),
    ]
    neighbours = [node(z, y + 1), node(z, y - 1), node(z + 1, y), node(z - 1, y)]
    barrier = pltpu.get_barrier_semaphore()
    for peer in neighbours:
        pl.semaphore_signal(barrier, inc=1, device_id={"inner": peer}, device_id_type=MESH_ID)
    pl.semaphore_wait(barrier, len(neighbours))

    counter = [0]

    def send(src, dst, dest):
        index = counter[0]
        counter[0] += 1
        copy = pltpu.make_async_remote_copy(
            src_ref=src, dst_ref=dst, send_sem=send_sems.at[index],
            recv_sem=recv_sems.at[index], device_id={"inner": dest},
            device_id_type=MESH_ID,
        )
        copy.start()
        return copy, (index, dst, src)

    def settle(sent, senders):
        for copy, _ in sent:
            copy.wait_send()
        for (_, (index, dst, src)), sender in zip(sent, senders):
            pltpu.make_async_remote_copy(
                src_ref=src, dst_ref=dst, send_sem=send_sems.at[index],
                recv_sem=recv_sems.at[index], device_id={"inner": sender},
                device_id_type=MESH_ID,
            ).wait_recv()

    sent, senders = [], []
    for h, (ring1, ring2, p1, p2, block) in enumerate(plans):
        for j in range(side):
            sent.append(send(x_ref.at[block(wrap(p1 + 2), j), rows[h]], recv_a.at[h, j], ring1(1)))
            senders.append(ring1(-1))
    settle(sent, senders)
    sent, senders = [], []
    for h, (ring1, ring2, p1, p2, block) in enumerate(plans):
        for j in range(side):
            mine = x_ref[block(wrap(p1 + 1), j), rows[h], :].astype(jnp.float32)
            send_b[h, j] = (mine + recv_a[h, j].astype(jnp.float32)).astype(send_b.dtype)
        for j in range(side):
            sent.append(send(send_b.at[h, j], recv_bp.at[h, j], ring1(1)))
            senders.append(ring1(-1))
            sent.append(send(x_ref.at[block(wrap(p1 - 1), j), rows[h]], recv_bm.at[h, j], ring1(-1)))
            senders.append(ring1(1))
    settle(sent, senders)
    for h, (ring1, ring2, p1, p2, block) in enumerate(plans):
        for j in range(side):
            partial[h, j] = (
                x_ref[block(p1, j), rows[h], :].astype(jnp.float32)
                + recv_bp[h, j].astype(jnp.float32)
                + recv_bm[h, j].astype(jnp.float32)
            )
    sent, senders = [], []
    for h, (ring1, ring2, p1, p2, block) in enumerate(plans):
        send_a2[h] = partial[h, wrap(p2 + 2)].astype(send_a2.dtype)
        sent.append(send(send_a2.at[h], recv_a2.at[h], ring2(1)))
        senders.append(ring2(-1))
    settle(sent, senders)
    sent, senders = [], []
    for h, (ring1, ring2, p1, p2, block) in enumerate(plans):
        send_b2[h] = (partial[h, wrap(p2 + 1)] + recv_a2[h].astype(jnp.float32)).astype(send_b2.dtype)
        send_c2[h] = partial[h, wrap(p2 - 1)].astype(send_c2.dtype)
        sent.append(send(send_b2.at[h], recv_b2p.at[h], ring2(1)))
        senders.append(ring2(-1))
        sent.append(send(send_c2.at[h], recv_b2m.at[h], ring2(-1)))
        senders.append(ring2(1))
    settle(sent, senders)
    for h, (ring1, ring2, p1, p2, block) in enumerate(plans):
        out_ref[rows[h], :] = (
            partial[h, p2]
            + recv_b2p[h].astype(jnp.float32)
            + recv_b2m[h].astype(jnp.float32)
        ).astype(out_ref.dtype)


def torus_reduce(parts, side, collective_id):
    _, row_count, width = parts.shape
    half = row_count // 2
    piece = (2, side, half, width)
    one = (2, half, width)
    copies = 2 * side + 4 * side + 2 + 4
    vmem = pltpu.VMEM
    return pl.pallas_call(
        functools.partial(torus_reduce_kernel, side),
        out_shape=jax.ShapeDtypeStruct((row_count, width), jnp.bfloat16),
        in_specs=[pl.BlockSpec(memory_space=vmem)],
        out_specs=pl.BlockSpec(memory_space=vmem),
        scratch_shapes=[
            vmem(piece, parts.dtype),
            vmem(piece, parts.dtype),
            vmem(piece, parts.dtype),
            vmem(piece, parts.dtype),
            vmem(piece, jnp.float32),
            vmem(one, parts.dtype),
            vmem(one, parts.dtype),
            vmem(one, parts.dtype),
            vmem(one, parts.dtype),
            vmem(one, parts.dtype),
            vmem(one, parts.dtype),
            pltpu.SemaphoreType.DMA((copies,)),
            pltpu.SemaphoreType.DMA((copies,)),
        ],
        compiler_params=pltpu.CompilerParams(
            collective_id=collective_id, has_side_effects=True
        ),
    )(parts)


def exchange_kernel(axis, rows, send_ref, recv_ref, send_sems, recv_sems, local_sem):
    count = lax.axis_size(axis)
    me = lax.axis_index(axis)
    barrier = pltpu.get_barrier_semaphore()

    @pl.loop(1, count)
    def _(step):
        peer = lax.rem(me + step, count)
        pl.semaphore_signal(barrier, inc=1, device_id={axis: peer}, device_id_type=MESH_ID)

    pl.semaphore_wait(barrier, count - 1)
    local = pltpu.make_async_copy(
        send_ref.at[pl.ds(me * rows, rows)], recv_ref.at[pl.ds(me * rows, rows)], local_sem
    )
    local.start()

    @pl.loop(1, count)
    def _(step):
        peer = lax.rem(me + step, count)
        pltpu.make_async_remote_copy(
            src_ref=send_ref.at[pl.ds(peer * rows, rows)],
            dst_ref=recv_ref.at[pl.ds(me * rows, rows)],
            send_sem=send_sems.at[peer],
            recv_sem=recv_sems.at[me],
            device_id={axis: peer},
            device_id_type=MESH_ID,
        ).start()

    @pl.loop(1, count)
    def _(step):
        peer = lax.rem(me + step, count)
        pltpu.make_async_remote_copy(
            src_ref=send_ref.at[pl.ds(peer * rows, rows)],
            dst_ref=recv_ref.at[pl.ds(peer * rows, rows)],
            send_sem=send_sems.at[peer],
            recv_sem=recv_sems.at[peer],
            device_id={axis: peer},
            device_id_type=MESH_ID,
        ).wait()

    local.wait()


def exchange(send, axis, collective_id):
    count = lax.axis_size(axis)
    rows = send.shape[0] // count
    return pl.pallas_call(
        functools.partial(exchange_kernel, axis, rows),
        out_shape=jax.ShapeDtypeStruct(send.shape, send.dtype),
        in_specs=[pl.BlockSpec(memory_space=pl.ANY)],
        out_specs=pl.BlockSpec(memory_space=pl.ANY),
        scratch_shapes=[
            pltpu.SemaphoreType.DMA((count,)),
            pltpu.SemaphoreType.DMA((count,)),
            pltpu.SemaphoreType.DMA(()),
        ],
        compiler_params=pltpu.CompilerParams(
            collective_id=collective_id, has_side_effects=True
        ),
    )(send)


def gated_mlp(inputs, gate_matrix, up_matrix, down_matrix):
    gate_part = jnp.dot(inputs, gate_matrix, preferred_element_type=jnp.float32)
    up_part = jnp.dot(inputs, up_matrix, preferred_element_type=jnp.float32)
    hidden = (jax.nn.silu(gate_part) * up_part).astype(jnp.bfloat16)
    return jnp.dot(hidden, down_matrix, preferred_element_type=jnp.float32).astype(jnp.bfloat16)


def gate_weights(gate_score):
    values = gate_score.astype(jnp.float32)
    return 2.5 * values / jnp.sum(values, axis=-1, keepdims=True)


def weighted_rows(weights, rows):
    high = weights.astype(jnp.bfloat16)
    low = (weights - high.astype(jnp.float32)).astype(jnp.bfloat16)
    return jnp.dot(high, rows, preferred_element_type=jnp.float32) + jnp.dot(
        low, rows, preferred_element_type=jnp.float32
    )


def per_device(
    tokens,
    experts,
    gate_score,
    expert_gate,
    expert_up,
    expert_down,
    shared_gate,
    shared_up,
    shared_down,
):
    row_count = tokens.shape[0]
    model_width = tokens.shape[1]
    inner_count = lax.axis_size("inner")
    outer_count = lax.axis_size("outer")
    capacity = TOPK // TOP_GROUPS
    me = lax.axis_index("inner")
    side = math.isqrt(inner_count)
    routing = jnp.concatenate([experts, gate_score], axis=1).astype(jnp.bfloat16)
    routing = jnp.pad(routing, ((0, 0), (0, 128 - routing.shape[1])))
    gathered, gathered_routing = torus_gather([tokens, routing], side, 0)
    segment = gathered.reshape(inner_count * row_count, model_width)
    all_experts = gathered_routing[:, :, :TOPK].astype(jnp.int32)
    all_scores = gathered_routing[:, :, TOPK:2 * TOPK].astype(jnp.int32)
    weights = gate_weights(all_scores)
    local_experts = jnp.arange(outer_count, dtype=jnp.int32) * inner_count + me
    matches = all_experts[..., None] == local_experts
    named = jnp.any(matches, axis=2)
    named_int = named.astype(jnp.int32)
    earlier = jnp.cumsum(named_int, axis=1) - named_int
    slot_ids = jnp.arange(capacity, dtype=jnp.int32)
    placed = jnp.logical_and(named[..., None], earlier[..., None] == slot_ids)
    same_block = jnp.eye(inner_count, dtype=jnp.bool_)
    selector = jnp.logical_and(
        jnp.transpose(placed, (2, 0, 3, 1))[:, :, :, None, :],
        same_block[None, :, None, :, None],
    ).reshape(outer_count * inner_count * capacity, inner_count * row_count)
    outbound = jnp.dot(
        selector.astype(jnp.bfloat16), segment, preferred_element_type=jnp.float32
    ).astype(jnp.bfloat16)
    received = exchange(outbound, "outer", 1)
    answer = gated_mlp(received, expert_gate[0], expert_up[0], expert_down[0])
    returned = exchange(answer, "outer", 2)
    slot_weight = jnp.sum(jnp.where(matches, weights[..., None], 0.0), axis=2)
    placed_weight = jnp.where(placed, slot_weight[..., None], 0.0)
    combine = jnp.where(
        same_block[:, None, None, :, None],
        jnp.transpose(placed_weight, (0, 1, 2, 3))[:, :, :, None, :],
        0.0,
    ).reshape(inner_count * row_count, outer_count * inner_count * capacity)
    routed = weighted_rows(combine, returned)
    gate_part = jnp.dot(segment, shared_gate, preferred_element_type=jnp.float32)
    up_part = jnp.dot(segment, shared_up, preferred_element_type=jnp.float32)
    shared_hidden = (jax.nn.silu(gate_part) * up_part).astype(jnp.bfloat16)
    shared = jnp.dot(shared_hidden, shared_down, preferred_element_type=jnp.float32)
    total = (shared + routed).astype(jnp.bfloat16)
    return torus_reduce(total.reshape(inner_count, row_count, model_width), side, 3)


def solution(mesh):
    return jax.shard_map(
        per_device,
        mesh=mesh,
        in_specs=(
            P(("outer", "inner"), None),
            P(("outer", "inner"), None),
            P(("outer", "inner"), None),
            P(("outer", "inner"), None, None),
            P(("outer", "inner"), None, None),
            P(("outer", "inner"), None, None),
            P(None, "inner"),
            P(None, "inner"),
            P("inner", None),
        ),
        out_specs=P(("outer", "inner"), None),
        check_vma=False,
    )
```

```python
import functools
import math

import jax
import jax.numpy as jnp
from jax import lax
from jax.experimental import pallas as pl
from jax.experimental.pallas import tpu as pltpu
from jax.sharding import PartitionSpec as P

TOPK = 8
TOP_GROUPS = 4
MESH_ID = pl.DeviceIdType.MESH


def torus_gather_kernel(side, count, *refs):
    sources = refs[:count]
    outs = refs[count:2 * count]
    send_sems, recv_sems, local_sems = refs[2 * count:]
    me = lax.axis_index("inner")
    z, y = me // side, me % side
    half = sources[0].shape[0] // 2

    def node(zz, yy):
        return lax.rem(zz + side, side) * side + lax.rem(yy + side, side)

    steps = [
        (lambda zz, yy, k: node(zz, yy + k), lambda zz, yy, k: node(zz + k, yy)),
        (lambda zz, yy, k: node(zz + k, yy), lambda zz, yy, k: node(zz, yy + k)),
    ]
    neighbours = [node(z, y + 1), node(z, y - 1), node(z + 1, y), node(z - 1, y)]
    barrier = pltpu.get_barrier_semaphore()
    for peer in neighbours:
        pl.semaphore_signal(barrier, inc=1, device_id={"inner": peer}, device_id_type=MESH_ID)
    pl.semaphore_wait(barrier, len(neighbours))

    rows = [pl.ds(0, half), pl.ds(half, half)]
    local_copies = []
    for a in range(count):
        for h in range(2):
            copy = pltpu.make_async_copy(
                sources[a].at[rows[h]], outs[a].at[me, rows[h]], local_sems.at[a, h]
            )
            copy.start()
            local_copies.append(copy)

    counter = [0]

    def run_round(moves):
        started = []
        for block, h, dest, from_input in moves:
            index = counter[0]
            counter[0] += 1
            for a in range(count):
                src = sources[a].at[rows[h]] if from_input else outs[a].at[block, rows[h]]
                copy = pltpu.make_async_remote_copy(
                    src_ref=src,
                    dst_ref=outs[a].at[block, rows[h]],
                    send_sem=send_sems.at[a, index],
                    recv_sem=recv_sems.at[a, index],
                    device_id={"inner": dest},
                    device_id_type=MESH_ID,
                )
                copy.start()
                started.append(copy)
        return started

    def finish(started, incoming):
        for copy in started:
            copy.wait_send()
        for index, block, h, sender in incoming:
            for a in range(count):
                pltpu.make_async_remote_copy(
                    src_ref=outs[a].at[block, rows[h]],
                    dst_ref=outs[a].at[block, rows[h]],
                    send_sem=send_sems.at[a, index],
                    recv_sem=recv_sems.at[a, index],
                    device_id={"inner": sender},
                    device_id_type=MESH_ID,
                ).wait_recv()

    base = counter[0]
    moves, incoming = [], []
    for h in range(2):
        first = steps[h][0]
        for k in (1, -1):
            moves.append((me, h, first(z, y, k), True))
            incoming.append((base + len(incoming), first(z, y, -k), h, first(z, y, -k)))
    finish(run_round(moves), incoming)
    base = counter[0]
    moves, incoming = [], []
    for h in range(2):
        first = steps[h][0]
        moves.append((first(z, y, -1), h, first(z, y, 1), False))
        incoming.append((base + len(incoming), first(z, y, -2), h, first(z, y, -1)))
    finish(run_round(moves), incoming)
    for copy in local_copies:
        copy.wait()
    base = counter[0]
    moves, incoming = [], []
    for h in range(2):
        first, second = steps[h]
        for k in (1, -1):
            for j in range(side):
                moves.append((first(z, y, j), h, second(z, y, k), False))
                origin = second(z, y, -k)
                oz, oy = origin // side, origin % side
                incoming.append((base + len(incoming), first(oz, oy, j), h, origin))
    finish(run_round(moves), incoming)
    base = counter[0]
    moves, incoming = [], []
    for h in range(2):
        first, second = steps[h]
        src_node = second(z, y, -1)
        sz, sy = src_node // side, src_node % side
        far = second(z, y, -2)
        fz, fy = far // side, far % side
        for j in range(side):
            moves.append((first(sz, sy, j), h, second(z, y, 1), False))
            incoming.append((base + len(incoming), first(fz, fy, j), h, src_node))
    finish(run_round(moves), incoming)


def torus_gather(arrays, side, collective_id):
    members = lax.axis_size("inner")
    count = len(arrays)
    copies = 4 + 2 + 4 * side + 2 * side
    return pl.pallas_call(
        functools.partial(torus_gather_kernel, side, count),
        out_shape=tuple(
            jax.ShapeDtypeStruct((members,) + x.shape, x.dtype) for x in arrays
        ),
        in_specs=[pl.BlockSpec(memory_space=pl.ANY)] * count,
        out_specs=tuple(pl.BlockSpec(memory_space=pl.ANY) for _ in arrays),
        scratch_shapes=[
            pltpu.SemaphoreType.DMA((count, copies)),
            pltpu.SemaphoreType.DMA((count, copies)),
            pltpu.SemaphoreType.DMA((count, 2)),
        ],
        compiler_params=pltpu.CompilerParams(
            collective_id=collective_id, has_side_effects=True
        ),
    )(*arrays)


def torus_reduce_kernel(side, x_ref, out_ref, recv_a, recv_bp, recv_bm, send_b, partial,
                        send_a2, recv_a2, send_b2, send_c2, recv_b2p, recv_b2m,
                        send_sems, recv_sems):
    me = lax.axis_index("inner")
    z, y = me // side, me % side
    half = x_ref.shape[1] // 2
    rows = [pl.ds(0, half), pl.ds(half, half)]

    def node(zz, yy):
        return lax.rem(zz + side, side) * side + lax.rem(yy + side, side)

    def wrap(p):
        return lax.rem(p + side, side)

    plans = [
        (lambda k: node(z + k, y), lambda k: node(z, y + k), z, y,
         lambda pos, j: pos * side + j),
        (lambda k: node(z, y + k), lambda k: node(z + k, y), y, z,
         lambda pos, j: j * side + pos),
    ]
    neighbours = [node(z, y + 1), node(z, y - 1), node(z + 1, y), node(z - 1, y)]
    barrier = pltpu.get_barrier_semaphore()
    for peer in neighbours:
        pl.semaphore_signal(barrier, inc=1, device_id={"inner": peer}, device_id_type=MESH_ID)
    pl.semaphore_wait(barrier, len(neighbours))

    counter = [0]

    def send(src, dst, dest):
        index = counter[0]
        counter[0] += 1
        copy = pltpu.make_async_remote_copy(
            src_ref=src, dst_ref=dst, send_sem=send_sems.at[index],
            recv_sem=recv_sems.at[index], device_id={"inner": dest},
            device_id_type=MESH_ID,
        )
        copy.start()
        return copy, (index, dst, src)

    def settle(sent, senders):
        for copy, _ in sent:
            copy.wait_send()
        for (_, (index, dst, src)), sender in zip(sent, senders):
            pltpu.make_async_remote_copy(
                src_ref=src, dst_ref=dst, send_sem=send_sems.at[index],
                recv_sem=recv_sems.at[index], device_id={"inner": sender},
                device_id_type=MESH_ID,
            ).wait_recv()

    sent, senders = [], []
    for h, (ring1, ring2, p1, p2, block) in enumerate(plans):
        for j in range(side):
            sent.append(send(x_ref.at[block(wrap(p1 + 2), j), rows[h]], recv_a.at[h, j], ring1(1)))
            senders.append(ring1(-1))
    settle(sent, senders)
    sent, senders = [], []
    for h, (ring1, ring2, p1, p2, block) in enumerate(plans):
        for j in range(side):
            mine = x_ref[block(wrap(p1 + 1), j), rows[h], :].astype(jnp.float32)
            send_b[h, j] = (mine + recv_a[h, j].astype(jnp.float32)).astype(send_b.dtype)
        for j in range(side):
            sent.append(send(send_b.at[h, j], recv_bp.at[h, j], ring1(1)))
            senders.append(ring1(-1))
            sent.append(send(x_ref.at[block(wrap(p1 - 1), j), rows[h]], recv_bm.at[h, j], ring1(-1)))
            senders.append(ring1(1))
    settle(sent, senders)
    for h, (ring1, ring2, p1, p2, block) in enumerate(plans):
        for j in range(side):
            partial[h, j] = (
                x_ref[block(p1, j), rows[h], :].astype(jnp.float32)
                + recv_bp[h, j].astype(jnp.float32)
                + recv_bm[h, j].astype(jnp.float32)
            )
    sent, senders = [], []
    for h, (ring1, ring2, p1, p2, block) in enumerate(plans):
        send_a2[h] = partial[h, wrap(p2 + 2)].astype(send_a2.dtype)
        sent.append(send(send_a2.at[h], recv_a2.at[h], ring2(1)))
        senders.append(ring2(-1))
    settle(sent, senders)
    sent, senders = [], []
    for h, (ring1, ring2, p1, p2, block) in enumerate(plans):
        send_b2[h] = (partial[h, wrap(p2 + 1)] + recv_a2[h].astype(jnp.float32)).astype(send_b2.dtype)
        send_c2[h] = partial[h, wrap(p2 - 1)].astype(send_c2.dtype)
        sent.append(send(send_b2.at[h], recv_b2p.at[h], ring2(1)))
        senders.append(ring2(-1))
        sent.append(send(send_c2.at[h], recv_b2m.at[h], ring2(-1)))
        senders.append(ring2(1))
    settle(sent, senders)
    for h, (ring1, ring2, p1, p2, block) in enumerate(plans):
        out_ref[rows[h], :] = (
            partial[h, p2]
            + recv_b2p[h].astype(jnp.float32)
            + recv_b2m[h].astype(jnp.float32)
        ).astype(out_ref.dtype)


def torus_reduce(parts, side, collective_id):
    _, row_count, width = parts.shape
    half = row_count // 2
    piece = (2, side, half, width)
    one = (2, half, width)
    copies = 2 * side + 4 * side + 2 + 4
    vmem = pltpu.VMEM
    return pl.pallas_call(
        functools.partial(torus_reduce_kernel, side),
        out_shape=jax.ShapeDtypeStruct((row_count, width), jnp.bfloat16),
        in_specs=[pl.BlockSpec(memory_space=vmem)],
        out_specs=pl.BlockSpec(memory_space=vmem),
        scratch_shapes=[
            vmem(piece, parts.dtype),
            vmem(piece, parts.dtype),
            vmem(piece, parts.dtype),
            vmem(piece, parts.dtype),
            vmem(piece, jnp.float32),
            vmem(one, parts.dtype),
            vmem(one, parts.dtype),
            vmem(one, parts.dtype),
            vmem(one, parts.dtype),
            vmem(one, parts.dtype),
            vmem(one, parts.dtype),
            pltpu.SemaphoreType.DMA((copies,)),
            pltpu.SemaphoreType.DMA((copies,)),
        ],
        compiler_params=pltpu.CompilerParams(
            collective_id=collective_id, has_side_effects=True
        ),
    )(parts)


def exchange_kernel(axis, rows, send_ref, recv_ref, send_sems, recv_sems, local_sem):
    count = lax.axis_size(axis)
    me = lax.axis_index(axis)
    barrier = pltpu.get_barrier_semaphore()

    @pl.loop(1, count)
    def _(step):
        peer = lax.rem(me + step, count)
        pl.semaphore_signal(barrier, inc=1, device_id={axis: peer}, device_id_type=MESH_ID)

    pl.semaphore_wait(barrier, count - 1)
    local = pltpu.make_async_copy(
        send_ref.at[pl.ds(me * rows, rows)], recv_ref.at[pl.ds(me * rows, rows)], local_sem
    )
    local.start()

    @pl.loop(1, count)
    def _(step):
        peer = lax.rem(me + step, count)
        pltpu.make_async_remote_copy(
            src_ref=send_ref.at[pl.ds(peer * rows, rows)],
            dst_ref=recv_ref.at[pl.ds(me * rows, rows)],
            send_sem=send_sems.at[peer],
            recv_sem=recv_sems.at[me],
            device_id={axis: peer},
            device_id_type=MESH_ID,
        ).start()

    @pl.loop(1, count)
    def _(step):
        peer = lax.rem(me + step, count)
        pltpu.make_async_remote_copy(
            src_ref=send_ref.at[pl.ds(peer * rows, rows)],
            dst_ref=recv_ref.at[pl.ds(peer * rows, rows)],
            send_sem=send_sems.at[peer],
            recv_sem=recv_sems.at[peer],
            device_id={axis: peer},
            device_id_type=MESH_ID,
        ).wait()

    local.wait()


def exchange(send, axis, collective_id):
    count = lax.axis_size(axis)
    rows = send.shape[0] // count
    return pl.pallas_call(
        functools.partial(exchange_kernel, axis, rows),
        out_shape=jax.ShapeDtypeStruct(send.shape, send.dtype),
        in_specs=[pl.BlockSpec(memory_space=pl.ANY)],
        out_specs=pl.BlockSpec(memory_space=pl.ANY),
        scratch_shapes=[
            pltpu.SemaphoreType.DMA((count,)),
            pltpu.SemaphoreType.DMA((count,)),
            pltpu.SemaphoreType.DMA(()),
        ],
        compiler_params=pltpu.CompilerParams(
            collective_id=collective_id, has_side_effects=True
        ),
    )(send)


def dispatch_expert_kernel(axis, rows, tile, send_ref, gate_hbm, up_hbm, down_hbm, out_ref,
                           recv, gate_w, up_w, down_w, hidden, send_sems, recv_sems,
                           local_sems):
    count = lax.axis_size(axis)
    me = lax.axis_index(axis)
    weights = [
        pltpu.make_async_copy(gate_hbm.at[0], gate_w, local_sems.at[0]),
        pltpu.make_async_copy(up_hbm.at[0], up_w, local_sems.at[1]),
        pltpu.make_async_copy(down_hbm.at[0], down_w, local_sems.at[2]),
    ]
    for copy in weights:
        copy.start()
    barrier = pltpu.get_barrier_semaphore()

    @pl.loop(1, count)
    def _(step):
        peer = lax.rem(me + step, count)
        pl.semaphore_signal(barrier, inc=1, device_id={axis: peer}, device_id_type=MESH_ID)

    pl.semaphore_wait(barrier, count - 1)
    local = pltpu.make_async_copy(
        send_ref.at[pl.ds(me * rows, rows)], recv.at[pl.ds(me * rows, rows)], local_sems.at[3]
    )
    local.start()

    @pl.loop(1, count)
    def _(step):
        peer = lax.rem(me + step, count)
        pltpu.make_async_remote_copy(
            src_ref=send_ref.at[pl.ds(peer * rows, rows)],
            dst_ref=recv.at[pl.ds(me * rows, rows)],
            send_sem=send_sems.at[peer],
            recv_sem=recv_sems.at[me],
            device_id={axis: peer},
            device_id_type=MESH_ID,
        ).start()

    @pl.loop(1, count)
    def _(step):
        peer = lax.rem(me + step, count)
        pltpu.make_async_remote_copy(
            src_ref=send_ref.at[pl.ds(peer * rows, rows)],
            dst_ref=recv.at[pl.ds(peer * rows, rows)],
            send_sem=send_sems.at[peer],
            recv_sem=recv_sems.at[peer],
            device_id={axis: peer},
            device_id_type=MESH_ID,
        ).wait()

    local.wait()
    weights[0].wait()
    weights[1].wait()

    @pl.loop(0, gate_w.shape[1] // tile)
    def _(t):
        cols = pl.ds(pl.multiple_of(t * tile, tile), tile)
        tokens = recv[...]
        gate_part = jnp.dot(tokens, gate_w[:, cols], preferred_element_type=jnp.float32)
        up_part = jnp.dot(tokens, up_w[:, cols], preferred_element_type=jnp.float32)
        hidden[:, cols] = (gate_part / (1.0 + jnp.exp(-gate_part)) * up_part).astype(hidden.dtype)

    weights[2].wait()

    @pl.loop(0, down_w.shape[1] // (2 * tile))
    def _(t):
        cols = pl.ds(pl.multiple_of(t * 2 * tile, 2 * tile), 2 * tile)
        out_ref[:, cols] = jnp.dot(
            hidden[...], down_w[:, cols], preferred_element_type=jnp.float32
        ).astype(out_ref.dtype)


def dispatch_expert(send, gate, up, down, axis, collective_id):
    count = lax.axis_size(axis)
    rows = send.shape[0] // count
    width = gate.shape[2]
    any_space = pl.BlockSpec(memory_space=pl.ANY)
    return pl.pallas_call(
        functools.partial(dispatch_expert_kernel, axis, rows, 256),
        out_shape=jax.ShapeDtypeStruct(send.shape, send.dtype),
        in_specs=[any_space] * 4,
        out_specs=pl.BlockSpec(memory_space=pltpu.VMEM),
        scratch_shapes=[
            pltpu.VMEM(send.shape, send.dtype),
            pltpu.VMEM(gate.shape[1:], gate.dtype),
            pltpu.VMEM(up.shape[1:], up.dtype),
            pltpu.VMEM(down.shape[1:], down.dtype),
            pltpu.VMEM((send.shape[0], width), jnp.bfloat16),
            pltpu.SemaphoreType.DMA((count,)),
            pltpu.SemaphoreType.DMA((count,)),
            pltpu.SemaphoreType.DMA((4,)),
        ],
        compiler_params=pltpu.CompilerParams(
            collective_id=collective_id, has_side_effects=True,
            vmem_limit_bytes=56 * 1024 * 1024,
        ),
    )(send, gate, up, down)


def gated_mlp(inputs, gate_matrix, up_matrix, down_matrix):
    gate_part = jnp.dot(inputs, gate_matrix, preferred_element_type=jnp.float32)
    up_part = jnp.dot(inputs, up_matrix, preferred_element_type=jnp.float32)
    hidden = (jax.nn.silu(gate_part) * up_part).astype(jnp.bfloat16)
    return jnp.dot(hidden, down_matrix, preferred_element_type=jnp.float32).astype(jnp.bfloat16)


def gate_weights(gate_score):
    values = gate_score.astype(jnp.float32)
    return 2.5 * values / jnp.sum(values, axis=-1, keepdims=True)


def weighted_rows(weights, rows):
    high = weights.astype(jnp.bfloat16)
    low = (weights - high.astype(jnp.float32)).astype(jnp.bfloat16)
    return jnp.dot(high, rows, preferred_element_type=jnp.float32) + jnp.dot(
        low, rows, preferred_element_type=jnp.float32
    )


def per_device(
    tokens,
    experts,
    gate_score,
    expert_gate,
    expert_up,
    expert_down,
    shared_gate,
    shared_up,
    shared_down,
):
    row_count = tokens.shape[0]
    model_width = tokens.shape[1]
    inner_count = lax.axis_size("inner")
    outer_count = lax.axis_size("outer")
    capacity = TOPK // TOP_GROUPS
    me = lax.axis_index("inner")
    side = math.isqrt(inner_count)
    routing = jnp.concatenate([experts, gate_score], axis=1).astype(jnp.bfloat16)
    routing = jnp.pad(routing, ((0, 0), (0, 128 - routing.shape[1])))
    gathered, gathered_routing = torus_gather([tokens, routing], side, 0)
    segment = gathered.reshape(inner_count * row_count, model_width)
    all_experts = gathered_routing[:, :, :TOPK].astype(jnp.int32)
    all_scores = gathered_routing[:, :, TOPK:2 * TOPK].astype(jnp.int32)
    weights = gate_weights(all_scores)
    local_experts = jnp.arange(outer_count, dtype=jnp.int32) * inner_count + me
    matches = all_experts[..., None] == local_experts
    named = jnp.any(matches, axis=2)
    named_int = named.astype(jnp.int32)
    earlier = jnp.cumsum(named_int, axis=1) - named_int
    slot_ids = jnp.arange(capacity, dtype=jnp.int32)
    placed = jnp.logical_and(named[..., None], earlier[..., None] == slot_ids)
    same_block = jnp.eye(inner_count, dtype=jnp.bool_)
    selector = jnp.logical_and(
        jnp.transpose(placed, (2, 0, 3, 1))[:, :, :, None, :],
        same_block[None, :, None, :, None],
    ).reshape(outer_count * inner_count * capacity, inner_count * row_count)
    outbound = jnp.dot(
        selector.astype(jnp.bfloat16), segment, preferred_element_type=jnp.float32
    ).astype(jnp.bfloat16)
    answer = dispatch_expert(outbound, expert_gate, expert_up, expert_down, "outer", 1)
    returned = exchange(answer, "outer", 2)
    slot_weight = jnp.sum(jnp.where(matches, weights[..., None], 0.0), axis=2)
    placed_weight = jnp.where(placed, slot_weight[..., None], 0.0)
    combine = jnp.where(
        same_block[:, None, None, :, None],
        jnp.transpose(placed_weight, (0, 1, 2, 3))[:, :, :, None, :],
        0.0,
    ).reshape(inner_count * row_count, outer_count * inner_count * capacity)
    routed = weighted_rows(combine, returned)
    gate_part = jnp.dot(segment, shared_gate, preferred_element_type=jnp.float32)
    up_part = jnp.dot(segment, shared_up, preferred_element_type=jnp.float32)
    shared_hidden = (jax.nn.silu(gate_part) * up_part).astype(jnp.bfloat16)
    shared = jnp.dot(shared_hidden, shared_down, preferred_element_type=jnp.float32)
    total = (shared + routed).astype(jnp.bfloat16)
    return torus_reduce(total.reshape(inner_count, row_count, model_width), side, 3)


def solution(mesh):
    return jax.shard_map(
        per_device,
        mesh=mesh,
        in_specs=(
            P(("outer", "inner"), None),
            P(("outer", "inner"), None),
            P(("outer", "inner"), None),
            P(("outer", "inner"), None, None),
            P(("outer", "inner"), None, None),
            P(("outer", "inner"), None, None),
            P(None, "inner"),
            P(None, "inner"),
            P("inner", None),
        ),
        out_specs=P(("outer", "inner"), None),
        check_vma=False,
    )
```

```python
import functools
import math

import jax
import jax.numpy as jnp
from jax import lax
from jax.experimental import pallas as pl
from jax.experimental.pallas import tpu as pltpu
from jax.sharding import PartitionSpec as P

TOPK = 8
TOP_GROUPS = 4
MESH_ID = pl.DeviceIdType.MESH


def torus_gather_kernel(side, count, *refs):
    sources = refs[:count]
    outs = refs[count:2 * count]
    send_sems, recv_sems, local_sems = refs[2 * count:]
    me = lax.axis_index("inner")
    z, y = me // side, me % side
    half = sources[0].shape[0] // 2

    def node(zz, yy):
        return lax.rem(zz + side, side) * side + lax.rem(yy + side, side)

    steps = [
        (lambda zz, yy, k: node(zz, yy + k), lambda zz, yy, k: node(zz + k, yy)),
        (lambda zz, yy, k: node(zz + k, yy), lambda zz, yy, k: node(zz, yy + k)),
    ]
    neighbours = [node(z, y + 1), node(z, y - 1), node(z + 1, y), node(z - 1, y)]
    barrier = pltpu.get_barrier_semaphore()
    for peer in neighbours:
        pl.semaphore_signal(barrier, inc=1, device_id={"inner": peer}, device_id_type=MESH_ID)
    pl.semaphore_wait(barrier, len(neighbours))

    rows = [pl.ds(0, half), pl.ds(half, half)]
    local_copies = []
    for a in range(count):
        for h in range(2):
            copy = pltpu.make_async_copy(
                sources[a].at[rows[h]], outs[a].at[me, rows[h]], local_sems.at[a, h]
            )
            copy.start()
            local_copies.append(copy)

    counter = [0]

    def run_round(moves):
        started = []
        for block, h, dest, from_input in moves:
            index = counter[0]
            counter[0] += 1
            for a in range(count):
                src = sources[a].at[rows[h]] if from_input else outs[a].at[block, rows[h]]
                copy = pltpu.make_async_remote_copy(
                    src_ref=src,
                    dst_ref=outs[a].at[block, rows[h]],
                    send_sem=send_sems.at[a, index],
                    recv_sem=recv_sems.at[a, index],
                    device_id={"inner": dest},
                    device_id_type=MESH_ID,
                )
                copy.start()
                started.append(copy)
        return started

    def finish(started, incoming):
        for copy in started:
            copy.wait_send()
        for index, block, h, sender in incoming:
            for a in range(count):
                pltpu.make_async_remote_copy(
                    src_ref=outs[a].at[block, rows[h]],
                    dst_ref=outs[a].at[block, rows[h]],
                    send_sem=send_sems.at[a, index],
                    recv_sem=recv_sems.at[a, index],
                    device_id={"inner": sender},
                    device_id_type=MESH_ID,
                ).wait_recv()

    base = counter[0]
    moves, incoming = [], []
    for h in range(2):
        first = steps[h][0]
        for k in (1, -1):
            moves.append((me, h, first(z, y, k), True))
            incoming.append((base + len(incoming), first(z, y, -k), h, first(z, y, -k)))
    finish(run_round(moves), incoming)
    base = counter[0]
    moves, incoming = [], []
    for h in range(2):
        first = steps[h][0]
        moves.append((first(z, y, -1), h, first(z, y, 1), False))
        incoming.append((base + len(incoming), first(z, y, -2), h, first(z, y, -1)))
    finish(run_round(moves), incoming)
    for copy in local_copies:
        copy.wait()
    base = counter[0]
    moves, incoming = [], []
    for h in range(2):
        first, second = steps[h]
        for k in (1, -1):
            for j in range(side):
                moves.append((first(z, y, j), h, second(z, y, k), False))
                origin = second(z, y, -k)
                oz, oy = origin // side, origin % side
                incoming.append((base + len(incoming), first(oz, oy, j), h, origin))
    finish(run_round(moves), incoming)
    base = counter[0]
    moves, incoming = [], []
    for h in range(2):
        first, second = steps[h]
        src_node = second(z, y, -1)
        sz, sy = src_node // side, src_node % side
        far = second(z, y, -2)
        fz, fy = far // side, far % side
        for j in range(side):
            moves.append((first(sz, sy, j), h, second(z, y, 1), False))
            incoming.append((base + len(incoming), first(fz, fy, j), h, src_node))
    finish(run_round(moves), incoming)


def torus_gather(arrays, side, collective_id):
    members = lax.axis_size("inner")
    count = len(arrays)
    copies = 4 + 2 + 4 * side + 2 * side
    return pl.pallas_call(
        functools.partial(torus_gather_kernel, side, count),
        out_shape=tuple(
            jax.ShapeDtypeStruct((members,) + x.shape, x.dtype) for x in arrays
        ),
        in_specs=[pl.BlockSpec(memory_space=pl.ANY)] * count,
        out_specs=tuple(pl.BlockSpec(memory_space=pl.ANY) for _ in arrays),
        scratch_shapes=[
            pltpu.SemaphoreType.DMA((count, copies)),
            pltpu.SemaphoreType.DMA((count, copies)),
            pltpu.SemaphoreType.DMA((count, 2)),
        ],
        compiler_params=pltpu.CompilerParams(
            collective_id=collective_id, has_side_effects=True
        ),
    )(*arrays)


def torus_reduce_kernel(side, x_ref, out_ref, recv_a, recv_bp, recv_bm, send_b, partial,
                        send_a2, recv_a2, send_b2, send_c2, recv_b2p, recv_b2m,
                        send_sems, recv_sems):
    me = lax.axis_index("inner")
    z, y = me // side, me % side
    half = x_ref.shape[1] // 2
    rows = [pl.ds(0, half), pl.ds(half, half)]

    def node(zz, yy):
        return lax.rem(zz + side, side) * side + lax.rem(yy + side, side)

    def wrap(p):
        return lax.rem(p + side, side)

    plans = [
        (lambda k: node(z + k, y), lambda k: node(z, y + k), z, y,
         lambda pos, j: pos * side + j),
        (lambda k: node(z, y + k), lambda k: node(z + k, y), y, z,
         lambda pos, j: j * side + pos),
    ]
    neighbours = [node(z, y + 1), node(z, y - 1), node(z + 1, y), node(z - 1, y)]
    barrier = pltpu.get_barrier_semaphore()
    for peer in neighbours:
        pl.semaphore_signal(barrier, inc=1, device_id={"inner": peer}, device_id_type=MESH_ID)
    pl.semaphore_wait(barrier, len(neighbours))

    counter = [0]

    def send(src, dst, dest):
        index = counter[0]
        counter[0] += 1
        copy = pltpu.make_async_remote_copy(
            src_ref=src, dst_ref=dst, send_sem=send_sems.at[index],
            recv_sem=recv_sems.at[index], device_id={"inner": dest},
            device_id_type=MESH_ID,
        )
        copy.start()
        return copy, (index, dst, src)

    def settle(sent, senders):
        for copy, _ in sent:
            copy.wait_send()
        for (_, (index, dst, src)), sender in zip(sent, senders):
            pltpu.make_async_remote_copy(
                src_ref=src, dst_ref=dst, send_sem=send_sems.at[index],
                recv_sem=recv_sems.at[index], device_id={"inner": sender},
                device_id_type=MESH_ID,
            ).wait_recv()

    sent, senders = [], []
    for h, (ring1, ring2, p1, p2, block) in enumerate(plans):
        for j in range(side):
            sent.append(send(x_ref.at[block(wrap(p1 + 2), j), rows[h]], recv_a.at[h, j], ring1(1)))
            senders.append(ring1(-1))
    settle(sent, senders)
    sent, senders = [], []
    for h, (ring1, ring2, p1, p2, block) in enumerate(plans):
        for j in range(side):
            mine = x_ref[block(wrap(p1 + 1), j), rows[h], :].astype(jnp.float32)
            send_b[h, j] = (mine + recv_a[h, j].astype(jnp.float32)).astype(send_b.dtype)
        for j in range(side):
            sent.append(send(send_b.at[h, j], recv_bp.at[h, j], ring1(1)))
            senders.append(ring1(-1))
            sent.append(send(x_ref.at[block(wrap(p1 - 1), j), rows[h]], recv_bm.at[h, j], ring1(-1)))
            senders.append(ring1(1))
    settle(sent, senders)
    for h, (ring1, ring2, p1, p2, block) in enumerate(plans):
        for j in range(side):
            partial[h, j] = (
                x_ref[block(p1, j), rows[h], :].astype(jnp.float32)
                + recv_bp[h, j].astype(jnp.float32)
                + recv_bm[h, j].astype(jnp.float32)
            )
    sent, senders = [], []
    for h, (ring1, ring2, p1, p2, block) in enumerate(plans):
        send_a2[h] = partial[h, wrap(p2 + 2)].astype(send_a2.dtype)
        sent.append(send(send_a2.at[h], recv_a2.at[h], ring2(1)))
        senders.append(ring2(-1))
    settle(sent, senders)
    sent, senders = [], []
    for h, (ring1, ring2, p1, p2, block) in enumerate(plans):
        send_b2[h] = (partial[h, wrap(p2 + 1)] + recv_a2[h].astype(jnp.float32)).astype(send_b2.dtype)
        send_c2[h] = partial[h, wrap(p2 - 1)].astype(send_c2.dtype)
        sent.append(send(send_b2.at[h], recv_b2p.at[h], ring2(1)))
        senders.append(ring2(-1))
        sent.append(send(send_c2.at[h], recv_b2m.at[h], ring2(-1)))
        senders.append(ring2(1))
    settle(sent, senders)
    for h, (ring1, ring2, p1, p2, block) in enumerate(plans):
        out_ref[rows[h], :] = (
            partial[h, p2]
            + recv_b2p[h].astype(jnp.float32)
            + recv_b2m[h].astype(jnp.float32)
        ).astype(out_ref.dtype)


def torus_reduce(parts, side, collective_id):
    _, row_count, width = parts.shape
    half = row_count // 2
    piece = (2, side, half, width)
    one = (2, half, width)
    copies = 2 * side + 4 * side + 2 + 4
    vmem = pltpu.VMEM
    return pl.pallas_call(
        functools.partial(torus_reduce_kernel, side),
        out_shape=jax.ShapeDtypeStruct((row_count, width), jnp.bfloat16),
        in_specs=[pl.BlockSpec(memory_space=vmem)],
        out_specs=pl.BlockSpec(memory_space=vmem),
        scratch_shapes=[
            vmem(piece, parts.dtype),
            vmem(piece, parts.dtype),
            vmem(piece, parts.dtype),
            vmem(piece, parts.dtype),
            vmem(piece, jnp.float32),
            vmem(one, parts.dtype),
            vmem(one, parts.dtype),
            vmem(one, parts.dtype),
            vmem(one, parts.dtype),
            vmem(one, parts.dtype),
            vmem(one, parts.dtype),
            pltpu.SemaphoreType.DMA((copies,)),
            pltpu.SemaphoreType.DMA((copies,)),
        ],
        compiler_params=pltpu.CompilerParams(
            collective_id=collective_id, has_side_effects=True
        ),
    )(parts)


def exchange_kernel(axis, rows, send_ref, recv_ref, send_sems, recv_sems, local_sem):
    count = lax.axis_size(axis)
    me = lax.axis_index(axis)
    barrier = pltpu.get_barrier_semaphore()

    @pl.loop(1, count)
    def _(step):
        peer = lax.rem(me + step, count)
        pl.semaphore_signal(barrier, inc=1, device_id={axis: peer}, device_id_type=MESH_ID)

    pl.semaphore_wait(barrier, count - 1)
    local = pltpu.make_async_copy(
        send_ref.at[pl.ds(me * rows, rows)], recv_ref.at[pl.ds(me * rows, rows)], local_sem
    )
    local.start()

    @pl.loop(1, count)
    def _(step):
        peer = lax.rem(me + step, count)
        pltpu.make_async_remote_copy(
            src_ref=send_ref.at[pl.ds(peer * rows, rows)],
            dst_ref=recv_ref.at[pl.ds(me * rows, rows)],
            send_sem=send_sems.at[peer],
            recv_sem=recv_sems.at[me],
            device_id={axis: peer},
            device_id_type=MESH_ID,
        ).start()

    @pl.loop(1, count)
    def _(step):
        peer = lax.rem(me + step, count)
        pltpu.make_async_remote_copy(
            src_ref=send_ref.at[pl.ds(peer * rows, rows)],
            dst_ref=recv_ref.at[pl.ds(peer * rows, rows)],
            send_sem=send_sems.at[peer],
            recv_sem=recv_sems.at[peer],
            device_id={axis: peer},
            device_id_type=MESH_ID,
        ).wait()

    local.wait()


def exchange(send, axis, collective_id):
    count = lax.axis_size(axis)
    rows = send.shape[0] // count
    return pl.pallas_call(
        functools.partial(exchange_kernel, axis, rows),
        out_shape=jax.ShapeDtypeStruct(send.shape, send.dtype),
        in_specs=[pl.BlockSpec(memory_space=pl.ANY)],
        out_specs=pl.BlockSpec(memory_space=pl.ANY),
        scratch_shapes=[
            pltpu.SemaphoreType.DMA((count,)),
            pltpu.SemaphoreType.DMA((count,)),
            pltpu.SemaphoreType.DMA(()),
        ],
        compiler_params=pltpu.CompilerParams(
            collective_id=collective_id, has_side_effects=True
        ),
    )(send)


def dispatch_expert_kernel(axis, rows, tile, send_ref, gate_hbm, up_hbm, down_hbm,
                           segment_hbm, sgate_hbm, sup_hbm, sdown_hbm, out_ref, shared_ref,
                           recv, gate_w, up_w, down_w, hidden, segment, sgate, sup, sdown,
                           send_sems, recv_sems, local_sems):
    count = lax.axis_size(axis)
    me = lax.axis_index(axis)
    weights = [
        pltpu.make_async_copy(gate_hbm.at[0], gate_w, local_sems.at[0]),
        pltpu.make_async_copy(up_hbm.at[0], up_w, local_sems.at[1]),
        pltpu.make_async_copy(down_hbm.at[0], down_w, local_sems.at[2]),
    ]
    shared_inputs = [
        pltpu.make_async_copy(segment_hbm, segment, local_sems.at[4]),
        pltpu.make_async_copy(sgate_hbm, sgate, local_sems.at[5]),
        pltpu.make_async_copy(sup_hbm, sup, local_sems.at[6]),
        pltpu.make_async_copy(sdown_hbm, sdown, local_sems.at[7]),
    ]
    for copy in shared_inputs + weights:
        copy.start()
    barrier = pltpu.get_barrier_semaphore()

    @pl.loop(1, count)
    def _(step):
        peer = lax.rem(me + step, count)
        pl.semaphore_signal(barrier, inc=1, device_id={axis: peer}, device_id_type=MESH_ID)

    pl.semaphore_wait(barrier, count - 1)
    local = pltpu.make_async_copy(
        send_ref.at[pl.ds(me * rows, rows)], recv.at[pl.ds(me * rows, rows)], local_sems.at[3]
    )
    local.start()

    @pl.loop(1, count)
    def _(step):
        peer = lax.rem(me + step, count)
        pltpu.make_async_remote_copy(
            src_ref=send_ref.at[pl.ds(peer * rows, rows)],
            dst_ref=recv.at[pl.ds(me * rows, rows)],
            send_sem=send_sems.at[peer],
            recv_sem=recv_sems.at[me],
            device_id={axis: peer},
            device_id_type=MESH_ID,
        ).start()

    for copy in shared_inputs:
        copy.wait()
    tokens = segment[...]
    gate_part = jnp.dot(tokens, sgate[...], preferred_element_type=jnp.float32)
    up_part = jnp.dot(tokens, sup[...], preferred_element_type=jnp.float32)
    shared_hidden = (gate_part / (1.0 + jnp.exp(-gate_part)) * up_part).astype(sdown.dtype)

    @pl.loop(0, sdown.shape[1] // (2 * tile))
    def _(t):
        cols = pl.ds(pl.multiple_of(t * 2 * tile, 2 * tile), 2 * tile)
        shared_ref[:, cols] = jnp.dot(
            shared_hidden, sdown[:, cols], preferred_element_type=jnp.float32
        )

    @pl.loop(1, count)
    def _(step):
        peer = lax.rem(me + step, count)
        pltpu.make_async_remote_copy(
            src_ref=send_ref.at[pl.ds(peer * rows, rows)],
            dst_ref=recv.at[pl.ds(peer * rows, rows)],
            send_sem=send_sems.at[peer],
            recv_sem=recv_sems.at[peer],
            device_id={axis: peer},
            device_id_type=MESH_ID,
        ).wait()

    local.wait()
    weights[0].wait()
    weights[1].wait()

    @pl.loop(0, gate_w.shape[1] // tile)
    def _(t):
        cols = pl.ds(pl.multiple_of(t * tile, tile), tile)
        tokens = recv[...]
        gate_part = jnp.dot(tokens, gate_w[:, cols], preferred_element_type=jnp.float32)
        up_part = jnp.dot(tokens, up_w[:, cols], preferred_element_type=jnp.float32)
        hidden[:, cols] = (gate_part / (1.0 + jnp.exp(-gate_part)) * up_part).astype(hidden.dtype)

    weights[2].wait()

    @pl.loop(0, down_w.shape[1] // (2 * tile))
    def _(t):
        cols = pl.ds(pl.multiple_of(t * 2 * tile, 2 * tile), 2 * tile)
        out_ref[:, cols] = jnp.dot(
            hidden[...], down_w[:, cols], preferred_element_type=jnp.float32
        ).astype(out_ref.dtype)


def dispatch_expert(send, gate, up, down, segment, sgate, sup, sdown, axis, collective_id):
    count = lax.axis_size(axis)
    rows = send.shape[0] // count
    width = gate.shape[2]
    any_space = pl.BlockSpec(memory_space=pl.ANY)
    vmem_space = pl.BlockSpec(memory_space=pltpu.VMEM)
    return pl.pallas_call(
        functools.partial(dispatch_expert_kernel, axis, rows, 256),
        out_shape=(
            jax.ShapeDtypeStruct(send.shape, send.dtype),
            jax.ShapeDtypeStruct((segment.shape[0], sdown.shape[1]), jnp.float32),
        ),
        in_specs=[any_space] * 8,
        out_specs=(vmem_space, vmem_space),
        scratch_shapes=[
            pltpu.VMEM(send.shape, send.dtype),
            pltpu.VMEM(gate.shape[1:], gate.dtype),
            pltpu.VMEM(up.shape[1:], up.dtype),
            pltpu.VMEM(down.shape[1:], down.dtype),
            pltpu.VMEM((send.shape[0], width), jnp.bfloat16),
            pltpu.VMEM(segment.shape, segment.dtype),
            pltpu.VMEM(sgate.shape, sgate.dtype),
            pltpu.VMEM(sup.shape, sup.dtype),
            pltpu.VMEM(sdown.shape, sdown.dtype),
            pltpu.SemaphoreType.DMA((count,)),
            pltpu.SemaphoreType.DMA((count,)),
            pltpu.SemaphoreType.DMA((8,)),
        ],
        compiler_params=pltpu.CompilerParams(
            collective_id=collective_id, has_side_effects=True,
            vmem_limit_bytes=56 * 1024 * 1024,
        ),
    )(send, gate, up, down, segment, sgate, sup, sdown)


def gated_mlp(inputs, gate_matrix, up_matrix, down_matrix):
    gate_part = jnp.dot(inputs, gate_matrix, preferred_element_type=jnp.float32)
    up_part = jnp.dot(inputs, up_matrix, preferred_element_type=jnp.float32)
    hidden = (jax.nn.silu(gate_part) * up_part).astype(jnp.bfloat16)
    return jnp.dot(hidden, down_matrix, preferred_element_type=jnp.float32).astype(jnp.bfloat16)


def gate_weights(gate_score):
    values = gate_score.astype(jnp.float32)
    return 2.5 * values / jnp.sum(values, axis=-1, keepdims=True)


def weighted_rows(weights, rows):
    high = weights.astype(jnp.bfloat16)
    low = (weights - high.astype(jnp.float32)).astype(jnp.bfloat16)
    return jnp.dot(high, rows, preferred_element_type=jnp.float32) + jnp.dot(
        low, rows, preferred_element_type=jnp.float32
    )


def per_device(
    tokens,
    experts,
    gate_score,
    expert_gate,
    expert_up,
    expert_down,
    shared_gate,
    shared_up,
    shared_down,
):
    row_count = tokens.shape[0]
    model_width = tokens.shape[1]
    inner_count = lax.axis_size("inner")
    outer_count = lax.axis_size("outer")
    capacity = TOPK // TOP_GROUPS
    me = lax.axis_index("inner")
    side = math.isqrt(inner_count)
    routing = jnp.concatenate([experts, gate_score], axis=1).astype(jnp.bfloat16)
    routing = jnp.pad(routing, ((0, 0), (0, 128 - routing.shape[1])))
    gathered, gathered_routing = torus_gather([tokens, routing], side, 0)
    segment = gathered.reshape(inner_count * row_count, model_width)
    all_experts = gathered_routing[:, :, :TOPK].astype(jnp.int32)
    all_scores = gathered_routing[:, :, TOPK:2 * TOPK].astype(jnp.int32)
    weights = gate_weights(all_scores)
    local_experts = jnp.arange(outer_count, dtype=jnp.int32) * inner_count + me
    matches = all_experts[..., None] == local_experts
    named = jnp.any(matches, axis=2)
    named_int = named.astype(jnp.int32)
    earlier = jnp.cumsum(named_int, axis=1) - named_int
    slot_ids = jnp.arange(capacity, dtype=jnp.int32)
    placed = jnp.logical_and(named[..., None], earlier[..., None] == slot_ids)
    same_block = jnp.eye(inner_count, dtype=jnp.bool_)
    selector = jnp.logical_and(
        jnp.transpose(placed, (2, 0, 3, 1))[:, :, :, None, :],
        same_block[None, :, None, :, None],
    ).reshape(outer_count * inner_count * capacity, inner_count * row_count)
    outbound = jnp.dot(
        selector.astype(jnp.bfloat16), segment, preferred_element_type=jnp.float32
    ).astype(jnp.bfloat16)
    answer, shared = dispatch_expert(
        outbound, expert_gate, expert_up, expert_down,
        segment, shared_gate, shared_up, shared_down, "outer", 1,
    )
    returned = exchange(answer, "outer", 2)
    slot_weight = jnp.sum(jnp.where(matches, weights[..., None], 0.0), axis=2)
    placed_weight = jnp.where(placed, slot_weight[..., None], 0.0)
    combine = jnp.where(
        same_block[:, None, None, :, None],
        jnp.transpose(placed_weight, (0, 1, 2, 3))[:, :, :, None, :],
        0.0,
    ).reshape(inner_count * row_count, outer_count * inner_count * capacity)
    routed = weighted_rows(combine, returned)
    total = (shared + routed).astype(jnp.bfloat16)
    return torus_reduce(total.reshape(inner_count, row_count, model_width), side, 3)


def solution(mesh):
    return jax.shard_map(
        per_device,
        mesh=mesh,
        in_specs=(
            P(("outer", "inner"), None),
            P(("outer", "inner"), None),
            P(("outer", "inner"), None),
            P(("outer", "inner"), None, None),
            P(("outer", "inner"), None, None),
            P(("outer", "inner"), None, None),
            P(None, "inner"),
            P(None, "inner"),
            P("inner", None),
        ),
        out_specs=P(("outer", "inner"), None),
        check_vma=False,
    )
```

```python
import functools
import math

import jax
import jax.numpy as jnp
from jax import lax
from jax.experimental import pallas as pl
from jax.experimental.pallas import tpu as pltpu
from jax.sharding import PartitionSpec as P

TOPK = 8
TOP_GROUPS = 4
MESH_ID = pl.DeviceIdType.MESH


def torus_gather_kernel(side, count, *refs):
    sources = refs[:count]
    outs = refs[count:2 * count]
    send_sems, recv_sems, local_sems = refs[2 * count:]
    me = lax.axis_index("inner")
    z, y = me // side, me % side
    half = sources[0].shape[0] // 2

    def node(zz, yy):
        return lax.rem(zz + side, side) * side + lax.rem(yy + side, side)

    steps = [
        (lambda zz, yy, k: node(zz, yy + k), lambda zz, yy, k: node(zz + k, yy)),
        (lambda zz, yy, k: node(zz + k, yy), lambda zz, yy, k: node(zz, yy + k)),
    ]
    neighbours = [node(z, y + 1), node(z, y - 1), node(z + 1, y), node(z - 1, y)]
    barrier = pltpu.get_barrier_semaphore()
    for peer in neighbours:
        pl.semaphore_signal(barrier, inc=1, device_id={"inner": peer}, device_id_type=MESH_ID)
    pl.semaphore_wait(barrier, len(neighbours))

    rows = [pl.ds(0, half), pl.ds(half, half)]
    local_copies = []
    for a in range(count):
        for h in range(2):
            copy = pltpu.make_async_copy(
                sources[a].at[rows[h]], outs[a].at[me, rows[h]], local_sems.at[a, h]
            )
            copy.start()
            local_copies.append(copy)

    counter = [0]

    def run_round(moves):
        started = []
        for block, h, dest, from_input in moves:
            index = counter[0]
            counter[0] += 1
            for a in range(count):
                src = sources[a].at[rows[h]] if from_input else outs[a].at[block, rows[h]]
                copy = pltpu.make_async_remote_copy(
                    src_ref=src,
                    dst_ref=outs[a].at[block, rows[h]],
                    send_sem=send_sems.at[a, index],
                    recv_sem=recv_sems.at[a, index],
                    device_id={"inner": dest},
                    device_id_type=MESH_ID,
                )
                copy.start()
                started.append(copy)
        return started

    def finish(started, incoming):
        for copy in started:
            copy.wait_send()
        for index, block, h, sender in incoming:
            for a in range(count):
                pltpu.make_async_remote_copy(
                    src_ref=outs[a].at[block, rows[h]],
                    dst_ref=outs[a].at[block, rows[h]],
                    send_sem=send_sems.at[a, index],
                    recv_sem=recv_sems.at[a, index],
                    device_id={"inner": sender},
                    device_id_type=MESH_ID,
                ).wait_recv()

    base = counter[0]
    moves, incoming = [], []
    for h in range(2):
        first = steps[h][0]
        for k in (1, -1):
            moves.append((me, h, first(z, y, k), True))
            incoming.append((base + len(incoming), first(z, y, -k), h, first(z, y, -k)))
    finish(run_round(moves), incoming)
    base = counter[0]
    moves, incoming = [], []
    for h in range(2):
        first = steps[h][0]
        moves.append((first(z, y, -1), h, first(z, y, 1), False))
        incoming.append((base + len(incoming), first(z, y, -2), h, first(z, y, -1)))
    finish(run_round(moves), incoming)
    for copy in local_copies:
        copy.wait()
    base = counter[0]
    moves, incoming = [], []
    for h in range(2):
        first, second = steps[h]
        for k in (1, -1):
            for j in range(side):
                moves.append((first(z, y, j), h, second(z, y, k), False))
                origin = second(z, y, -k)
                oz, oy = origin // side, origin % side
                incoming.append((base + len(incoming), first(oz, oy, j), h, origin))
    finish(run_round(moves), incoming)
    base = counter[0]
    moves, incoming = [], []
    for h in range(2):
        first, second = steps[h]
        src_node = second(z, y, -1)
        sz, sy = src_node // side, src_node % side
        far = second(z, y, -2)
        fz, fy = far // side, far % side
        for j in range(side):
            moves.append((first(sz, sy, j), h, second(z, y, 1), False))
            incoming.append((base + len(incoming), first(fz, fy, j), h, src_node))
    finish(run_round(moves), incoming)


def torus_gather(arrays, side, collective_id):
    members = lax.axis_size("inner")
    count = len(arrays)
    copies = 4 + 2 + 4 * side + 2 * side
    return pl.pallas_call(
        functools.partial(torus_gather_kernel, side, count),
        out_shape=tuple(
            jax.ShapeDtypeStruct((members,) + x.shape, x.dtype) for x in arrays
        ),
        in_specs=[pl.BlockSpec(memory_space=pl.ANY)] * count,
        out_specs=tuple(pl.BlockSpec(memory_space=pl.ANY) for _ in arrays),
        scratch_shapes=[
            pltpu.SemaphoreType.DMA((count, copies)),
            pltpu.SemaphoreType.DMA((count, copies)),
            pltpu.SemaphoreType.DMA((count, 2)),
        ],
        compiler_params=pltpu.CompilerParams(
            collective_id=collective_id, has_side_effects=True
        ),
    )(*arrays)


def torus_reduce_kernel(side, x_ref, out_ref, recv_a, recv_bp, recv_bm, send_b, partial,
                        send_a2, recv_a2, send_b2, send_c2, recv_b2p, recv_b2m,
                        send_sems, recv_sems):
    me = lax.axis_index("inner")
    z, y = me // side, me % side
    half = x_ref.shape[1] // 2
    rows = [pl.ds(0, half), pl.ds(half, half)]

    def node(zz, yy):
        return lax.rem(zz + side, side) * side + lax.rem(yy + side, side)

    def wrap(p):
        return lax.rem(p + side, side)

    plans = [
        (lambda k: node(z + k, y), lambda k: node(z, y + k), z, y,
         lambda pos, j: pos * side + j),
        (lambda k: node(z, y + k), lambda k: node(z + k, y), y, z,
         lambda pos, j: j * side + pos),
    ]
    neighbours = [node(z, y + 1), node(z, y - 1), node(z + 1, y), node(z - 1, y)]
    barrier = pltpu.get_barrier_semaphore()
    for peer in neighbours:
        pl.semaphore_signal(barrier, inc=1, device_id={"inner": peer}, device_id_type=MESH_ID)
    pl.semaphore_wait(barrier, len(neighbours))

    counter = [0]

    def send(src, dst, dest):
        index = counter[0]
        counter[0] += 1
        copy = pltpu.make_async_remote_copy(
            src_ref=src, dst_ref=dst, send_sem=send_sems.at[index],
            recv_sem=recv_sems.at[index], device_id={"inner": dest},
            device_id_type=MESH_ID,
        )
        copy.start()
        return copy, (index, dst, src)

    def settle(sent, senders):
        for copy, _ in sent:
            copy.wait_send()
        for (_, (index, dst, src)), sender in zip(sent, senders):
            pltpu.make_async_remote_copy(
                src_ref=src, dst_ref=dst, send_sem=send_sems.at[index],
                recv_sem=recv_sems.at[index], device_id={"inner": sender},
                device_id_type=MESH_ID,
            ).wait_recv()

    sent, senders = [], []
    for h, (ring1, ring2, p1, p2, block) in enumerate(plans):
        for j in range(side):
            sent.append(send(x_ref.at[block(wrap(p1 + 2), j), rows[h]], recv_a.at[h, j], ring1(1)))
            senders.append(ring1(-1))
    settle(sent, senders)
    sent, senders = [], []
    for h, (ring1, ring2, p1, p2, block) in enumerate(plans):
        for j in range(side):
            mine = x_ref[block(wrap(p1 + 1), j), rows[h], :].astype(jnp.float32)
            send_b[h, j] = (mine + recv_a[h, j].astype(jnp.float32)).astype(send_b.dtype)
        for j in range(side):
            sent.append(send(send_b.at[h, j], recv_bp.at[h, j], ring1(1)))
            senders.append(ring1(-1))
            sent.append(send(x_ref.at[block(wrap(p1 - 1), j), rows[h]], recv_bm.at[h, j], ring1(-1)))
            senders.append(ring1(1))
    settle(sent, senders)
    for h, (ring1, ring2, p1, p2, block) in enumerate(plans):
        for j in range(side):
            partial[h, j] = (
                x_ref[block(p1, j), rows[h], :].astype(jnp.float32)
                + recv_bp[h, j].astype(jnp.float32)
                + recv_bm[h, j].astype(jnp.float32)
            )
    sent, senders = [], []
    for h, (ring1, ring2, p1, p2, block) in enumerate(plans):
        send_a2[h] = partial[h, wrap(p2 + 2)].astype(send_a2.dtype)
        sent.append(send(send_a2.at[h], recv_a2.at[h], ring2(1)))
        senders.append(ring2(-1))
    settle(sent, senders)
    sent, senders = [], []
    for h, (ring1, ring2, p1, p2, block) in enumerate(plans):
        send_b2[h] = (partial[h, wrap(p2 + 1)] + recv_a2[h].astype(jnp.float32)).astype(send_b2.dtype)
        send_c2[h] = partial[h, wrap(p2 - 1)].astype(send_c2.dtype)
        sent.append(send(send_b2.at[h], recv_b2p.at[h], ring2(1)))
        senders.append(ring2(-1))
        sent.append(send(send_c2.at[h], recv_b2m.at[h], ring2(-1)))
        senders.append(ring2(1))
    settle(sent, senders)
    for h, (ring1, ring2, p1, p2, block) in enumerate(plans):
        out_ref[rows[h], :] = (
            partial[h, p2]
            + recv_b2p[h].astype(jnp.float32)
            + recv_b2m[h].astype(jnp.float32)
        ).astype(out_ref.dtype)


def torus_reduce(parts, side, collective_id):
    _, row_count, width = parts.shape
    half = row_count // 2
    piece = (2, side, half, width)
    one = (2, half, width)
    copies = 2 * side + 4 * side + 2 + 4
    vmem = pltpu.VMEM
    return pl.pallas_call(
        functools.partial(torus_reduce_kernel, side),
        out_shape=jax.ShapeDtypeStruct((row_count, width), jnp.bfloat16),
        in_specs=[pl.BlockSpec(memory_space=vmem)],
        out_specs=pl.BlockSpec(memory_space=vmem),
        scratch_shapes=[
            vmem(piece, parts.dtype),
            vmem(piece, parts.dtype),
            vmem(piece, parts.dtype),
            vmem(piece, parts.dtype),
            vmem(piece, jnp.float32),
            vmem(one, parts.dtype),
            vmem(one, parts.dtype),
            vmem(one, parts.dtype),
            vmem(one, parts.dtype),
            vmem(one, parts.dtype),
            vmem(one, parts.dtype),
            pltpu.SemaphoreType.DMA((copies,)),
            pltpu.SemaphoreType.DMA((copies,)),
        ],
        compiler_params=pltpu.CompilerParams(
            collective_id=collective_id, has_side_effects=True
        ),
    )(parts)


def exchange_kernel(axis, rows, send_ref, recv_ref, send_sems, recv_sems, local_sem):
    count = lax.axis_size(axis)
    me = lax.axis_index(axis)
    barrier = pltpu.get_barrier_semaphore()

    @pl.loop(1, count)
    def _(step):
        peer = lax.rem(me + step, count)
        pl.semaphore_signal(barrier, inc=1, device_id={axis: peer}, device_id_type=MESH_ID)

    pl.semaphore_wait(barrier, count - 1)
    local = pltpu.make_async_copy(
        send_ref.at[pl.ds(me * rows, rows)], recv_ref.at[pl.ds(me * rows, rows)], local_sem
    )
    local.start()

    @pl.loop(1, count)
    def _(step):
        peer = lax.rem(me + step, count)
        pltpu.make_async_remote_copy(
            src_ref=send_ref.at[pl.ds(peer * rows, rows)],
            dst_ref=recv_ref.at[pl.ds(me * rows, rows)],
            send_sem=send_sems.at[peer],
            recv_sem=recv_sems.at[me],
            device_id={axis: peer},
            device_id_type=MESH_ID,
        ).start()

    @pl.loop(1, count)
    def _(step):
        peer = lax.rem(me + step, count)
        pltpu.make_async_remote_copy(
            src_ref=send_ref.at[pl.ds(peer * rows, rows)],
            dst_ref=recv_ref.at[pl.ds(peer * rows, rows)],
            send_sem=send_sems.at[peer],
            recv_sem=recv_sems.at[peer],
            device_id={axis: peer},
            device_id_type=MESH_ID,
        ).wait()

    local.wait()


def exchange(send, axis, collective_id):
    count = lax.axis_size(axis)
    rows = send.shape[0] // count
    return pl.pallas_call(
        functools.partial(exchange_kernel, axis, rows),
        out_shape=jax.ShapeDtypeStruct(send.shape, send.dtype),
        in_specs=[pl.BlockSpec(memory_space=pl.ANY)],
        out_specs=pl.BlockSpec(memory_space=pl.ANY),
        scratch_shapes=[
            pltpu.SemaphoreType.DMA((count,)),
            pltpu.SemaphoreType.DMA((count,)),
            pltpu.SemaphoreType.DMA(()),
        ],
        compiler_params=pltpu.CompilerParams(
            collective_id=collective_id, has_side_effects=True
        ),
    )(send)


def dispatch_expert_kernel(axis, rows, tile, send_ref, gate_hbm, up_hbm, down_hbm,
                           segment_hbm, sgate_hbm, sup_hbm, sdown_hbm, back_ref, shared_ref,
                           recv, gate_w, up_w, down_w, hidden, segment, sgate, sup, sdown,
                           out_ref, send_sems, recv_sems, local_sems, back_send, back_recv):
    count = lax.axis_size(axis)
    me = lax.axis_index(axis)
    weights = [
        pltpu.make_async_copy(gate_hbm.at[0], gate_w, local_sems.at[0]),
        pltpu.make_async_copy(up_hbm.at[0], up_w, local_sems.at[1]),
        pltpu.make_async_copy(down_hbm.at[0], down_w, local_sems.at[2]),
    ]
    shared_inputs = [
        pltpu.make_async_copy(segment_hbm, segment, local_sems.at[4]),
        pltpu.make_async_copy(sgate_hbm, sgate, local_sems.at[5]),
        pltpu.make_async_copy(sup_hbm, sup, local_sems.at[6]),
        pltpu.make_async_copy(sdown_hbm, sdown, local_sems.at[7]),
    ]
    for copy in shared_inputs + weights:
        copy.start()
    barrier = pltpu.get_barrier_semaphore()

    @pl.loop(1, count)
    def _(step):
        peer = lax.rem(me + step, count)
        pl.semaphore_signal(barrier, inc=1, device_id={axis: peer}, device_id_type=MESH_ID)

    pl.semaphore_wait(barrier, count - 1)
    local = pltpu.make_async_copy(
        send_ref.at[pl.ds(me * rows, rows)], recv.at[pl.ds(me * rows, rows)], local_sems.at[3]
    )
    local.start()

    @pl.loop(1, count)
    def _(step):
        peer = lax.rem(me + step, count)
        pltpu.make_async_remote_copy(
            src_ref=send_ref.at[pl.ds(peer * rows, rows)],
            dst_ref=recv.at[pl.ds(me * rows, rows)],
            send_sem=send_sems.at[peer],
            recv_sem=recv_sems.at[me],
            device_id={axis: peer},
            device_id_type=MESH_ID,
        ).start()

    for copy in shared_inputs:
        copy.wait()
    tokens = segment[...]
    gate_part = jnp.dot(tokens, sgate[...], preferred_element_type=jnp.float32)
    up_part = jnp.dot(tokens, sup[...], preferred_element_type=jnp.float32)
    shared_hidden = (gate_part / (1.0 + jnp.exp(-gate_part)) * up_part).astype(sdown.dtype)

    @pl.loop(0, sdown.shape[1] // (2 * tile))
    def _(t):
        cols = pl.ds(pl.multiple_of(t * 2 * tile, 2 * tile), 2 * tile)
        shared_ref[:, cols] = jnp.dot(
            shared_hidden, sdown[:, cols], preferred_element_type=jnp.float32
        )

    @pl.loop(1, count)
    def _(step):
        peer = lax.rem(me + step, count)
        pltpu.make_async_remote_copy(
            src_ref=send_ref.at[pl.ds(peer * rows, rows)],
            dst_ref=recv.at[pl.ds(peer * rows, rows)],
            send_sem=send_sems.at[peer],
            recv_sem=recv_sems.at[peer],
            device_id={axis: peer},
            device_id_type=MESH_ID,
        ).wait()

    local.wait()
    weights[0].wait()
    weights[1].wait()

    @pl.loop(0, gate_w.shape[1] // tile)
    def _(t):
        cols = pl.ds(pl.multiple_of(t * tile, tile), tile)
        tokens = recv[...]
        gate_part = jnp.dot(tokens, gate_w[:, cols], preferred_element_type=jnp.float32)
        up_part = jnp.dot(tokens, up_w[:, cols], preferred_element_type=jnp.float32)
        hidden[:, cols] = (gate_part / (1.0 + jnp.exp(-gate_part)) * up_part).astype(hidden.dtype)

    weights[2].wait()
    chunks = 2
    per_chunk = count // chunks
    chunk_rows = per_chunk * rows
    for part in range(chunks):
        lines = pl.ds(part * chunk_rows, chunk_rows)

        @pl.loop(0, down_w.shape[1] // (2 * tile))
        def _(t):
            cols = pl.ds(pl.multiple_of(t * 2 * tile, 2 * tile), 2 * tile)
            out_ref[lines, cols] = jnp.dot(
                hidden[lines, :], down_w[:, cols], preferred_element_type=jnp.float32
            ).astype(out_ref.dtype)

        @pl.loop(part * per_chunk, (part + 1) * per_chunk)
        def _(peer):
            @pl.when(peer != me)
            def _():
                pltpu.make_async_remote_copy(
                    src_ref=out_ref.at[pl.ds(peer * rows, rows)],
                    dst_ref=back_ref.at[pl.ds(me * rows, rows)],
                    send_sem=back_send.at[peer],
                    recv_sem=back_recv.at[me],
                    device_id={axis: peer},
                    device_id_type=MESH_ID,
                ).start()

            @pl.when(peer == me)
            def _():
                pltpu.make_async_copy(
                    out_ref.at[pl.ds(peer * rows, rows)],
                    back_ref.at[pl.ds(me * rows, rows)],
                    local_sems.at[8],
                ).start()

    @pl.loop(0, count)
    def _(peer):
        @pl.when(peer != me)
        def _():
            pltpu.make_async_remote_copy(
                src_ref=out_ref.at[pl.ds(peer * rows, rows)],
                dst_ref=back_ref.at[pl.ds(peer * rows, rows)],
                send_sem=back_send.at[peer],
                recv_sem=back_recv.at[peer],
                device_id={axis: peer},
                device_id_type=MESH_ID,
            ).wait()

        @pl.when(peer == me)
        def _():
            pltpu.make_async_copy(
                out_ref.at[pl.ds(peer * rows, rows)],
                back_ref.at[pl.ds(me * rows, rows)],
                local_sems.at[8],
            ).wait()


def dispatch_expert(send, gate, up, down, segment, sgate, sup, sdown, axis, collective_id):
    count = lax.axis_size(axis)
    rows = send.shape[0] // count
    width = gate.shape[2]
    any_space = pl.BlockSpec(memory_space=pl.ANY)
    vmem_space = pl.BlockSpec(memory_space=pltpu.VMEM)
    return pl.pallas_call(
        functools.partial(dispatch_expert_kernel, axis, rows, 256),
        out_shape=(
            jax.ShapeDtypeStruct(send.shape, send.dtype),
            jax.ShapeDtypeStruct((segment.shape[0], sdown.shape[1]), jnp.float32),
        ),
        in_specs=[any_space] * 8,
        out_specs=(vmem_space, vmem_space),
        scratch_shapes=[
            pltpu.VMEM(send.shape, send.dtype),
            pltpu.VMEM(gate.shape[1:], gate.dtype),
            pltpu.VMEM(up.shape[1:], up.dtype),
            pltpu.VMEM(down.shape[1:], down.dtype),
            pltpu.VMEM((send.shape[0], width), jnp.bfloat16),
            pltpu.VMEM(segment.shape, segment.dtype),
            pltpu.VMEM(sgate.shape, sgate.dtype),
            pltpu.VMEM(sup.shape, sup.dtype),
            pltpu.VMEM(sdown.shape, sdown.dtype),
            pltpu.VMEM(send.shape, send.dtype),
            pltpu.SemaphoreType.DMA((count,)),
            pltpu.SemaphoreType.DMA((count,)),
            pltpu.SemaphoreType.DMA((9,)),
            pltpu.SemaphoreType.DMA((count,)),
            pltpu.SemaphoreType.DMA((count,)),
        ],
        compiler_params=pltpu.CompilerParams(
            collective_id=collective_id, has_side_effects=True,
            vmem_limit_bytes=56 * 1024 * 1024,
        ),
    )(send, gate, up, down, segment, sgate, sup, sdown)


def gated_mlp(inputs, gate_matrix, up_matrix, down_matrix):
    gate_part = jnp.dot(inputs, gate_matrix, preferred_element_type=jnp.float32)
    up_part = jnp.dot(inputs, up_matrix, preferred_element_type=jnp.float32)
    hidden = (jax.nn.silu(gate_part) * up_part).astype(jnp.bfloat16)
    return jnp.dot(hidden, down_matrix, preferred_element_type=jnp.float32).astype(jnp.bfloat16)


def gate_weights(gate_score):
    values = gate_score.astype(jnp.float32)
    return 2.5 * values / jnp.sum(values, axis=-1, keepdims=True)


def weighted_rows(weights, rows):
    high = weights.astype(jnp.bfloat16)
    low = (weights - high.astype(jnp.float32)).astype(jnp.bfloat16)
    return jnp.dot(high, rows, preferred_element_type=jnp.float32) + jnp.dot(
        low, rows, preferred_element_type=jnp.float32
    )


def per_device(
    tokens,
    experts,
    gate_score,
    expert_gate,
    expert_up,
    expert_down,
    shared_gate,
    shared_up,
    shared_down,
):
    row_count = tokens.shape[0]
    model_width = tokens.shape[1]
    inner_count = lax.axis_size("inner")
    outer_count = lax.axis_size("outer")
    capacity = TOPK // TOP_GROUPS
    me = lax.axis_index("inner")
    side = math.isqrt(inner_count)
    routing = jnp.concatenate([experts, gate_score], axis=1).astype(jnp.bfloat16)
    routing = jnp.pad(routing, ((0, 0), (0, 128 - routing.shape[1])))
    gathered, gathered_routing = torus_gather([tokens, routing], side, 0)
    segment = gathered.reshape(inner_count * row_count, model_width)
    all_experts = gathered_routing[:, :, :TOPK].astype(jnp.int32)
    all_scores = gathered_routing[:, :, TOPK:2 * TOPK].astype(jnp.int32)
    weights = gate_weights(all_scores)
    local_experts = jnp.arange(outer_count, dtype=jnp.int32) * inner_count + me
    matches = all_experts[..., None] == local_experts
    named = jnp.any(matches, axis=2)
    named_int = named.astype(jnp.int32)
    earlier = jnp.cumsum(named_int, axis=1) - named_int
    slot_ids = jnp.arange(capacity, dtype=jnp.int32)
    placed = jnp.logical_and(named[..., None], earlier[..., None] == slot_ids)
    same_block = jnp.eye(inner_count, dtype=jnp.bool_)
    selector = jnp.logical_and(
        jnp.transpose(placed, (2, 0, 3, 1))[:, :, :, None, :],
        same_block[None, :, None, :, None],
    ).reshape(outer_count * inner_count * capacity, inner_count * row_count)
    outbound = jnp.dot(
        selector.astype(jnp.bfloat16), segment, preferred_element_type=jnp.float32
    ).astype(jnp.bfloat16)
    returned, shared = dispatch_expert(
        outbound, expert_gate, expert_up, expert_down,
        segment, shared_gate, shared_up, shared_down, "outer", 1,
    )
    slot_weight = jnp.sum(jnp.where(matches, weights[..., None], 0.0), axis=2)
    placed_weight = jnp.where(placed, slot_weight[..., None], 0.0)
    combine = jnp.where(
        same_block[:, None, None, :, None],
        jnp.transpose(placed_weight, (0, 1, 2, 3))[:, :, :, None, :],
        0.0,
    ).reshape(inner_count * row_count, outer_count * inner_count * capacity)
    routed = weighted_rows(combine, returned)
    total = (shared + routed).astype(jnp.bfloat16)
    return torus_reduce(total.reshape(inner_count, row_count, model_width), side, 3)


def solution(mesh):
    return jax.shard_map(
        per_device,
        mesh=mesh,
        in_specs=(
            P(("outer", "inner"), None),
            P(("outer", "inner"), None),
            P(("outer", "inner"), None),
            P(("outer", "inner"), None, None),
            P(("outer", "inner"), None, None),
            P(("outer", "inner"), None, None),
            P(None, "inner"),
            P(None, "inner"),
            P("inner", None),
        ),
        out_specs=P(("outer", "inner"), None),
        check_vma=False,
    )
```

```python
import functools
import math

import jax
import jax.numpy as jnp
from jax import lax
from jax.experimental import pallas as pl
from jax.experimental.pallas import tpu as pltpu
from jax.sharding import PartitionSpec as P

TOPK = 8
TOP_GROUPS = 4
MESH_ID = pl.DeviceIdType.MESH


def torus_gather_kernel(side, count, *refs):
    sources = refs[:count]
    outs = refs[count:2 * count]
    send_sems, recv_sems, local_sems = refs[2 * count:]
    me = lax.axis_index("inner")
    z, y = me // side, me % side
    half = sources[0].shape[0] // 2

    def node(zz, yy):
        return lax.rem(zz + side, side) * side + lax.rem(yy + side, side)

    steps = [
        (lambda zz, yy, k: node(zz, yy + k), lambda zz, yy, k: node(zz + k, yy)),
        (lambda zz, yy, k: node(zz + k, yy), lambda zz, yy, k: node(zz, yy + k)),
    ]
    neighbours = [
        node(z, y + 1), node(z, y - 1), node(z, y + 2),
        node(z + 1, y), node(z - 1, y), node(z + 2, y),
    ]
    barrier = pltpu.get_barrier_semaphore()
    for peer in neighbours:
        pl.semaphore_signal(barrier, inc=1, device_id={"inner": peer}, device_id_type=MESH_ID)
    pl.semaphore_wait(barrier, len(neighbours))

    rows = [pl.ds(0, half), pl.ds(half, half)]
    local_copies = []
    for a in range(count):
        for h in range(2):
            copy = pltpu.make_async_copy(
                sources[a].at[rows[h]], outs[a].at[me, rows[h]], local_sems.at[a, h]
            )
            copy.start()
            local_copies.append(copy)

    counter = [0]

    def run_round(moves):
        started = []
        for block, h, dest, from_input in moves:
            index = counter[0]
            counter[0] += 1
            for a in range(count):
                src = sources[a].at[rows[h]] if from_input else outs[a].at[block, rows[h]]
                copy = pltpu.make_async_remote_copy(
                    src_ref=src,
                    dst_ref=outs[a].at[block, rows[h]],
                    send_sem=send_sems.at[a, index],
                    recv_sem=recv_sems.at[a, index],
                    device_id={"inner": dest},
                    device_id_type=MESH_ID,
                )
                copy.start()
                started.append(copy)
        return started

    def finish(started, incoming):
        for copy in started:
            copy.wait_send()
        for index, block, h, sender in incoming:
            for a in range(count):
                pltpu.make_async_remote_copy(
                    src_ref=outs[a].at[block, rows[h]],
                    dst_ref=outs[a].at[block, rows[h]],
                    send_sem=send_sems.at[a, index],
                    recv_sem=recv_sems.at[a, index],
                    device_id={"inner": sender},
                    device_id_type=MESH_ID,
                ).wait_recv()

    base = counter[0]
    moves, incoming = [], []
    for h in range(2):
        first = steps[h][0]
        for k in (1, -1, 2):
            moves.append((me, h, first(z, y, k), True))
            incoming.append((base + len(incoming), first(z, y, -k), h, first(z, y, -k)))
    finish(run_round(moves), incoming)
    for copy in local_copies:
        copy.wait()
    base = counter[0]
    moves, incoming = [], []
    for h in range(2):
        first, second = steps[h]
        for k in (1, -1):
            for j in range(side):
                moves.append((first(z, y, j), h, second(z, y, k), False))
                origin = second(z, y, -k)
                oz, oy = origin // side, origin % side
                incoming.append((base + len(incoming), first(oz, oy, j), h, origin))
    finish(run_round(moves), incoming)
    base = counter[0]
    moves, incoming = [], []
    for h in range(2):
        first, second = steps[h]
        src_node = second(z, y, -1)
        sz, sy = src_node // side, src_node % side
        far = second(z, y, -2)
        fz, fy = far // side, far % side
        for j in range(side):
            moves.append((first(sz, sy, j), h, second(z, y, 1), False))
            incoming.append((base + len(incoming), first(fz, fy, j), h, src_node))
    finish(run_round(moves), incoming)


def torus_gather(arrays, side, collective_id):
    members = lax.axis_size("inner")
    count = len(arrays)
    copies = 4 + 2 + 4 * side + 2 * side
    return pl.pallas_call(
        functools.partial(torus_gather_kernel, side, count),
        out_shape=tuple(
            jax.ShapeDtypeStruct((members,) + x.shape, x.dtype) for x in arrays
        ),
        in_specs=[pl.BlockSpec(memory_space=pl.ANY)] * count,
        out_specs=tuple(pl.BlockSpec(memory_space=pl.ANY) for _ in arrays),
        scratch_shapes=[
            pltpu.SemaphoreType.DMA((count, copies)),
            pltpu.SemaphoreType.DMA((count, copies)),
            pltpu.SemaphoreType.DMA((count, 2)),
        ],
        compiler_params=pltpu.CompilerParams(
            collective_id=collective_id, has_side_effects=True
        ),
    )(*arrays)


def torus_reduce_kernel(side, x_ref, out_ref, recv_a, recv_bp, recv_bm, send_b, partial,
                        send_a2, recv_a2, send_b2, send_c2, recv_b2p, recv_b2m,
                        send_sems, recv_sems):
    me = lax.axis_index("inner")
    z, y = me // side, me % side
    half = x_ref.shape[1] // 2
    rows = [pl.ds(0, half), pl.ds(half, half)]

    def node(zz, yy):
        return lax.rem(zz + side, side) * side + lax.rem(yy + side, side)

    def wrap(p):
        return lax.rem(p + side, side)

    plans = [
        (lambda k: node(z + k, y), lambda k: node(z, y + k), z, y,
         lambda pos, j: pos * side + j),
        (lambda k: node(z, y + k), lambda k: node(z + k, y), y, z,
         lambda pos, j: j * side + pos),
    ]
    neighbours = [
        node(z, y + 1), node(z, y - 1), node(z, y + 2),
        node(z + 1, y), node(z - 1, y), node(z + 2, y),
    ]
    barrier = pltpu.get_barrier_semaphore()
    for peer in neighbours:
        pl.semaphore_signal(barrier, inc=1, device_id={"inner": peer}, device_id_type=MESH_ID)
    pl.semaphore_wait(barrier, len(neighbours))

    counter = [0]

    def send(src, dst, dest):
        index = counter[0]
        counter[0] += 1
        copy = pltpu.make_async_remote_copy(
            src_ref=src, dst_ref=dst, send_sem=send_sems.at[index],
            recv_sem=recv_sems.at[index], device_id={"inner": dest},
            device_id_type=MESH_ID,
        )
        copy.start()
        return copy, (index, dst, src)

    def settle(sent, senders):
        for copy, _ in sent:
            copy.wait_send()
        for (_, (index, dst, src)), sender in zip(sent, senders):
            pltpu.make_async_remote_copy(
                src_ref=src, dst_ref=dst, send_sem=send_sems.at[index],
                recv_sem=recv_sems.at[index], device_id={"inner": sender},
                device_id_type=MESH_ID,
            ).wait_recv()

    sent, senders = [], []
    for h, (ring1, ring2, p1, p2, block) in enumerate(plans):
        for j in range(side):
            sent.append(send(x_ref.at[block(wrap(p1 + 2), j), rows[h]], recv_a.at[h, j], ring1(1)))
            senders.append(ring1(-1))
    settle(sent, senders)
    sent, senders = [], []
    for h, (ring1, ring2, p1, p2, block) in enumerate(plans):
        for j in range(side):
            mine = x_ref[block(wrap(p1 + 1), j), rows[h], :].astype(jnp.float32)
            send_b[h, j] = (mine + recv_a[h, j].astype(jnp.float32)).astype(send_b.dtype)
        for j in range(side):
            sent.append(send(send_b.at[h, j], recv_bp.at[h, j], ring1(1)))
            senders.append(ring1(-1))
            sent.append(send(x_ref.at[block(wrap(p1 - 1), j), rows[h]], recv_bm.at[h, j], ring1(-1)))
            senders.append(ring1(1))
    settle(sent, senders)
    for h, (ring1, ring2, p1, p2, block) in enumerate(plans):
        for j in range(side):
            partial[h, j] = (
                x_ref[block(p1, j), rows[h], :].astype(jnp.float32)
                + recv_bp[h, j].astype(jnp.float32)
                + recv_bm[h, j].astype(jnp.float32)
            )
    sent, senders = [], []
    for h, (ring1, ring2, p1, p2, block) in enumerate(plans):
        send_a2[h] = partial[h, wrap(p2 + 2)].astype(send_a2.dtype)
        send_b2[h] = partial[h, wrap(p2 + 1)].astype(send_b2.dtype)
        send_c2[h] = partial[h, wrap(p2 - 1)].astype(send_c2.dtype)
        sent.append(send(send_a2.at[h], recv_a2.at[h], ring2(2)))
        senders.append(ring2(-2))
        sent.append(send(send_b2.at[h], recv_b2p.at[h], ring2(1)))
        senders.append(ring2(-1))
        sent.append(send(send_c2.at[h], recv_b2m.at[h], ring2(-1)))
        senders.append(ring2(1))
    settle(sent, senders)
    for h, (ring1, ring2, p1, p2, block) in enumerate(plans):
        out_ref[rows[h], :] = (
            partial[h, p2]
            + recv_a2[h].astype(jnp.float32)
            + recv_b2p[h].astype(jnp.float32)
            + recv_b2m[h].astype(jnp.float32)
        ).astype(out_ref.dtype)


def torus_reduce(parts, side, collective_id):
    _, row_count, width = parts.shape
    half = row_count // 2
    piece = (2, side, half, width)
    one = (2, half, width)
    copies = 2 * side + 4 * side + 2 + 4
    vmem = pltpu.VMEM
    return pl.pallas_call(
        functools.partial(torus_reduce_kernel, side),
        out_shape=jax.ShapeDtypeStruct((row_count, width), jnp.bfloat16),
        in_specs=[pl.BlockSpec(memory_space=vmem)],
        out_specs=pl.BlockSpec(memory_space=vmem),
        scratch_shapes=[
            vmem(piece, parts.dtype),
            vmem(piece, parts.dtype),
            vmem(piece, parts.dtype),
            vmem(piece, parts.dtype),
            vmem(piece, jnp.float32),
            vmem(one, parts.dtype),
            vmem(one, parts.dtype),
            vmem(one, parts.dtype),
            vmem(one, parts.dtype),
            vmem(one, parts.dtype),
            vmem(one, parts.dtype),
            pltpu.SemaphoreType.DMA((copies,)),
            pltpu.SemaphoreType.DMA((copies,)),
        ],
        compiler_params=pltpu.CompilerParams(
            collective_id=collective_id, has_side_effects=True
        ),
    )(parts)


def exchange_kernel(axis, rows, send_ref, recv_ref, send_sems, recv_sems, local_sem):
    count = lax.axis_size(axis)
    me = lax.axis_index(axis)
    barrier = pltpu.get_barrier_semaphore()

    @pl.loop(1, count)
    def _(step):
        peer = lax.rem(me + step, count)
        pl.semaphore_signal(barrier, inc=1, device_id={axis: peer}, device_id_type=MESH_ID)

    pl.semaphore_wait(barrier, count - 1)
    local = pltpu.make_async_copy(
        send_ref.at[pl.ds(me * rows, rows)], recv_ref.at[pl.ds(me * rows, rows)], local_sem
    )
    local.start()

    @pl.loop(1, count)
    def _(step):
        peer = lax.rem(me + step, count)
        pltpu.make_async_remote_copy(
            src_ref=send_ref.at[pl.ds(peer * rows, rows)],
            dst_ref=recv_ref.at[pl.ds(me * rows, rows)],
            send_sem=send_sems.at[peer],
            recv_sem=recv_sems.at[me],
            device_id={axis: peer},
            device_id_type=MESH_ID,
        ).start()

    @pl.loop(1, count)
    def _(step):
        peer = lax.rem(me + step, count)
        pltpu.make_async_remote_copy(
            src_ref=send_ref.at[pl.ds(peer * rows, rows)],
            dst_ref=recv_ref.at[pl.ds(peer * rows, rows)],
            send_sem=send_sems.at[peer],
            recv_sem=recv_sems.at[peer],
            device_id={axis: peer},
            device_id_type=MESH_ID,
        ).wait()

    local.wait()


def exchange(send, axis, collective_id):
    count = lax.axis_size(axis)
    rows = send.shape[0] // count
    return pl.pallas_call(
        functools.partial(exchange_kernel, axis, rows),
        out_shape=jax.ShapeDtypeStruct(send.shape, send.dtype),
        in_specs=[pl.BlockSpec(memory_space=pl.ANY)],
        out_specs=pl.BlockSpec(memory_space=pl.ANY),
        scratch_shapes=[
            pltpu.SemaphoreType.DMA((count,)),
            pltpu.SemaphoreType.DMA((count,)),
            pltpu.SemaphoreType.DMA(()),
        ],
        compiler_params=pltpu.CompilerParams(
            collective_id=collective_id, has_side_effects=True
        ),
    )(send)


def dispatch_expert_kernel(axis, rows, tile, send_ref, gate_hbm, up_hbm, down_hbm,
                           segment_hbm, sgate_hbm, sup_hbm, sdown_hbm, back_ref, shared_ref,
                           recv, gate_w, up_w, down_w, hidden, segment, sgate, sup, sdown,
                           out_ref, send_sems, recv_sems, local_sems, back_send, back_recv):
    count = lax.axis_size(axis)
    me = lax.axis_index(axis)
    weights = [
        pltpu.make_async_copy(gate_hbm.at[0], gate_w, local_sems.at[0]),
        pltpu.make_async_copy(up_hbm.at[0], up_w, local_sems.at[1]),
        pltpu.make_async_copy(down_hbm.at[0], down_w, local_sems.at[2]),
    ]
    shared_inputs = [
        pltpu.make_async_copy(segment_hbm, segment, local_sems.at[4]),
        pltpu.make_async_copy(sgate_hbm, sgate, local_sems.at[5]),
        pltpu.make_async_copy(sup_hbm, sup, local_sems.at[6]),
        pltpu.make_async_copy(sdown_hbm, sdown, local_sems.at[7]),
    ]
    for copy in shared_inputs + weights:
        copy.start()
    barrier = pltpu.get_barrier_semaphore()

    @pl.loop(1, count)
    def _(step):
        peer = lax.rem(me + step, count)
        pl.semaphore_signal(barrier, inc=1, device_id={axis: peer}, device_id_type=MESH_ID)

    pl.semaphore_wait(barrier, count - 1)
    local = pltpu.make_async_copy(
        send_ref.at[pl.ds(me * rows, rows)], recv.at[pl.ds(me * rows, rows)], local_sems.at[3]
    )
    local.start()

    @pl.loop(1, count)
    def _(step):
        peer = lax.rem(me + step, count)
        pltpu.make_async_remote_copy(
            src_ref=send_ref.at[pl.ds(peer * rows, rows)],
            dst_ref=recv.at[pl.ds(me * rows, rows)],
            send_sem=send_sems.at[peer],
            recv_sem=recv_sems.at[me],
            device_id={axis: peer},
            device_id_type=MESH_ID,
        ).start()

    for copy in shared_inputs:
        copy.wait()
    tokens = segment[...]
    gate_part = jnp.dot(tokens, sgate[...], preferred_element_type=jnp.float32)
    up_part = jnp.dot(tokens, sup[...], preferred_element_type=jnp.float32)
    shared_hidden = (gate_part / (1.0 + jnp.exp(-gate_part)) * up_part).astype(sdown.dtype)

    @pl.loop(0, sdown.shape[1] // (2 * tile))
    def _(t):
        cols = pl.ds(pl.multiple_of(t * 2 * tile, 2 * tile), 2 * tile)
        shared_ref[:, cols] = jnp.dot(
            shared_hidden, sdown[:, cols], preferred_element_type=jnp.float32
        )

    @pl.loop(1, count)
    def _(step):
        peer = lax.rem(me + step, count)
        pltpu.make_async_remote_copy(
            src_ref=send_ref.at[pl.ds(peer * rows, rows)],
            dst_ref=recv.at[pl.ds(peer * rows, rows)],
            send_sem=send_sems.at[peer],
            recv_sem=recv_sems.at[peer],
            device_id={axis: peer},
            device_id_type=MESH_ID,
        ).wait()

    local.wait()
    weights[0].wait()
    weights[1].wait()

    @pl.loop(0, gate_w.shape[1] // tile)
    def _(t):
        cols = pl.ds(pl.multiple_of(t * tile, tile), tile)
        tokens = recv[...]
        gate_part = jnp.dot(tokens, gate_w[:, cols], preferred_element_type=jnp.float32)
        up_part = jnp.dot(tokens, up_w[:, cols], preferred_element_type=jnp.float32)
        hidden[:, cols] = (gate_part / (1.0 + jnp.exp(-gate_part)) * up_part).astype(hidden.dtype)

    weights[2].wait()
    chunks = 2
    per_chunk = count // chunks
    chunk_rows = per_chunk * rows
    for part in range(chunks):
        lines = pl.ds(part * chunk_rows, chunk_rows)

        @pl.loop(0, down_w.shape[1] // (2 * tile))
        def _(t):
            cols = pl.ds(pl.multiple_of(t * 2 * tile, 2 * tile), 2 * tile)
            out_ref[lines, cols] = jnp.dot(
                hidden[lines, :], down_w[:, cols], preferred_element_type=jnp.float32
            ).astype(out_ref.dtype)

        @pl.loop(part * per_chunk, (part + 1) * per_chunk)
        def _(peer):
            @pl.when(peer != me)
            def _():
                pltpu.make_async_remote_copy(
                    src_ref=out_ref.at[pl.ds(peer * rows, rows)],
                    dst_ref=back_ref.at[pl.ds(me * rows, rows)],
                    send_sem=back_send.at[peer],
                    recv_sem=back_recv.at[me],
                    device_id={axis: peer},
                    device_id_type=MESH_ID,
                ).start()

            @pl.when(peer == me)
            def _():
                pltpu.make_async_copy(
                    out_ref.at[pl.ds(peer * rows, rows)],
                    back_ref.at[pl.ds(me * rows, rows)],
                    local_sems.at[8],
                ).start()

    @pl.loop(0, count)
    def _(peer):
        @pl.when(peer != me)
        def _():
            pltpu.make_async_remote_copy(
                src_ref=out_ref.at[pl.ds(peer * rows, rows)],
                dst_ref=back_ref.at[pl.ds(peer * rows, rows)],
                send_sem=back_send.at[peer],
                recv_sem=back_recv.at[peer],
                device_id={axis: peer},
                device_id_type=MESH_ID,
            ).wait()

        @pl.when(peer == me)
        def _():
            pltpu.make_async_copy(
                out_ref.at[pl.ds(peer * rows, rows)],
                back_ref.at[pl.ds(me * rows, rows)],
                local_sems.at[8],
            ).wait()


def dispatch_expert(send, gate, up, down, segment, sgate, sup, sdown, axis, collective_id):
    count = lax.axis_size(axis)
    rows = send.shape[0] // count
    width = gate.shape[2]
    any_space = pl.BlockSpec(memory_space=pl.ANY)
    vmem_space = pl.BlockSpec(memory_space=pltpu.VMEM)
    return pl.pallas_call(
        functools.partial(dispatch_expert_kernel, axis, rows, 256),
        out_shape=(
            jax.ShapeDtypeStruct(send.shape, send.dtype),
            jax.ShapeDtypeStruct((segment.shape[0], sdown.shape[1]), jnp.float32),
        ),
        in_specs=[any_space] * 8,
        out_specs=(vmem_space, vmem_space),
        scratch_shapes=[
            pltpu.VMEM(send.shape, send.dtype),
            pltpu.VMEM(gate.shape[1:], gate.dtype),
            pltpu.VMEM(up.shape[1:], up.dtype),
            pltpu.VMEM(down.shape[1:], down.dtype),
            pltpu.VMEM((send.shape[0], width), jnp.bfloat16),
            pltpu.VMEM(segment.shape, segment.dtype),
            pltpu.VMEM(sgate.shape, sgate.dtype),
            pltpu.VMEM(sup.shape, sup.dtype),
            pltpu.VMEM(sdown.shape, sdown.dtype),
            pltpu.VMEM(send.shape, send.dtype),
            pltpu.SemaphoreType.DMA((count,)),
            pltpu.SemaphoreType.DMA((count,)),
            pltpu.SemaphoreType.DMA((9,)),
            pltpu.SemaphoreType.DMA((count,)),
            pltpu.SemaphoreType.DMA((count,)),
        ],
        compiler_params=pltpu.CompilerParams(
            collective_id=collective_id, has_side_effects=True,
            vmem_limit_bytes=56 * 1024 * 1024,
        ),
    )(send, gate, up, down, segment, sgate, sup, sdown)


def gated_mlp(inputs, gate_matrix, up_matrix, down_matrix):
    gate_part = jnp.dot(inputs, gate_matrix, preferred_element_type=jnp.float32)
    up_part = jnp.dot(inputs, up_matrix, preferred_element_type=jnp.float32)
    hidden = (jax.nn.silu(gate_part) * up_part).astype(jnp.bfloat16)
    return jnp.dot(hidden, down_matrix, preferred_element_type=jnp.float32).astype(jnp.bfloat16)


def gate_weights(gate_score):
    values = gate_score.astype(jnp.float32)
    return 2.5 * values / jnp.sum(values, axis=-1, keepdims=True)


def weighted_rows(weights, rows):
    high = weights.astype(jnp.bfloat16)
    low = (weights - high.astype(jnp.float32)).astype(jnp.bfloat16)
    return jnp.dot(high, rows, preferred_element_type=jnp.float32) + jnp.dot(
        low, rows, preferred_element_type=jnp.float32
    )


def per_device(
    tokens,
    experts,
    gate_score,
    expert_gate,
    expert_up,
    expert_down,
    shared_gate,
    shared_up,
    shared_down,
):
    row_count = tokens.shape[0]
    model_width = tokens.shape[1]
    inner_count = lax.axis_size("inner")
    outer_count = lax.axis_size("outer")
    capacity = TOPK // TOP_GROUPS
    me = lax.axis_index("inner")
    side = math.isqrt(inner_count)
    routing = jnp.concatenate([experts, gate_score], axis=1).astype(jnp.bfloat16)
    routing = jnp.pad(routing, ((0, 0), (0, 128 - routing.shape[1])))
    gathered, gathered_routing = torus_gather([tokens, routing], side, 0)
    segment = gathered.reshape(inner_count * row_count, model_width)
    all_experts = gathered_routing[:, :, :TOPK].astype(jnp.int32)
    all_scores = gathered_routing[:, :, TOPK:2 * TOPK].astype(jnp.int32)
    weights = gate_weights(all_scores)
    local_experts = jnp.arange(outer_count, dtype=jnp.int32) * inner_count + me
    matches = all_experts[..., None] == local_experts
    named = jnp.any(matches, axis=2)
    named_int = named.astype(jnp.int32)
    earlier = jnp.cumsum(named_int, axis=1) - named_int
    slot_ids = jnp.arange(capacity, dtype=jnp.int32)
    placed = jnp.logical_and(named[..., None], earlier[..., None] == slot_ids)
    same_block = jnp.eye(inner_count, dtype=jnp.bool_)
    selector = jnp.logical_and(
        jnp.transpose(placed, (2, 0, 3, 1))[:, :, :, None, :],
        same_block[None, :, None, :, None],
    ).reshape(outer_count * inner_count * capacity, inner_count * row_count)
    outbound = jnp.dot(
        selector.astype(jnp.bfloat16), segment, preferred_element_type=jnp.float32
    ).astype(jnp.bfloat16)
    returned, shared = dispatch_expert(
        outbound, expert_gate, expert_up, expert_down,
        segment, shared_gate, shared_up, shared_down, "outer", 1,
    )
    slot_weight = jnp.sum(jnp.where(matches, weights[..., None], 0.0), axis=2)
    placed_weight = jnp.where(placed, slot_weight[..., None], 0.0)
    combine = jnp.where(
        same_block[:, None, None, :, None],
        jnp.transpose(placed_weight, (0, 1, 2, 3))[:, :, :, None, :],
        0.0,
    ).reshape(inner_count * row_count, outer_count * inner_count * capacity)
    routed = weighted_rows(combine, returned)
    total = (shared + routed).astype(jnp.bfloat16)
    return torus_reduce(total.reshape(inner_count, row_count, model_width), side, 3)


def solution(mesh):
    return jax.shard_map(
        per_device,
        mesh=mesh,
        in_specs=(
            P(("outer", "inner"), None),
            P(("outer", "inner"), None),
            P(("outer", "inner"), None),
            P(("outer", "inner"), None, None),
            P(("outer", "inner"), None, None),
            P(("outer", "inner"), None, None),
            P(None, "inner"),
            P(None, "inner"),
            P("inner", None),
        ),
        out_specs=P(("outer", "inner"), None),
        check_vma=False,
    )
```

```python
import functools
import math

import jax
import jax.numpy as jnp
from jax import lax
from jax.experimental import pallas as pl
from jax.experimental.pallas import tpu as pltpu
from jax.sharding import PartitionSpec as P

TOPK = 8
TOP_GROUPS = 4
MESH_ID = pl.DeviceIdType.MESH


def torus_gather_kernel(side, count, *refs):
    sources = refs[:count]
    outs = refs[count:2 * count]
    send_sems, recv_sems, local_sems = refs[2 * count:]
    me = lax.axis_index("inner")
    z, y = me // side, me % side
    half = sources[0].shape[0] // 2

    def node(zz, yy):
        return lax.rem(zz + side, side) * side + lax.rem(yy + side, side)

    steps = [
        (lambda zz, yy, k: node(zz, yy + k), lambda zz, yy, k: node(zz + k, yy)),
        (lambda zz, yy, k: node(zz + k, yy), lambda zz, yy, k: node(zz, yy + k)),
    ]
    neighbours = [
        node(z, y + 1), node(z, y - 1), node(z, y + 2),
        node(z + 1, y), node(z - 1, y), node(z + 2, y),
    ]
    barrier = pltpu.get_barrier_semaphore()
    for peer in neighbours:
        pl.semaphore_signal(barrier, inc=1, device_id={"inner": peer}, device_id_type=MESH_ID)
    pl.semaphore_wait(barrier, len(neighbours))

    rows = [pl.ds(0, half), pl.ds(half, half)]
    local_copies = []
    for a in range(count):
        for h in range(2):
            copy = pltpu.make_async_copy(
                sources[a].at[rows[h]], outs[a].at[me, rows[h]], local_sems.at[a, h]
            )
            copy.start()
            local_copies.append(copy)

    counter = [0]

    def run_round(moves):
        started = []
        for block, h, dest, from_input in moves:
            index = counter[0]
            counter[0] += 1
            for a in range(count):
                src = sources[a].at[rows[h]] if from_input else outs[a].at[block, rows[h]]
                copy = pltpu.make_async_remote_copy(
                    src_ref=src,
                    dst_ref=outs[a].at[block, rows[h]],
                    send_sem=send_sems.at[a, index],
                    recv_sem=recv_sems.at[a, index],
                    device_id={"inner": dest},
                    device_id_type=MESH_ID,
                )
                copy.start()
                started.append(copy)
        return started

    def finish(started, incoming):
        for copy in started:
            copy.wait_send()
        for index, block, h, sender in incoming:
            for a in range(count):
                pltpu.make_async_remote_copy(
                    src_ref=outs[a].at[block, rows[h]],
                    dst_ref=outs[a].at[block, rows[h]],
                    send_sem=send_sems.at[a, index],
                    recv_sem=recv_sems.at[a, index],
                    device_id={"inner": sender},
                    device_id_type=MESH_ID,
                ).wait_recv()

    base = counter[0]
    moves, incoming = [], []
    for h in range(2):
        first = steps[h][0]
        for k in (1, -1, 2):
            moves.append((me, h, first(z, y, k), True))
            incoming.append((base + len(incoming), first(z, y, -k), h, first(z, y, -k)))
    finish(run_round(moves), incoming)
    for copy in local_copies:
        copy.wait()
    base = counter[0]
    moves, incoming = [], []
    for h in range(2):
        first, second = steps[h]
        for k in (1, -1):
            for j in range(side):
                moves.append((first(z, y, j), h, second(z, y, k), False))
                origin = second(z, y, -k)
                oz, oy = origin // side, origin % side
                incoming.append((base + len(incoming), first(oz, oy, j), h, origin))
    finish(run_round(moves), incoming)
    base = counter[0]
    moves, incoming = [], []
    for h in range(2):
        first, second = steps[h]
        src_node = second(z, y, -1)
        sz, sy = src_node // side, src_node % side
        far = second(z, y, -2)
        fz, fy = far // side, far % side
        for j in range(side):
            moves.append((first(sz, sy, j), h, second(z, y, 1), False))
            incoming.append((base + len(incoming), first(fz, fy, j), h, src_node))
    finish(run_round(moves), incoming)


def torus_gather(arrays, side, collective_id):
    members = lax.axis_size("inner")
    count = len(arrays)
    copies = 4 + 2 + 4 * side + 2 * side
    return pl.pallas_call(
        functools.partial(torus_gather_kernel, side, count),
        out_shape=tuple(
            jax.ShapeDtypeStruct((members,) + x.shape, x.dtype) for x in arrays
        ),
        in_specs=[pl.BlockSpec(memory_space=pl.ANY)] * count,
        out_specs=tuple(pl.BlockSpec(memory_space=pl.ANY) for _ in arrays),
        scratch_shapes=[
            pltpu.SemaphoreType.DMA((count, copies)),
            pltpu.SemaphoreType.DMA((count, copies)),
            pltpu.SemaphoreType.DMA((count, 2)),
        ],
        compiler_params=pltpu.CompilerParams(
            collective_id=collective_id, has_side_effects=True
        ),
    )(*arrays)


def torus_reduce_kernel(side, tile, shared_ref, rows_ref, high_ref, low_ref, out_ref, x_ref, recv_a, recv_bp, recv_bm, send_b, partial,
                        send_a2, recv_a2, send_b2, send_c2, recv_b2p, recv_b2m,
                        send_sems, recv_sems):
    me = lax.axis_index("inner")
    z, y = me // side, me % side
    block_rows = out_ref.shape[0]
    half = block_rows // 2
    rows = [pl.ds(0, half), pl.ds(half, half)]

    def piece(block, h):
        return pl.ds(block * block_rows + h * half, half)

    def node(zz, yy):
        return lax.rem(zz + side, side) * side + lax.rem(yy + side, side)

    def wrap(p):
        return lax.rem(p + side, side)

    plans = [
        (lambda k: node(z + k, y), lambda k: node(z, y + k), z, y,
         lambda pos, j: pos * side + j),
        (lambda k: node(z, y + k), lambda k: node(z + k, y), y, z,
         lambda pos, j: j * side + pos),
    ]
    neighbours = [
        node(z, y + 1), node(z, y - 1), node(z, y + 2),
        node(z + 1, y), node(z - 1, y), node(z + 2, y),
    ]
    barrier = pltpu.get_barrier_semaphore()
    for peer in neighbours:
        pl.semaphore_signal(barrier, inc=1, device_id={"inner": peer}, device_id_type=MESH_ID)

    @pl.loop(0, x_ref.shape[1] // tile)
    def _(t):
        cols = pl.ds(pl.multiple_of(t * tile, tile), tile)
        back = rows_ref[:, cols]
        x_ref[:, cols] = (
            shared_ref[:, cols]
            + jnp.dot(high_ref[...], back, preferred_element_type=jnp.float32)
            + jnp.dot(low_ref[...], back, preferred_element_type=jnp.float32)
        ).astype(x_ref.dtype)

    pl.semaphore_wait(barrier, len(neighbours))

    counter = [0]

    def send(src, dst, dest):
        index = counter[0]
        counter[0] += 1
        copy = pltpu.make_async_remote_copy(
            src_ref=src, dst_ref=dst, send_sem=send_sems.at[index],
            recv_sem=recv_sems.at[index], device_id={"inner": dest},
            device_id_type=MESH_ID,
        )
        copy.start()
        return copy, (index, dst, src)

    def settle(sent, senders):
        for copy, _ in sent:
            copy.wait_send()
        for (_, (index, dst, src)), sender in zip(sent, senders):
            pltpu.make_async_remote_copy(
                src_ref=src, dst_ref=dst, send_sem=send_sems.at[index],
                recv_sem=recv_sems.at[index], device_id={"inner": sender},
                device_id_type=MESH_ID,
            ).wait_recv()

    sent, senders = [], []
    for h, (ring1, ring2, p1, p2, block) in enumerate(plans):
        for j in range(side):
            sent.append(send(x_ref.at[piece(block(wrap(p1 + 2), j), h)], recv_a.at[h, j], ring1(1)))
            senders.append(ring1(-1))
    settle(sent, senders)
    sent, senders = [], []
    for h, (ring1, ring2, p1, p2, block) in enumerate(plans):
        for j in range(side):
            mine = x_ref[piece(block(wrap(p1 + 1), j), h), :].astype(jnp.float32)
            send_b[h, j] = (mine + recv_a[h, j].astype(jnp.float32)).astype(send_b.dtype)
        for j in range(side):
            sent.append(send(send_b.at[h, j], recv_bp.at[h, j], ring1(1)))
            senders.append(ring1(-1))
            sent.append(send(x_ref.at[piece(block(wrap(p1 - 1), j), h)], recv_bm.at[h, j], ring1(-1)))
            senders.append(ring1(1))
    settle(sent, senders)
    for h, (ring1, ring2, p1, p2, block) in enumerate(plans):
        for j in range(side):
            partial[h, j] = (
                x_ref[piece(block(p1, j), h), :].astype(jnp.float32)
                + recv_bp[h, j].astype(jnp.float32)
                + recv_bm[h, j].astype(jnp.float32)
            )
    sent, senders = [], []
    for h, (ring1, ring2, p1, p2, block) in enumerate(plans):
        send_a2[h] = partial[h, wrap(p2 + 2)].astype(send_a2.dtype)
        send_b2[h] = partial[h, wrap(p2 + 1)].astype(send_b2.dtype)
        send_c2[h] = partial[h, wrap(p2 - 1)].astype(send_c2.dtype)
        sent.append(send(send_a2.at[h], recv_a2.at[h], ring2(2)))
        senders.append(ring2(-2))
        sent.append(send(send_b2.at[h], recv_b2p.at[h], ring2(1)))
        senders.append(ring2(-1))
        sent.append(send(send_c2.at[h], recv_b2m.at[h], ring2(-1)))
        senders.append(ring2(1))
    settle(sent, senders)
    for h, (ring1, ring2, p1, p2, block) in enumerate(plans):
        out_ref[rows[h], :] = (
            partial[h, p2]
            + recv_a2[h].astype(jnp.float32)
            + recv_b2p[h].astype(jnp.float32)
            + recv_b2m[h].astype(jnp.float32)
        ).astype(out_ref.dtype)


def torus_reduce(shared, back, high, low, side, collective_id):
    members = lax.axis_size("inner")
    width = shared.shape[1]
    row_count = shared.shape[0] // members
    half = row_count // 2
    piece = (2, side, half, width)
    one = (2, half, width)
    copies = 2 * side + 4 * side + 2 + 4
    vmem = pltpu.VMEM
    dtype = jnp.bfloat16
    return pl.pallas_call(
        functools.partial(torus_reduce_kernel, side, 512),
        out_shape=jax.ShapeDtypeStruct((row_count, width), jnp.float32),
        in_specs=[pl.BlockSpec(memory_space=vmem)] * 4,
        out_specs=pl.BlockSpec(memory_space=vmem),
        scratch_shapes=[
            vmem(shared.shape, dtype),
            vmem(piece, dtype),
            vmem(piece, dtype),
            vmem(piece, dtype),
            vmem(piece, dtype),
            vmem(piece, jnp.float32),
            vmem(one, dtype),
            vmem(one, dtype),
            vmem(one, dtype),
            vmem(one, dtype),
            vmem(one, dtype),
            vmem(one, dtype),
            pltpu.SemaphoreType.DMA((copies,)),
            pltpu.SemaphoreType.DMA((copies,)),
        ],
        compiler_params=pltpu.CompilerParams(
            collective_id=collective_id, has_side_effects=True
        ),
    )(shared, back, high, low)


def exchange_kernel(axis, rows, send_ref, recv_ref, send_sems, recv_sems, local_sem):
    count = lax.axis_size(axis)
    me = lax.axis_index(axis)
    barrier = pltpu.get_barrier_semaphore()

    @pl.loop(1, count)
    def _(step):
        peer = lax.rem(me + step, count)
        pl.semaphore_signal(barrier, inc=1, device_id={axis: peer}, device_id_type=MESH_ID)

    pl.semaphore_wait(barrier, count - 1)
    local = pltpu.make_async_copy(
        send_ref.at[pl.ds(me * rows, rows)], recv_ref.at[pl.ds(me * rows, rows)], local_sem
    )
    local.start()

    @pl.loop(1, count)
    def _(step):
        peer = lax.rem(me + step, count)
        pltpu.make_async_remote_copy(
            src_ref=send_ref.at[pl.ds(peer * rows, rows)],
            dst_ref=recv_ref.at[pl.ds(me * rows, rows)],
            send_sem=send_sems.at[peer],
            recv_sem=recv_sems.at[me],
            device_id={axis: peer},
            device_id_type=MESH_ID,
        ).start()

    @pl.loop(1, count)
    def _(step):
        peer = lax.rem(me + step, count)
        pltpu.make_async_remote_copy(
            src_ref=send_ref.at[pl.ds(peer * rows, rows)],
            dst_ref=recv_ref.at[pl.ds(peer * rows, rows)],
            send_sem=send_sems.at[peer],
            recv_sem=recv_sems.at[peer],
            device_id={axis: peer},
            device_id_type=MESH_ID,
        ).wait()

    local.wait()


def exchange(send, axis, collective_id):
    count = lax.axis_size(axis)
    rows = send.shape[0] // count
    return pl.pallas_call(
        functools.partial(exchange_kernel, axis, rows),
        out_shape=jax.ShapeDtypeStruct(send.shape, send.dtype),
        in_specs=[pl.BlockSpec(memory_space=pl.ANY)],
        out_specs=pl.BlockSpec(memory_space=pl.ANY),
        scratch_shapes=[
            pltpu.SemaphoreType.DMA((count,)),
            pltpu.SemaphoreType.DMA((count,)),
            pltpu.SemaphoreType.DMA(()),
        ],
        compiler_params=pltpu.CompilerParams(
            collective_id=collective_id, has_side_effects=True
        ),
    )(send)


def dispatch_expert_kernel(axis, rows, tile, send_ref, gate_hbm, up_hbm, down_hbm,
                           segment_hbm, sgate_hbm, sup_hbm, sdown_hbm, back_ref, shared_ref,
                           recv, gate_w, up_w, down_w, hidden, segment, sgate, sup, sdown,
                           out_ref, send_sems, recv_sems, local_sems, back_send, back_recv):
    count = lax.axis_size(axis)
    me = lax.axis_index(axis)
    weights = [
        pltpu.make_async_copy(gate_hbm.at[0], gate_w, local_sems.at[0]),
        pltpu.make_async_copy(up_hbm.at[0], up_w, local_sems.at[1]),
        pltpu.make_async_copy(down_hbm.at[0], down_w, local_sems.at[2]),
    ]
    shared_inputs = [
        pltpu.make_async_copy(segment_hbm, segment, local_sems.at[4]),
        pltpu.make_async_copy(sgate_hbm, sgate, local_sems.at[5]),
        pltpu.make_async_copy(sup_hbm, sup, local_sems.at[6]),
        pltpu.make_async_copy(sdown_hbm, sdown, local_sems.at[7]),
    ]
    for copy in shared_inputs + weights:
        copy.start()
    barrier = pltpu.get_barrier_semaphore()

    @pl.loop(1, count)
    def _(step):
        peer = lax.rem(me + step, count)
        pl.semaphore_signal(barrier, inc=1, device_id={axis: peer}, device_id_type=MESH_ID)

    pl.semaphore_wait(barrier, count - 1)
    local = pltpu.make_async_copy(
        send_ref.at[pl.ds(me * rows, rows)], recv.at[pl.ds(me * rows, rows)], local_sems.at[3]
    )
    local.start()

    @pl.loop(1, count)
    def _(step):
        peer = lax.rem(me + step, count)
        pltpu.make_async_remote_copy(
            src_ref=send_ref.at[pl.ds(peer * rows, rows)],
            dst_ref=recv.at[pl.ds(me * rows, rows)],
            send_sem=send_sems.at[peer],
            recv_sem=recv_sems.at[me],
            device_id={axis: peer},
            device_id_type=MESH_ID,
        ).start()

    for copy in shared_inputs:
        copy.wait()
    tokens = segment[...]
    gate_part = jnp.dot(tokens, sgate[...], preferred_element_type=jnp.float32)
    up_part = jnp.dot(tokens, sup[...], preferred_element_type=jnp.float32)
    shared_hidden = (gate_part / (1.0 + jnp.exp(-gate_part)) * up_part).astype(sdown.dtype)

    @pl.loop(0, sdown.shape[1] // (2 * tile))
    def _(t):
        cols = pl.ds(pl.multiple_of(t * 2 * tile, 2 * tile), 2 * tile)
        shared_ref[:, cols] = jnp.dot(
            shared_hidden, sdown[:, cols], preferred_element_type=jnp.float32
        )

    @pl.loop(1, count)
    def _(step):
        peer = lax.rem(me + step, count)
        pltpu.make_async_remote_copy(
            src_ref=send_ref.at[pl.ds(peer * rows, rows)],
            dst_ref=recv.at[pl.ds(peer * rows, rows)],
            send_sem=send_sems.at[peer],
            recv_sem=recv_sems.at[peer],
            device_id={axis: peer},
            device_id_type=MESH_ID,
        ).wait()

    local.wait()
    weights[0].wait()
    weights[1].wait()

    @pl.loop(0, gate_w.shape[1] // tile)
    def _(t):
        cols = pl.ds(pl.multiple_of(t * tile, tile), tile)
        tokens = recv[...]
        gate_part = jnp.dot(tokens, gate_w[:, cols], preferred_element_type=jnp.float32)
        up_part = jnp.dot(tokens, up_w[:, cols], preferred_element_type=jnp.float32)
        hidden[:, cols] = (gate_part / (1.0 + jnp.exp(-gate_part)) * up_part).astype(hidden.dtype)

    weights[2].wait()
    chunks = 2
    per_chunk = count // chunks
    chunk_rows = per_chunk * rows
    for part in range(chunks):
        lines = pl.ds(part * chunk_rows, chunk_rows)

        @pl.loop(0, down_w.shape[1] // (2 * tile))
        def _(t):
            cols = pl.ds(pl.multiple_of(t * 2 * tile, 2 * tile), 2 * tile)
            out_ref[lines, cols] = jnp.dot(
                hidden[lines, :], down_w[:, cols], preferred_element_type=jnp.float32
            ).astype(out_ref.dtype)

        @pl.loop(part * per_chunk, (part + 1) * per_chunk)
        def _(peer):
            @pl.when(peer != me)
            def _():
                pltpu.make_async_remote_copy(
                    src_ref=out_ref.at[pl.ds(peer * rows, rows)],
                    dst_ref=back_ref.at[pl.ds(me * rows, rows)],
                    send_sem=back_send.at[peer],
                    recv_sem=back_recv.at[me],
                    device_id={axis: peer},
                    device_id_type=MESH_ID,
                ).start()

            @pl.when(peer == me)
            def _():
                pltpu.make_async_copy(
                    out_ref.at[pl.ds(peer * rows, rows)],
                    back_ref.at[pl.ds(me * rows, rows)],
                    local_sems.at[8],
                ).start()

    @pl.loop(0, count)
    def _(peer):
        @pl.when(peer != me)
        def _():
            pltpu.make_async_remote_copy(
                src_ref=out_ref.at[pl.ds(peer * rows, rows)],
                dst_ref=back_ref.at[pl.ds(peer * rows, rows)],
                send_sem=back_send.at[peer],
                recv_sem=back_recv.at[peer],
                device_id={axis: peer},
                device_id_type=MESH_ID,
            ).wait()

        @pl.when(peer == me)
        def _():
            pltpu.make_async_copy(
                out_ref.at[pl.ds(peer * rows, rows)],
                back_ref.at[pl.ds(me * rows, rows)],
                local_sems.at[8],
            ).wait()


def dispatch_expert(send, gate, up, down, segment, sgate, sup, sdown, axis, collective_id):
    count = lax.axis_size(axis)
    rows = send.shape[0] // count
    width = gate.shape[2]
    any_space = pl.BlockSpec(memory_space=pl.ANY)
    vmem_space = pl.BlockSpec(memory_space=pltpu.VMEM)
    return pl.pallas_call(
        functools.partial(dispatch_expert_kernel, axis, rows, 256),
        out_shape=(
            jax.ShapeDtypeStruct(send.shape, send.dtype),
            jax.ShapeDtypeStruct((segment.shape[0], sdown.shape[1]), jnp.float32),
        ),
        in_specs=[any_space] * 8,
        out_specs=(vmem_space, vmem_space),
        scratch_shapes=[
            pltpu.VMEM(send.shape, send.dtype),
            pltpu.VMEM(gate.shape[1:], gate.dtype),
            pltpu.VMEM(up.shape[1:], up.dtype),
            pltpu.VMEM(down.shape[1:], down.dtype),
            pltpu.VMEM((send.shape[0], width), jnp.bfloat16),
            pltpu.VMEM(segment.shape, segment.dtype),
            pltpu.VMEM(sgate.shape, sgate.dtype),
            pltpu.VMEM(sup.shape, sup.dtype),
            pltpu.VMEM(sdown.shape, sdown.dtype),
            pltpu.VMEM(send.shape, send.dtype),
            pltpu.SemaphoreType.DMA((count,)),
            pltpu.SemaphoreType.DMA((count,)),
            pltpu.SemaphoreType.DMA((9,)),
            pltpu.SemaphoreType.DMA((count,)),
            pltpu.SemaphoreType.DMA((count,)),
        ],
        compiler_params=pltpu.CompilerParams(
            collective_id=collective_id, has_side_effects=True,
            vmem_limit_bytes=56 * 1024 * 1024,
        ),
    )(send, gate, up, down, segment, sgate, sup, sdown)


def gated_mlp(inputs, gate_matrix, up_matrix, down_matrix):
    gate_part = jnp.dot(inputs, gate_matrix, preferred_element_type=jnp.float32)
    up_part = jnp.dot(inputs, up_matrix, preferred_element_type=jnp.float32)
    hidden = (jax.nn.silu(gate_part) * up_part).astype(jnp.bfloat16)
    return jnp.dot(hidden, down_matrix, preferred_element_type=jnp.float32).astype(jnp.bfloat16)


def gate_weights(gate_score):
    values = gate_score.astype(jnp.float32)
    return 2.5 * values / jnp.sum(values, axis=-1, keepdims=True)


def weighted_rows(weights, rows):
    high = weights.astype(jnp.bfloat16)
    low = (weights - high.astype(jnp.float32)).astype(jnp.bfloat16)
    return jnp.dot(high, rows, preferred_element_type=jnp.float32) + jnp.dot(
        low, rows, preferred_element_type=jnp.float32
    )


def per_device(
    tokens,
    experts,
    gate_score,
    expert_gate,
    expert_up,
    expert_down,
    shared_gate,
    shared_up,
    shared_down,
):
    row_count = tokens.shape[0]
    model_width = tokens.shape[1]
    inner_count = lax.axis_size("inner")
    outer_count = lax.axis_size("outer")
    capacity = TOPK // TOP_GROUPS
    me = lax.axis_index("inner")
    side = math.isqrt(inner_count)
    gathered, all_experts, all_scores = torus_gather(
        [tokens, experts, gate_score], side, 0
    )
    segment = gathered.reshape(inner_count * row_count, model_width)
    weights = gate_weights(all_scores)
    local_experts = jnp.arange(outer_count, dtype=jnp.int32) * inner_count + me
    matches = all_experts[..., None] == local_experts
    named = jnp.any(matches, axis=2)
    named_int = named.astype(jnp.int32)
    earlier = jnp.cumsum(named_int, axis=1) - named_int
    slot_ids = jnp.arange(capacity, dtype=jnp.int32)
    placed = jnp.logical_and(named[..., None], earlier[..., None] == slot_ids)
    same_block = jnp.eye(inner_count, dtype=jnp.bool_)
    selector = jnp.logical_and(
        jnp.transpose(placed, (2, 0, 3, 1))[:, :, :, None, :],
        same_block[None, :, None, :, None],
    ).reshape(outer_count * inner_count * capacity, inner_count * row_count)
    outbound = jnp.dot(
        selector.astype(jnp.bfloat16), segment, preferred_element_type=jnp.float32
    ).astype(jnp.bfloat16)
    returned, shared = dispatch_expert(
        outbound, expert_gate, expert_up, expert_down,
        segment, shared_gate, shared_up, shared_down, "outer", 1,
    )
    slot_weight = jnp.sum(jnp.where(matches, weights[..., None], 0.0), axis=2)
    placed_weight = jnp.where(placed, slot_weight[..., None], 0.0)
    combine = jnp.where(
        same_block[:, None, None, :, None],
        jnp.transpose(placed_weight, (0, 1, 2, 3))[:, :, :, None, :],
        0.0,
    ).reshape(inner_count * row_count, outer_count * inner_count * capacity)
    high = combine.astype(jnp.bfloat16)
    low = (combine - high.astype(jnp.float32)).astype(jnp.bfloat16)
    return torus_reduce(shared, returned, high, low, side, 3).astype(jnp.bfloat16)


def solution(mesh):
    return jax.shard_map(
        per_device,
        mesh=mesh,
        in_specs=(
            P(("outer", "inner"), None),
            P(("outer", "inner"), None),
            P(("outer", "inner"), None),
            P(("outer", "inner"), None, None),
            P(("outer", "inner"), None, None),
            P(("outer", "inner"), None, None),
            P(None, "inner"),
            P(None, "inner"),
            P("inner", None),
        ),
        out_specs=P(("outer", "inner"), None),
        check_vma=False,
    )
```

```python
import functools
import math

import jax
import jax.numpy as jnp
from jax import lax
from jax.experimental import pallas as pl
from jax.experimental.pallas import tpu as pltpu
from jax.sharding import PartitionSpec as P

TOPK = 8
TOP_GROUPS = 4
MESH_ID = pl.DeviceIdType.MESH


def torus_gather_kernel(side, count, *refs):
    sources = refs[:count]
    outs = refs[count:2 * count]
    send_sems, recv_sems, local_sems = refs[2 * count:]
    me = lax.axis_index("inner")
    z, y = me // side, me % side
    half = sources[0].shape[0] // 2

    def node(zz, yy):
        return lax.rem(zz + side, side) * side + lax.rem(yy + side, side)

    steps = [
        (lambda zz, yy, k: node(zz, yy + k), lambda zz, yy, k: node(zz + k, yy)),
        (lambda zz, yy, k: node(zz + k, yy), lambda zz, yy, k: node(zz, yy + k)),
    ]
    neighbours = [
        node(z, y + 1), node(z, y - 1), node(z, y + 2),
        node(z + 1, y), node(z - 1, y), node(z + 2, y),
    ]
    barrier = pltpu.get_barrier_semaphore()
    for peer in neighbours:
        pl.semaphore_signal(barrier, inc=1, device_id={"inner": peer}, device_id_type=MESH_ID)
    pl.semaphore_wait(barrier, len(neighbours))

    rows = [pl.ds(0, half), pl.ds(half, half)]
    local_copies = []
    for a in range(count):
        for h in range(2):
            copy = pltpu.make_async_copy(
                sources[a].at[rows[h]], outs[a].at[me, rows[h]], local_sems.at[a, h]
            )
            copy.start()
            local_copies.append(copy)

    counter = [0]

    def run_round(moves):
        started = []
        for block, h, dest, from_input in moves:
            index = counter[0]
            counter[0] += 1
            for a in range(count):
                src = sources[a].at[rows[h]] if from_input else outs[a].at[block, rows[h]]
                copy = pltpu.make_async_remote_copy(
                    src_ref=src,
                    dst_ref=outs[a].at[block, rows[h]],
                    send_sem=send_sems.at[a, index],
                    recv_sem=recv_sems.at[a, index],
                    device_id={"inner": dest},
                    device_id_type=MESH_ID,
                )
                copy.start()
                started.append(copy)
        return started

    def finish(started, incoming):
        for copy in started:
            copy.wait_send()
        for index, block, h, sender in incoming:
            for a in range(count):
                pltpu.make_async_remote_copy(
                    src_ref=outs[a].at[block, rows[h]],
                    dst_ref=outs[a].at[block, rows[h]],
                    send_sem=send_sems.at[a, index],
                    recv_sem=recv_sems.at[a, index],
                    device_id={"inner": sender},
                    device_id_type=MESH_ID,
                ).wait_recv()

    base = counter[0]
    moves, incoming = [], []
    for h in range(2):
        first = steps[h][0]
        for k in (1, -1, 2):
            moves.append((me, h, first(z, y, k), True))
            incoming.append((base + len(incoming), first(z, y, -k), h, first(z, y, -k)))
    finish(run_round(moves), incoming)
    for copy in local_copies:
        copy.wait()
    base = counter[0]
    moves, incoming = [], []
    for h in range(2):
        first, second = steps[h]
        for k in (1, -1):
            for j in range(side):
                moves.append((first(z, y, j), h, second(z, y, k), False))
                origin = second(z, y, -k)
                oz, oy = origin // side, origin % side
                incoming.append((base + len(incoming), first(oz, oy, j), h, origin))
    finish(run_round(moves), incoming)
    base = counter[0]
    moves, incoming = [], []
    for h in range(2):
        first, second = steps[h]
        src_node = second(z, y, -1)
        sz, sy = src_node // side, src_node % side
        far = second(z, y, -2)
        fz, fy = far // side, far % side
        for j in range(side):
            moves.append((first(sz, sy, j), h, second(z, y, 1), False))
            incoming.append((base + len(incoming), first(fz, fy, j), h, src_node))
    finish(run_round(moves), incoming)


def torus_gather(arrays, side, collective_id):
    members = lax.axis_size("inner")
    count = len(arrays)
    copies = 4 + 2 + 4 * side + 2 * side
    return pl.pallas_call(
        functools.partial(torus_gather_kernel, side, count),
        out_shape=tuple(
            jax.ShapeDtypeStruct((members,) + x.shape, x.dtype) for x in arrays
        ),
        in_specs=[pl.BlockSpec(memory_space=pl.ANY)] * count,
        out_specs=tuple(pl.BlockSpec(memory_space=pl.ANY) for _ in arrays),
        scratch_shapes=[
            pltpu.SemaphoreType.DMA((count, copies)),
            pltpu.SemaphoreType.DMA((count, copies)),
            pltpu.SemaphoreType.DMA((count, 2)),
        ],
        compiler_params=pltpu.CompilerParams(
            collective_id=collective_id, has_side_effects=True
        ),
    )(*arrays)


def torus_reduce_kernel(side, tile, shared_ref, rows_ref, high_ref, low_ref, out_ref, x_ref, recv_a, recv_bp, recv_bm, send_b, partial,
                        send_a2, recv_a2, send_b2, send_c2, recv_b2p, recv_b2m,
                        send_sems, recv_sems):
    me = lax.axis_index("inner")
    z, y = me // side, me % side
    block_rows = out_ref.shape[0]
    half = block_rows // 2
    rows = [pl.ds(0, half), pl.ds(half, half)]

    def piece(block, h):
        return pl.ds(block * block_rows + h * half, half)

    def node(zz, yy):
        return lax.rem(zz + side, side) * side + lax.rem(yy + side, side)

    def wrap(p):
        return lax.rem(p + side, side)

    plans = [
        (lambda k: node(z + k, y), lambda k: node(z, y + k), z, y,
         lambda pos, j: pos * side + j),
        (lambda k: node(z, y + k), lambda k: node(z + k, y), y, z,
         lambda pos, j: j * side + pos),
    ]
    neighbours = [
        node(z, y + 1), node(z, y - 1), node(z, y + 2),
        node(z + 1, y), node(z - 1, y), node(z + 2, y),
    ]
    barrier = pltpu.get_barrier_semaphore()
    for peer in neighbours:
        pl.semaphore_signal(barrier, inc=1, device_id={"inner": peer}, device_id_type=MESH_ID)

    @pl.loop(0, x_ref.shape[1] // tile)
    def _(t):
        cols = pl.ds(pl.multiple_of(t * tile, tile), tile)
        back = rows_ref[:, cols]
        x_ref[:, cols] = (
            shared_ref[:, cols]
            + jnp.dot(high_ref[...], back, preferred_element_type=jnp.float32)
            + jnp.dot(low_ref[...], back, preferred_element_type=jnp.float32)
        ).astype(x_ref.dtype)

    pl.semaphore_wait(barrier, len(neighbours))

    counter = [0]

    def send(src, dst, dest):
        index = counter[0]
        counter[0] += 1
        copy = pltpu.make_async_remote_copy(
            src_ref=src, dst_ref=dst, send_sem=send_sems.at[index],
            recv_sem=recv_sems.at[index], device_id={"inner": dest},
            device_id_type=MESH_ID,
        )
        copy.start()
        return copy, (index, dst, src)

    def settle(sent, senders):
        for copy, _ in sent:
            copy.wait_send()
        for (_, (index, dst, src)), sender in zip(sent, senders):
            pltpu.make_async_remote_copy(
                src_ref=src, dst_ref=dst, send_sem=send_sems.at[index],
                recv_sem=recv_sems.at[index], device_id={"inner": sender},
                device_id_type=MESH_ID,
            ).wait_recv()

    sent, senders = [], []
    for h, (ring1, ring2, p1, p2, block) in enumerate(plans):
        for j in range(side):
            sent.append(send(x_ref.at[piece(block(wrap(p1 + 2), j), h)], recv_a.at[h, j], ring1(1)))
            senders.append(ring1(-1))
    settle(sent, senders)
    sent, senders = [], []
    for h, (ring1, ring2, p1, p2, block) in enumerate(plans):
        for j in range(side):
            mine = x_ref[piece(block(wrap(p1 + 1), j), h), :].astype(jnp.float32)
            send_b[h, j] = (mine + recv_a[h, j].astype(jnp.float32)).astype(send_b.dtype)
        for j in range(side):
            sent.append(send(send_b.at[h, j], recv_bp.at[h, j], ring1(1)))
            senders.append(ring1(-1))
            sent.append(send(x_ref.at[piece(block(wrap(p1 - 1), j), h)], recv_bm.at[h, j], ring1(-1)))
            senders.append(ring1(1))
    settle(sent, senders)
    for h, (ring1, ring2, p1, p2, block) in enumerate(plans):
        for j in range(side):
            partial[h, j] = (
                x_ref[piece(block(p1, j), h), :].astype(jnp.float32)
                + recv_bp[h, j].astype(jnp.float32)
                + recv_bm[h, j].astype(jnp.float32)
            )
    sent, senders = [], []
    for h, (ring1, ring2, p1, p2, block) in enumerate(plans):
        send_a2[h] = partial[h, wrap(p2 + 2)].astype(send_a2.dtype)
        send_b2[h] = partial[h, wrap(p2 + 1)].astype(send_b2.dtype)
        send_c2[h] = partial[h, wrap(p2 - 1)].astype(send_c2.dtype)
        sent.append(send(send_a2.at[h], recv_a2.at[h], ring2(2)))
        senders.append(ring2(-2))
        sent.append(send(send_b2.at[h], recv_b2p.at[h], ring2(1)))
        senders.append(ring2(-1))
        sent.append(send(send_c2.at[h], recv_b2m.at[h], ring2(-1)))
        senders.append(ring2(1))
    settle(sent, senders)
    for h, (ring1, ring2, p1, p2, block) in enumerate(plans):
        out_ref[rows[h], :] = (
            partial[h, p2]
            + recv_a2[h].astype(jnp.float32)
            + recv_b2p[h].astype(jnp.float32)
            + recv_b2m[h].astype(jnp.float32)
        ).astype(out_ref.dtype)


def torus_reduce(shared, back, high, low, side, collective_id):
    members = lax.axis_size("inner")
    width = shared.shape[1]
    row_count = shared.shape[0] // members
    half = row_count // 2
    piece = (2, side, half, width)
    one = (2, half, width)
    copies = 2 * side + 4 * side + 2 + 4
    vmem = pltpu.VMEM
    dtype = jnp.bfloat16
    return pl.pallas_call(
        functools.partial(torus_reduce_kernel, side, 512),
        out_shape=jax.ShapeDtypeStruct((row_count, width), dtype),
        in_specs=[pl.BlockSpec(memory_space=vmem)] * 4,
        out_specs=pl.BlockSpec(memory_space=vmem),
        scratch_shapes=[
            vmem(shared.shape, dtype),
            vmem(piece, dtype),
            vmem(piece, dtype),
            vmem(piece, dtype),
            vmem(piece, dtype),
            vmem(piece, jnp.float32),
            vmem(one, dtype),
            vmem(one, dtype),
            vmem(one, dtype),
            vmem(one, dtype),
            vmem(one, dtype),
            vmem(one, dtype),
            pltpu.SemaphoreType.DMA((copies,)),
            pltpu.SemaphoreType.DMA((copies,)),
        ],
        compiler_params=pltpu.CompilerParams(
            collective_id=collective_id, has_side_effects=True
        ),
    )(shared, back, high, low)


def exchange_kernel(axis, rows, send_ref, recv_ref, send_sems, recv_sems, local_sem):
    count = lax.axis_size(axis)
    me = lax.axis_index(axis)
    barrier = pltpu.get_barrier_semaphore()

    @pl.loop(1, count)
    def _(step):
        peer = lax.rem(me + step, count)
        pl.semaphore_signal(barrier, inc=1, device_id={axis: peer}, device_id_type=MESH_ID)

    pl.semaphore_wait(barrier, count - 1)
    local = pltpu.make_async_copy(
        send_ref.at[pl.ds(me * rows, rows)], recv_ref.at[pl.ds(me * rows, rows)], local_sem
    )
    local.start()

    @pl.loop(1, count)
    def _(step):
        peer = lax.rem(me + step, count)
        pltpu.make_async_remote_copy(
            src_ref=send_ref.at[pl.ds(peer * rows, rows)],
            dst_ref=recv_ref.at[pl.ds(me * rows, rows)],
            send_sem=send_sems.at[peer],
            recv_sem=recv_sems.at[me],
            device_id={axis: peer},
            device_id_type=MESH_ID,
        ).start()

    @pl.loop(1, count)
    def _(step):
        peer = lax.rem(me + step, count)
        pltpu.make_async_remote_copy(
            src_ref=send_ref.at[pl.ds(peer * rows, rows)],
            dst_ref=recv_ref.at[pl.ds(peer * rows, rows)],
            send_sem=send_sems.at[peer],
            recv_sem=recv_sems.at[peer],
            device_id={axis: peer},
            device_id_type=MESH_ID,
        ).wait()

    local.wait()


def exchange(send, axis, collective_id):
    count = lax.axis_size(axis)
    rows = send.shape[0] // count
    return pl.pallas_call(
        functools.partial(exchange_kernel, axis, rows),
        out_shape=jax.ShapeDtypeStruct(send.shape, send.dtype),
        in_specs=[pl.BlockSpec(memory_space=pl.ANY)],
        out_specs=pl.BlockSpec(memory_space=pl.ANY),
        scratch_shapes=[
            pltpu.SemaphoreType.DMA((count,)),
            pltpu.SemaphoreType.DMA((count,)),
            pltpu.SemaphoreType.DMA(()),
        ],
        compiler_params=pltpu.CompilerParams(
            collective_id=collective_id, has_side_effects=True
        ),
    )(send)


def ring_device(xx, cc):
    return lax.rem(xx + 4, 4) * 2 + cc


def remote(src, dst, send_sem, recv_sem, peer):
    return pltpu.make_async_remote_copy(
        src_ref=src, dst_ref=dst, send_sem=send_sem, recv_sem=recv_sem,
        device_id={"outer": peer}, device_id_type=MESH_ID,
    )


def outer_start(me, rows, src, dst, stage, sems):
    send_s, recv_s, mid_send, mid_recv, _, _ = sems
    half = rows // 2
    x, c = me // 2, me % 2
    full = [ring_device(x, 1 - c)] + [ring_device(x + dx, cc) for dx in (1, 3) for cc in (0, 1)]
    for p in full:
        remote(src.at[pl.ds(p * rows, rows)], dst.at[pl.ds(me * rows, rows)],
               send_s.at[p], recv_s.at[me], p).start()
    for cc in (0, 1):
        p = ring_device(x + 2, cc)
        remote(src.at[pl.ds(p * rows, half)], dst.at[pl.ds(me * rows, half)],
               send_s.at[p], recv_s.at[me], p).start()
        remote(src.at[pl.ds(p * rows + half, half)], stage.at[c],
               mid_send.at[cc], mid_recv.at[c], ring_device(x - 1, cc)).start()


def outer_forward(me, rows, dst, stage, sems):
    _, _, mid_send, mid_recv, fwd_send, fwd_recv = sems
    half = rows // 2
    x, c = me // 2, me % 2
    for cs in (0, 1):
        source = ring_device(x + 1, cs)
        remote(stage.at[cs], stage.at[cs], mid_send.at[cs], mid_recv.at[cs], source).wait_recv()
        remote(stage.at[cs], dst.at[pl.ds(source * rows + half, half)],
               fwd_send.at[cs], fwd_recv.at[cs], ring_device(x - 1, c)).start()


def outer_finish(me, rows, src, dst, stage, sems):
    send_s, recv_s, mid_send, mid_recv, fwd_send, fwd_recv = sems
    half = rows // 2
    x, c = me // 2, me % 2
    full = [ring_device(x, 1 - c)] + [ring_device(x + dx, cc) for dx in (1, 3) for cc in (0, 1)]
    for p in full:
        remote(src.at[pl.ds(p * rows, rows)], dst.at[pl.ds(p * rows, rows)],
               send_s.at[p], recv_s.at[p], p).wait()
    for cc in (0, 1):
        p = ring_device(x + 2, cc)
        remote(src.at[pl.ds(p * rows, half)], dst.at[pl.ds(p * rows, half)],
               send_s.at[p], recv_s.at[p], p).wait()
        remote(src.at[pl.ds(p * rows + half, half)], stage.at[c],
               mid_send.at[cc], mid_recv.at[c], ring_device(x - 1, cc)).wait_send()
    for cs in (0, 1):
        source = ring_device(x + 1, cs)
        remote(stage.at[cs], dst.at[pl.ds(source * rows + half, half)],
               fwd_send.at[cs], fwd_recv.at[cs], ring_device(x - 1, c)).wait_send()
        far = ring_device(x + 2, cs)
        remote(stage.at[cs], dst.at[pl.ds(far * rows + half, half)],
               fwd_send.at[cs], fwd_recv.at[cs], ring_device(x + 1, c)).wait_recv()


def dispatch_expert_kernel(axis, rows, tile, send_ref, gate_hbm, up_hbm, down_hbm,
                           segment_hbm, sgate_hbm, sup_hbm, sdown_hbm, back_ref, shared_ref,
                           recv, gate_w, up_w, down_w, hidden, segment, sgate, sup, sdown,
                           out_ref, stage_a, stage_b, send_sems, recv_sems, local_sems,
                           sems_a, sems_b):
    count = lax.axis_size(axis)
    me = lax.axis_index(axis)
    weights = [
        pltpu.make_async_copy(gate_hbm.at[0], gate_w, local_sems.at[0]),
        pltpu.make_async_copy(up_hbm.at[0], up_w, local_sems.at[1]),
        pltpu.make_async_copy(down_hbm.at[0], down_w, local_sems.at[2]),
    ]
    shared_inputs = [
        pltpu.make_async_copy(segment_hbm, segment, local_sems.at[4]),
        pltpu.make_async_copy(sgate_hbm, sgate, local_sems.at[5]),
        pltpu.make_async_copy(sup_hbm, sup, local_sems.at[6]),
        pltpu.make_async_copy(sdown_hbm, sdown, local_sems.at[7]),
    ]
    for copy in shared_inputs + weights:
        copy.start()
    barrier = pltpu.get_barrier_semaphore()

    @pl.loop(1, count)
    def _(step):
        peer = lax.rem(me + step, count)
        pl.semaphore_signal(barrier, inc=1, device_id={axis: peer}, device_id_type=MESH_ID)

    pl.semaphore_wait(barrier, count - 1)
    local = pltpu.make_async_copy(
        send_ref.at[pl.ds(me * rows, rows)], recv.at[pl.ds(me * rows, rows)], local_sems.at[3]
    )
    local.start()

    outer_start(me, rows, send_ref, recv, stage_a, sems_a)

    for copy in shared_inputs:
        copy.wait()
    tokens = segment[...]
    gate_part = jnp.dot(tokens, sgate[...], preferred_element_type=jnp.float32)
    up_part = jnp.dot(tokens, sup[...], preferred_element_type=jnp.float32)
    shared_hidden = (gate_part / (1.0 + jnp.exp(-gate_part)) * up_part).astype(sdown.dtype)

    @pl.loop(0, sdown.shape[1] // (2 * tile))
    def _(t):
        cols = pl.ds(pl.multiple_of(t * 2 * tile, 2 * tile), 2 * tile)
        shared_ref[:, cols] = jnp.dot(
            shared_hidden, sdown[:, cols], preferred_element_type=jnp.float32
        )

    outer_forward(me, rows, recv, stage_a, sems_a)
    outer_finish(me, rows, send_ref, recv, stage_a, sems_a)
    local.wait()
    weights[0].wait()
    weights[1].wait()

    @pl.loop(0, gate_w.shape[1] // tile)
    def _(t):
        cols = pl.ds(pl.multiple_of(t * tile, tile), tile)
        tokens = recv[...]
        gate_part = jnp.dot(tokens, gate_w[:, cols], preferred_element_type=jnp.float32)
        up_part = jnp.dot(tokens, up_w[:, cols], preferred_element_type=jnp.float32)
        hidden[:, cols] = (gate_part / (1.0 + jnp.exp(-gate_part)) * up_part).astype(hidden.dtype)

    weights[2].wait()
    @pl.loop(0, down_w.shape[1] // (2 * tile))
    def _(t):
        cols = pl.ds(pl.multiple_of(t * 2 * tile, 2 * tile), 2 * tile)
        out_ref[:, cols] = jnp.dot(
            hidden[...], down_w[:, cols], preferred_element_type=jnp.float32
        ).astype(out_ref.dtype)

    home = pltpu.make_async_copy(
        out_ref.at[pl.ds(me * rows, rows)], back_ref.at[pl.ds(me * rows, rows)],
        local_sems.at[8],
    )
    home.start()
    outer_start(me, rows, out_ref, back_ref, stage_b, sems_b)
    outer_forward(me, rows, back_ref, stage_b, sems_b)
    outer_finish(me, rows, out_ref, back_ref, stage_b, sems_b)
    home.wait()


def dispatch_expert(send, gate, up, down, segment, sgate, sup, sdown, axis, collective_id):
    count = lax.axis_size(axis)
    rows = send.shape[0] // count
    width = gate.shape[2]
    any_space = pl.BlockSpec(memory_space=pl.ANY)
    vmem_space = pl.BlockSpec(memory_space=pltpu.VMEM)
    return pl.pallas_call(
        functools.partial(dispatch_expert_kernel, axis, rows, 256),
        out_shape=(
            jax.ShapeDtypeStruct(send.shape, send.dtype),
            jax.ShapeDtypeStruct((segment.shape[0], sdown.shape[1]), jnp.float32),
        ),
        in_specs=[any_space] * 8,
        out_specs=(vmem_space, vmem_space),
        scratch_shapes=[
            pltpu.VMEM(send.shape, send.dtype),
            pltpu.VMEM(gate.shape[1:], gate.dtype),
            pltpu.VMEM(up.shape[1:], up.dtype),
            pltpu.VMEM(down.shape[1:], down.dtype),
            pltpu.VMEM((send.shape[0], width), jnp.bfloat16),
            pltpu.VMEM(segment.shape, segment.dtype),
            pltpu.VMEM(sgate.shape, sgate.dtype),
            pltpu.VMEM(sup.shape, sup.dtype),
            pltpu.VMEM(sdown.shape, sdown.dtype),
            pltpu.VMEM(send.shape, send.dtype),
            pltpu.VMEM((2, rows // 2, send.shape[1]), send.dtype),
            pltpu.VMEM((2, rows // 2, send.shape[1]), send.dtype),
            pltpu.SemaphoreType.DMA((count,)),
            pltpu.SemaphoreType.DMA((count,)),
            pltpu.SemaphoreType.DMA((9,)),
            [pltpu.SemaphoreType.DMA((count,)), pltpu.SemaphoreType.DMA((count,))]
            + [pltpu.SemaphoreType.DMA((2,)) for _ in range(4)],
            [pltpu.SemaphoreType.DMA((count,)), pltpu.SemaphoreType.DMA((count,))]
            + [pltpu.SemaphoreType.DMA((2,)) for _ in range(4)],
        ],
        compiler_params=pltpu.CompilerParams(
            collective_id=collective_id, has_side_effects=True,
            vmem_limit_bytes=56 * 1024 * 1024,
        ),
    )(send, gate, up, down, segment, sgate, sup, sdown)


def gated_mlp(inputs, gate_matrix, up_matrix, down_matrix):
    gate_part = jnp.dot(inputs, gate_matrix, preferred_element_type=jnp.float32)
    up_part = jnp.dot(inputs, up_matrix, preferred_element_type=jnp.float32)
    hidden = (jax.nn.silu(gate_part) * up_part).astype(jnp.bfloat16)
    return jnp.dot(hidden, down_matrix, preferred_element_type=jnp.float32).astype(jnp.bfloat16)


def gate_weights(gate_score):
    values = gate_score.astype(jnp.float32)
    return 2.5 * values / jnp.sum(values, axis=-1, keepdims=True)


def weighted_rows(weights, rows):
    high = weights.astype(jnp.bfloat16)
    low = (weights - high.astype(jnp.float32)).astype(jnp.bfloat16)
    return jnp.dot(high, rows, preferred_element_type=jnp.float32) + jnp.dot(
        low, rows, preferred_element_type=jnp.float32
    )


def per_device(
    tokens,
    experts,
    gate_score,
    expert_gate,
    expert_up,
    expert_down,
    shared_gate,
    shared_up,
    shared_down,
):
    row_count = tokens.shape[0]
    model_width = tokens.shape[1]
    inner_count = lax.axis_size("inner")
    outer_count = lax.axis_size("outer")
    capacity = TOPK // TOP_GROUPS
    me = lax.axis_index("inner")
    side = math.isqrt(inner_count)
    routing = jnp.concatenate([experts, gate_score], axis=1).astype(jnp.bfloat16)
    routing = jnp.pad(routing, ((0, 0), (0, 128 - routing.shape[1])))
    gathered, gathered_routing = torus_gather([tokens, routing], side, 0)
    segment = gathered.reshape(inner_count * row_count, model_width)
    all_experts = gathered_routing[:, :, :TOPK].astype(jnp.int32)
    all_scores = gathered_routing[:, :, TOPK:2 * TOPK].astype(jnp.int32)
    weights = gate_weights(all_scores)
    local_experts = jnp.arange(outer_count, dtype=jnp.int32) * inner_count + me
    matches = all_experts[..., None] == local_experts
    named = jnp.any(matches, axis=2)
    named_int = named.astype(jnp.int32)
    earlier = jnp.cumsum(named_int, axis=1) - named_int
    slot_ids = jnp.arange(capacity, dtype=jnp.int32)
    placed = jnp.logical_and(named[..., None], earlier[..., None] == slot_ids)
    same_block = jnp.eye(inner_count, dtype=jnp.bool_)
    selector = jnp.logical_and(
        jnp.transpose(placed, (2, 0, 3, 1))[:, :, :, None, :],
        same_block[None, :, None, :, None],
    ).reshape(outer_count * inner_count * capacity, inner_count * row_count)
    outbound = jnp.dot(
        selector.astype(jnp.bfloat16), segment, preferred_element_type=jnp.float32
    ).astype(jnp.bfloat16)
    returned, shared = dispatch_expert(
        outbound, expert_gate, expert_up, expert_down,
        segment, shared_gate, shared_up, shared_down, "outer", 1,
    )
    slot_weight = jnp.sum(jnp.where(matches, weights[..., None], 0.0), axis=2)
    placed_weight = jnp.where(placed, slot_weight[..., None], 0.0)
    combine = jnp.where(
        same_block[:, None, None, :, None],
        jnp.transpose(placed_weight, (0, 1, 2, 3))[:, :, :, None, :],
        0.0,
    ).reshape(inner_count * row_count, outer_count * inner_count * capacity)
    high = combine.astype(jnp.bfloat16)
    low = (combine - high.astype(jnp.float32)).astype(jnp.bfloat16)
    return torus_reduce(shared, returned, high, low, side, 3)


def solution(mesh):
    return jax.shard_map(
        per_device,
        mesh=mesh,
        in_specs=(
            P(("outer", "inner"), None),
            P(("outer", "inner"), None),
            P(("outer", "inner"), None),
            P(("outer", "inner"), None, None),
            P(("outer", "inner"), None, None),
            P(("outer", "inner"), None, None),
            P(None, "inner"),
            P(None, "inner"),
            P("inner", None),
        ),
        out_specs=P(("outer", "inner"), None),
        check_vma=False,
    )
```
